32 devices in a mesh: groups: 2 (over x), slab: 16 (over z, y, core).
Axes of the slice: x: 2, y: 2, z: 4, core: 2. Of those that a mesh axis runs over, the one named last changes fastest.
Arguments:
- flow_state: float32 [10, 128, 8192], P('groups', 'slab'), parts along dimension 0, may hold values from -6 to 6
- flow_speed: float32 [4, 128, 8192], P('groups', 'slab'), parts along dimension 0, may hold values from -1 to 1
- wall_cell: int32 [16384], P(('groups', 'slab')), parts along dimension 0, may hold values from 0 to 65535
- base_shift: float32 [6, 8192], P('groups', 'slab'), parts along dimension 0, may hold values from -30 to 30
- normals: float32 [6, 8192], P('groups', 'slab'), parts along dimension 0, may hold values from -3 to 3
- centres: float32 [6, 8192], P('groups', 'slab'), parts along dimension 0, as said below
- tile_blocks: int32 [32, 4], P('groups'), parts along dimension 0, may hold values from 0 to 15, as said below
- near_count: int32 [32], P('groups'), parts along dimension 0, may hold values from 1 to 1024, 8192 in all
- near_nodes: float32 [6, 16384], P('groups', 'slab'), parts along dimension 0, as said below
Outputs:
- new_flow: float32 [10, 128, 8192], P('groups', 'slab'), parts along dimension 0
- coefficients: float32 [6, 8192], P('groups', 'slab'), parts along dimension 0
- node_shift: float32 [6, 16384], P('groups', 'slab'), parts along dimension 0
The draws below stay inside these ranges and needn't reach their ends.
There are 2 independent parts, one for each index of `groups`. The reference program is written for one: setup_inputs(seed, part) draws one part's arguments, and reference() takes and returns one part's arrays. A program takes and returns all parts, laid end to end along the dimension named above; each array names one. Nothing has to cross between parts.
Inputs may be any that keep to these rules, and one draw needn't show every extreme that they name: `centres`: centre c has its first two coordinates in [0, 1) and its third in [0.4 * (c // 512), 0.4 * (c // 512 + 1)). `tile_blocks`: each row lists 4 consecutive centre blocks in rising order. `near_count`: the counts sum to 8192 and the largest equals 1024. `near_nodes`: A node of block m has its first two coordinates in [0, 1) and its third in [0.4 * b, 0.4 * (b + 1)) for one block b listed in tile_blocks[m].
All inputs are finite; a program needn't handle non-finite values.
Results may differ from the reference program's by a relative error of at most 0.0003.
Values sent between devices are 32-bit elements; how exact they have to be, the bound alone decides.
No kernel may reach another device: no remote copies, remote signals or barrier semaphores. Data moves between devices by JAX's collectives and lax.ppermute only.
A program may use at most 64 MiB of HBM per device.

```python
import math
import jax
import jax.numpy as jnp
import numpy as np
from jax import lax

NVAR = 5
CZ = 8
PLANE = 8192
CENT_DEV = 512
NB = 1024
TILES = 4
ITERS = 3
BLOCKS = 16
NZ = 128
CENTRES = 8192
NODES = 16384


def tile_table(key):
    starts = jax.random.randint(jax.random.fold_in(key, 7), (BLOCKS,), 0, BLOCKS - TILES + 1)
    top_row = jax.random.randint(jax.random.fold_in(key, 8), (), 0, BLOCKS)
    low_row = (top_row + 1) % BLOCKS
    rows = jnp.arange(BLOCKS, dtype=jnp.int32)
    starts = jnp.where(rows == top_row, BLOCKS - TILES, starts)
    starts = jnp.where(rows == low_row, 0, starts)
    return (starts[:, None] + jnp.arange(TILES, dtype=jnp.int32)[None, :]).astype(jnp.int32)


def draw_tile_blocks(key, part):
    return tile_table(key)


def draw_near_nodes(key, part):
    tiles = tile_table(key)
    picks = jax.random.randint(jax.random.fold_in(key, 11), (BLOCKS, NB), 0, TILES)
    chosen = jnp.take_along_axis(tiles, picks, axis=1).astype(jnp.float32).reshape(-1)
    depth = jax.random.uniform(jax.random.fold_in(key, 13), (BLOCKS * NB,), jnp.float32)
    third = (chosen + depth) * 0.4
    first = jax.random.uniform(jax.random.fold_in(key, 17), (2, BLOCKS * NB), jnp.float32)
    return jnp.concatenate([first, third[None, :]], axis=0)


def draw_centres(key, part):
    owner = (jnp.arange(CENTRES, dtype=jnp.int32) // CENT_DEV).astype(jnp.float32)
    first = jax.random.uniform(jax.random.fold_in(key, 1), (2, CENTRES), jnp.float32)
    depth = jax.random.uniform(jax.random.fold_in(key, 2), (CENTRES,), jnp.float32)
    third = (owner + depth) * 0.4
    return jnp.concatenate([first, third[None, :]], axis=0)


def draw_base_shift(key, part):
    position = jnp.arange(CENTRES, dtype=jnp.float32) / CENTRES
    scale = 0.3 * jnp.exp(2.302585 * position)
    noise = jnp.clip(jax.random.normal(key, (3, CENTRES), jnp.float32), -6.0, 6.0)
    return noise * scale[None, :]


def plant(values, rng, low, largest):
    shape = values.shape
    spot = [jax.random.randint(jax.random.fold_in(rng, axis), (), 0, shape[axis]) for axis in range(len(shape))]
    values = values.at[tuple(spot)].set(low)
    longest = shape.index(max(shape))
    spot[longest] = (spot[longest] + 1) % shape[longest]
    return values.at[tuple(spot)].set(largest)


def block_levels(own_key, dims, split, low, largest):
    factor_of = 1.0
    for dim, parts in split:
        draws = jax.random.uniform(jax.random.fold_in(jax.random.fold_in(own_key, 6), dim), (parts,), jnp.float32, low / len(split), largest / len(split))
        factor_of = factor_of * jnp.repeat(jnp.exp(draws), dims[dim] // parts).reshape((-1,) + (1,) * (len(dims) - 1 - dim))
    return factor_of


def profile(number_of, total, limit, slope):
    weights = [(1 << 20) // math.isqrt(rank ** slope) + 1 for rank in range(2, number_of + 1)]
    rest, holding = total - limit - (number_of - 1), [1] * (number_of - 1)
    while rest > 0:
        movable = [i for i in range(number_of - 1) if holding[i] < limit]
        whole, left = sum([weights[i] for i in movable]), rest
        for i in movable:
            extra = min(limit - holding[i], max(1, left * weights[i] // whole), rest)
            holding[i] = holding[i] + extra
            rest = rest - extra
    return np.array([limit] + holding)


def uneven_parts(key, count, total, reach, slope):
    if count == 2:
        one = jax.random.randint(key, (), max(1, total - reach), min(reach, total - 1) + 1)
        return jnp.stack([one, total - one])
    sizes = jnp.asarray(profile(count, total, reach, slope), jnp.int32)
    twos = (count - 1) // 2
    giver, receiver = sizes[1:1 + 2 * twos:2], sizes[2:2 + 2 * twos:2]
    slack = jnp.minimum(giver - 1, reach - receiver)
    shifted = jax.random.randint(jax.random.fold_in(key, 1), (twos,), 0, 1 << 20) % (slack + 1)
    sizes = sizes.at[1:1 + 2 * twos:2].set(giver - shifted).at[2:2 + 2 * twos:2].set(receiver + shifted)
    return sizes[jax.random.permutation(jax.random.fold_in(key, 2), count)]


def centred(key, shape, spread, reach, cuts=(), held_as=jnp.bfloat16):
    drawn = jax.random.normal(key, shape, jnp.float32) * spread
    if len(cuts) > 0:
        drawn = block_levels(key, shape, cuts, -0.22, 0.18) * drawn
    return jnp.clip(drawn, min=-reach, max=reach).astype(held_as)


def setup_inputs(seed: int = 0, part: int = 0) -> dict:
    key_of = jax.random.split(jax.random.key(seed), 10)
    part_splits = jax.random.split(jax.random.fold_in(key_of[9], part), 10)
    return {
        "flow_state": centred(part_splits[0], (NVAR, NZ, PLANE), 1.0, 6.0, ((1, 16),), jnp.float32),
        "flow_speed": jnp.clip(jax.random.uniform(part_splits[1], (2, NZ, PLANE), jnp.float32, -1.0, 1.0) * block_levels(part_splits[1], (2, NZ, PLANE), ((1, 16),), -0.4, 0.0), -1.0, 1.0),
        "wall_cell": plant(jax.random.randint(part_splits[2], (CENTRES,), 0, CZ * PLANE), jax.random.fold_in(part_splits[2], 1), 0, (CZ * PLANE) - 1).astype(jnp.int32),
        "base_shift": draw_base_shift(jax.random.fold_in(jax.random.fold_in(key_of[9], part), 71), part),
        "normals": centred(part_splits[4], (3, CENTRES), 0.5, 3.0, ((1, 16),), jnp.float32),
        "centres": draw_centres(jax.random.fold_in(jax.random.fold_in(key_of[9], part), 71), part),
        "tile_blocks": draw_tile_blocks(jax.random.fold_in(jax.random.fold_in(key_of[9], part), 71), part),
        "near_count": uneven_parts(part_splits[7], BLOCKS, NB * BLOCKS // 2, NB, 2).astype(jnp.int32),
        "near_nodes": draw_near_nodes(jax.random.fold_in(jax.random.fold_in(key_of[9], part), 71), part),
    }


FLUX_STEP = 0.2
SUPPORT = 0.15
DIAG_SHIFT = 0.5

def wendland(squared):
    scaled = jnp.sqrt(squared) / SUPPORT
    inside = jnp.maximum(1.0 - scaled, 0.0)
    square_in = inside * inside
    return square_in * square_in * (4.0 * scaled + 1.0)

def kernel_table(sources, targets):
    diff_a = sources[0][:, None] - targets[0][None, :]
    diff_b = sources[1][:, None] - targets[1][None, :]
    diff_c = sources[2][:, None] - targets[2][None, :]
    return wendland(diff_a * diff_a + diff_b * diff_b + diff_c * diff_c)

def flux_update(padded_q, padded_w, flow_state, cycle_speed):
    face_w = 0.5 * (padded_w[:-1] + padded_w[1:])
    below_face = padded_q[:, :-1]
    above_face = padded_q[:, 1:]
    axial_flux = 0.5 * face_w * (below_face + above_face) - 0.5 * jnp.abs(face_w) * (above_face - below_face)
    following = jnp.roll(flow_state, -1, axis=2)
    cycle_w = 0.5 * (cycle_speed + jnp.roll(cycle_speed, -1, axis=1))
    cycle_flux = 0.5 * cycle_w * (flow_state + following) - 0.5 * jnp.abs(cycle_w) * (following - flow_state)
    change = axial_flux[:, 1:] - axial_flux[:, :-1] + (cycle_flux - jnp.roll(cycle_flux, 1, axis=2))
    return flow_state - FLUX_STEP * change

def reference(flow_state, flow_speed, wall_cell, base_shift, normals, centres, tile_blocks, near_count, near_nodes):
    padded_q = jnp.pad(flow_state, ((0, 0), (1, 1), (0, 0)))
    padded_w = jnp.pad(flow_speed[0], ((1, 1), (0, 0)))
    new_flow = flux_update(padded_q, padded_w, flow_state, flow_speed[1])
    pressure = new_flow[4].reshape(-1)
    owners = jnp.arange(CENTRES, dtype=jnp.int32) // CENT_DEV
    wall_load = jnp.take(pressure, owners * (CZ * PLANE) + wall_cell)
    right_side = base_shift + normals * wall_load[None, :]
    centre_blocks = centres.reshape(3, BLOCKS, CENT_DEV).transpose(1, 0, 2)
    padded_centres = jnp.pad(centre_blocks, ((1, 1), (0, 0), (0, 0)))

    def apply_matrix(direction):
        direction_blocks = direction.reshape(3, BLOCKS, CENT_DEV).transpose(1, 0, 2)
        padded_dir = jnp.pad(direction_blocks, ((1, 1), (0, 0), (0, 0)))

        def block_product(index):
            near_c = lax.dynamic_slice_in_dim(padded_centres, index, 3, 0).transpose(1, 0, 2).reshape(3, 3 * CENT_DEV)
            near_d = lax.dynamic_slice_in_dim(padded_dir, index, 3, 0).transpose(1, 0, 2).reshape(3, 3 * CENT_DEV)
            kernel = kernel_table(near_c, centre_blocks[index])
            product = jnp.dot(near_d, kernel, precision=lax.Precision.HIGHEST, preferred_element_type=jnp.float32)
            return product + DIAG_SHIFT * direction_blocks[index]
        result = lax.map(block_product, jnp.arange(BLOCKS, dtype=jnp.int32))
        return result.transpose(1, 0, 2).reshape(3, CENTRES)
    coefficients = jnp.zeros_like(right_side)
    residual = right_side
    search = right_side
    energy = lax.optimization_barrier(jnp.sum(residual * residual, axis=1))
    for iteration in range(ITERS):
        matrix_image = apply_matrix(search)
        step_len = energy / lax.optimization_barrier(jnp.sum(search * matrix_image, axis=1))
        coefficients = coefficients + step_len[:, None] * search
        residual = residual - step_len[:, None] * matrix_image
        new_energy = lax.optimization_barrier(jnp.sum(residual * residual, axis=1))
        search = residual + (new_energy / energy)[:, None] * search
        energy = new_energy
    coef_blocks = coefficients.reshape(3, BLOCKS, CENT_DEV).transpose(1, 0, 2)
    node_blocks = near_nodes.reshape(3, BLOCKS, NB).transpose(1, 0, 2)

    def node_block(index):
        points = node_blocks[index]
        node_sum = jnp.zeros((3, NB), jnp.float32)
        for listed in range(TILES):
            chosen = tile_blocks[index, listed]
            kernel = kernel_table(centre_blocks[chosen], points)
            node_sum = node_sum + jnp.dot(coef_blocks[chosen], kernel, precision=lax.Precision.HIGHEST, preferred_element_type=jnp.float32)
        live_mask = jnp.arange(NB, dtype=jnp.int32) < near_count[index]
        return jnp.where(live_mask[None, :], node_sum, 0.0)
    shifts = lax.map(node_block, jnp.arange(BLOCKS, dtype=jnp.int32))
    node_shift = shifts.transpose(1, 0, 2).reshape(3, NODES)
    return (new_flow, coefficients, node_shift)
```

```python
import functools

import jax
import jax.numpy as jnp
from jax import lax
from jax.experimental import pallas as pl
from jax.experimental.pallas import tpu as pltpu
from jax.sharding import Mesh
from jax.sharding import PartitionSpec as P

FLUX_STEP = 0.2
SUPPORT = 0.15
DIAG_SHIFT = 0.5
CENTRE_SHIFT = DIAG_SHIFT + 1.0
TINY = 1e-30
F32 = jnp.float32
BF16 = jnp.bfloat16
SLAB = ("chip", "core")
VMEM = pl.BlockSpec(memory_space=pltpu.VMEM)
SMEM = pl.BlockSpec(memory_space=pltpu.SMEM)
ANY = pl.BlockSpec(memory_space=pl.ANY)


def halves(values):
    high = values.astype(BF16)
    return high, (values - high.astype(F32)).astype(BF16)


def wendland(squared):
    scaled = squared * lax.rsqrt(jnp.maximum(squared, TINY))
    inside = jnp.maximum(1.0 - scaled, 0.0)
    square_in = inside * inside
    return square_in * square_in * (4.0 * scaled + 1.0)


def distances(columns, rows, width):
    total = None
    for axis in range(3):
        diff = columns[:, axis : axis + 1] - rows[axis : axis + 1, :]
        total = diff * diff if total is None else total + diff * diff
    return total


def doubled(values):
    high, low = halves(values)
    return jnp.concatenate([high, low], axis=0)


def edge_kernel(core_ref, q_ref, w_ref, a_ref, b_ref, sems):
    count = q_ref.shape[0]
    last = q_ref.shape[1] - 1

    def move(row_a, row_b):
        copies = [
            pltpu.make_async_copy(q_ref.at[:, row_a], a_ref.at[pl.ds(0, count)], sems.at[0]),
            pltpu.make_async_copy(q_ref.at[:, row_b], b_ref.at[pl.ds(0, count)], sems.at[1]),
            pltpu.make_async_copy(w_ref.at[pl.ds(0, 1), row_a], a_ref.at[pl.ds(count, 1)], sems.at[2]),
            pltpu.make_async_copy(w_ref.at[pl.ds(0, 1), row_b], b_ref.at[pl.ds(count, 1)], sems.at[3]),
        ]
        for copy in copies:
            copy.start()
        for copy in copies:
            copy.wait()

    @pl.when(core_ref[1] == 0)
    def _():
        move(last, 0)

    @pl.when(core_ref[1] != 0)
    def _():
        move(0, last)


def edge_rows(place, flow_state, flow_speed):
    count, _, plane = flow_state.shape
    rows = jax.ShapeDtypeStruct((count + 1, plane), F32)
    return pl.pallas_call(
        edge_kernel,
        out_shape=(rows, rows),
        in_specs=[SMEM, ANY, ANY],
        out_specs=(VMEM, VMEM),
        scratch_shapes=[pltpu.SemaphoreType.DMA((4,))],
        name="edge_rows",
    )(place, flow_state, flow_speed)


def flux_kernel(
    place_ref, q_ref, w_ref, a_ref, b_ref, cell_ref, base_ref, normal_ref, centre_ref, new_ref, out_ref
):
    count, rows, plane = q_ref.shape
    width = 512
    even = place_ref[1] == 0
    pressure = 4
    rate = 0.5 * FLUX_STEP

    def chunk(step, _):
        here = pl.multiple_of(step * width, 128)
        left = pl.multiple_of(lax.rem(here + plane - 128, plane), 128)
        right = pl.multiple_of(lax.rem(here + width, plane), 128)
        below = jnp.where(even, b_ref[:, pl.ds(here, width)], a_ref[:, pl.ds(here, width)])
        above = jnp.where(even, a_ref[:, pl.ds(here, width)], b_ref[:, pl.ds(here, width)])
        row = lax.broadcasted_iota(jnp.int32, (rows, width), 0)

        def axial(values, index):
            down = jnp.where(row == 0, below[index : index + 1], pltpu.roll(values, 1, 0))
            up = jnp.where(row == rows - 1, above[index : index + 1], pltpu.roll(values, rows - 1, 0))
            return down, up

        def cyclic(ref, index):
            values = ref[index, :, pl.ds(here, width)]
            wide = jnp.concatenate(
                [ref[index, :, pl.ds(left, 128)], values, ref[index, :, pl.ds(right, 128)]], axis=1
            )
            before = pltpu.roll(wide, 1, 1)[:, 128 : 128 + width]
            after = pltpu.roll(wide, width + 255, 1)[:, 128 : 128 + width]
            return values, before, after

        w = w_ref[0, :, pl.ds(here, width)]
        w_down, w_up = axial(w, count)
        face_low = rate * (w_down + w)
        face_high = rate * (w + w_up)
        speed, speed_before, speed_after = cyclic(w_ref, 1)
        face_left = rate * (speed_before + speed)
        face_right = rate * (speed + speed_after)
        low_in = jnp.maximum(face_low, 0.0)
        high_out = jnp.minimum(face_high, 0.0)
        left_in = jnp.maximum(face_left, 0.0)
        right_out = jnp.minimum(face_right, 0.0)
        keep = 1.0 - (
            (jnp.maximum(face_high, 0.0) - jnp.minimum(face_low, 0.0))
            + (jnp.maximum(face_right, 0.0) - jnp.minimum(face_left, 0.0))
        )
        for index in range(count):
            values, before, after = cyclic(q_ref, index)
            down, up = axial(values, index)
            new_ref[index, :, pl.ds(here, width)] = (
                keep * values + low_in * down - high_out * up + left_in * before - right_out * after
            )
        return 0

    lax.fori_loop(0, plane // width, chunk, 0)

    cells = cell_ref[...]
    lanes = plane // 128
    cell_row = cells // plane
    column = cells - cell_row * plane
    group = column // 128
    lane = column - group * 128
    stacked = jnp.concatenate(
        [new_ref[pressure, :, index * 128 : index * 128 + 128] for index in range(lanes)], axis=0
    )
    place = group * rows + cell_row
    centres = cells.shape[1]
    chosen = (lax.broadcasted_iota(jnp.int32, (rows * lanes, centres), 0) == place).astype(F32)
    picked = lax.dot_general(
        stacked,
        chosen,
        (((0,), (0,)), ((), ())),
        precision=lax.Precision.HIGHEST,
        preferred_element_type=F32,
    )
    load = jnp.sum(
        jnp.where(lax.broadcasted_iota(jnp.int32, (128, centres), 0) == lane, picked, 0.0), axis=0, keepdims=True
    )
    out_ref[...] = jnp.concatenate(
        [
            base_ref[...] + normal_ref[...] * load,
            centre_ref[...] * (1.0 / SUPPORT),
            jnp.zeros((2, centres), F32),
        ],
        axis=0,
    )


def flux_and_right_side(place, flow_state, flow_speed, from_a, from_b, wall_cell, base_shift, normals, centres):
    return pl.pallas_call(
        flux_kernel,
        out_shape=(
            jax.ShapeDtypeStruct(flow_state.shape, F32),
            jax.ShapeDtypeStruct((8, centres.shape[1]), F32),
        ),
        in_specs=[SMEM] + [VMEM] * 8,
        out_specs=(VMEM, VMEM),
        name="flux",
    )(place, flow_state, flow_speed, from_a, from_b, wall_cell.reshape(1, -1), base_shift, normals, centres)


def block_of(mine_ref, other_ref, block, core):
    chip = lax.div(block, 2)
    own = lax.rem(block, 2) == core
    return jnp.where(own, mine_ref[chip], other_ref[chip])


def apply_table(values, table, transposed):
    size = table.shape[1]
    lhs = doubled(values)
    if transposed:
        both = lax.dot_general(lhs, table, (((1,), (1,)), ((), ())), preferred_element_type=F32)
        both = both[:, :size] + both[:, size:]
    else:
        both = jnp.dot(jnp.concatenate([lhs, lhs], axis=1), table, preferred_element_type=F32)
    return both[:8] + both[8:]


def powers_kernel(count, place_ref, mine_ref, other_ref, out_ref, blocks, columns, tables):
    size = mine_ref.shape[2]
    chip, core = place_ref[0], place_ref[1]
    me = chip * 2 + core
    rows = 64
    value_row = lax.broadcasted_iota(jnp.int32, (8, size), 0) < 3

    live = []
    for slot in range(6):
        block = me + slot - 2
        valid = jnp.logical_and(block >= 0, block < count)
        live.append(valid)
        data = block_of(mine_ref, other_ref, jnp.clip(block, 0, count - 1), core)
        blocks[slot] = data
        columns[slot] = data.T

    def build(index, source, target, diagonal):
        def part(step, _):
            start = pl.multiple_of(step * rows, rows)
            table = wendland(
                distances(columns[source, pl.ds(start, rows), 3:6], blocks[target, 3:6], size)
            )
            if diagonal:
                same = lax.broadcasted_iota(jnp.int32, (rows, size), 0) + start == lax.broadcasted_iota(
                    jnp.int32, (rows, size), 1
                )
                table = jnp.where(same, 0.0, table)
            high, low = halves(table)
            tables[index, pl.ds(start, rows)] = high
            tables[index, pl.ds(pl.multiple_of(start + size, rows), rows)] = low
            return 0

        lax.fori_loop(0, size // rows, part, 0)

    def diagonal(step, _):
        build(step, step + 1, step + 1, True)
        return 0

    def pair(step, _):
        build(step + 4, step, step + 1, False)
        return 0

    lax.fori_loop(0, 4, diagonal, 0)
    lax.fori_loop(0, 5, pair, 0)

    def power(values, slots):
        result = {}
        for slot in slots:
            total = apply_table(values[slot], tables[slot - 1], False)
            total = total + apply_table(values[slot - 1], tables[slot + 3], False)
            total = total + apply_table(values[slot + 1], tables[slot + 4], True)
            result[slot] = jnp.where(live[slot], total, 0.0)
        return result

    zeroth = {
        slot: jnp.where(jnp.logical_and(value_row, live[slot]), blocks[slot], 0.0) for slot in range(6)
    }
    first = power(zeroth, range(1, 5))
    second = power(first, range(2, 4))
    own = apply_table(second[2], tables[1], False)
    beside = apply_table(second[3], tables[6], True)

    def inner(left, right):
        return jnp.sum(left * right, axis=1, keepdims=True)

    moments = [
        inner(zeroth[2], zeroth[2]),
        inner(zeroth[2], first[2]),
        inner(first[2], first[2]),
        inner(first[2], second[2]),
        inner(second[2], second[2]),
        inner(second[2], own + 2.0 * beside),
    ]
    lane = lax.broadcasted_iota(jnp.int32, (8, 128), 1)
    packed = jnp.zeros((8, 128), F32)
    for index, moment in enumerate(moments):
        packed = jnp.where(lane == index, moment, packed)
    out_ref[:, :size] = jnp.concatenate([first[2][:3], second[2][:3], jnp.zeros((2, size), F32)], axis=0)
    out_ref[:, size:] = packed


def powers(place, mine, other, count):
    size = mine.shape[2]
    return pl.pallas_call(
        functools.partial(powers_kernel, count),
        out_shape=jax.ShapeDtypeStruct((8, size + 128), F32),
        in_specs=[SMEM, VMEM, VMEM],
        out_specs=VMEM,
        scratch_shapes=[
            pltpu.VMEM((6, 8, size), F32),
            pltpu.VMEM((6, size, 8), F32),
            pltpu.VMEM((9, 2 * size, size), BF16),
        ],
        name="powers",
    )(place, mine, other)


def ratio(top, bottom):
    safe = bottom > 0.0
    return jnp.where(safe, top / jnp.where(safe, bottom, 1.0), 0.0)


def weights_of(moments):
    def inner(left, right):
        total = None
        for i, a in enumerate(left):
            for j, c in enumerate(right):
                term = a * c * moments[i + j]
                total = term if total is None else total + term
        return total

    one = jnp.ones_like(moments[0])
    residual, search = [one], [one]
    coefficients = [0.0 * one] * 3
    energy = moments[0]
    for step in range(3):
        image = [CENTRE_SHIFT * value for value in search] + [0.0 * one]
        for index, value in enumerate(search):
            image[index + 1] = image[index + 1] + value
        length = ratio(energy, inner(search, image))
        for index, value in enumerate(search):
            coefficients[index] = coefficients[index] + length * value
        if step == 2:
            break
        longer = residual + [0.0 * one]
        residual = [value - length * other for value, other in zip(longer, image)]
        fresh = jnp.maximum(inner(residual, residual), 0.0)
        scale = ratio(fresh, energy)
        search = [
            value + scale * (search[index] if index < len(search) else 0.0)
            for index, value in enumerate(residual)
        ]
        energy = fresh
    return coefficients


def near_kernel(
    place_ref, tile_ref, count_ref, mine_ref, other_ref, mine_power, other_power, nodes_ref, coef_ref, shift_ref, columns, tables
):
    size = mine_ref.shape[2]
    slots = nodes_ref.shape[1]
    chips = mine_ref.shape[0]
    chip, core = place_ref[0], place_ref[1]
    me = chip * 2 + core
    listed = tile_ref.shape[1]
    rows = 64
    width = min(512, slots)

    summed = mine_power[0, :, size:] + other_power[0, :, size:]
    for index in range(1, chips):
        summed = summed + (mine_power[index, :, size:] + other_power[index, :, size:])
    moments = [summed[:, index : index + 1] for index in range(6)]
    weights = weights_of(moments)

    def coefficients_of(block):
        data = block_of(mine_ref, other_ref, block, core)
        power = block_of(mine_power, other_power, block, core)[:, :size]
        values = weights[0] * data + weights[1] * power + weights[2] * pltpu.roll(power, 5, 0)
        keep = lax.broadcasted_iota(jnp.int32, (8, size), 0) < 3
        return data, jnp.where(keep, values, 0.0)

    coef_ref[...] = coefficients_of(me)[1][:3]
    lhs = []
    for index in range(listed):
        data, values = coefficients_of(tile_ref[me, index])
        columns[index] = data.T
        both = doubled(values)
        lhs.append(jnp.concatenate([both, both], axis=1))

    live = count_ref[me]
    for tile in range(slots // width):
        points = nodes_ref[:, tile * width : (tile + 1) * width] * (1.0 / SUPPORT)
        total = jnp.zeros((16, width), F32)
        for index in range(listed):

            def part(step, _, index=index, points=points):
                start = pl.multiple_of(step * rows, rows)
                table = wendland(distances(columns[index, pl.ds(start, rows), 3:6], points, width))
                high, low = halves(table)
                tables[index % 2, pl.ds(start, rows)] = high
                tables[index % 2, pl.ds(pl.multiple_of(start + size, rows), rows)] = low
                return 0

            lax.fori_loop(0, size // rows, part, 0)
            total = total + jnp.dot(lhs[index], tables[index % 2], preferred_element_type=F32)
        slot = lax.broadcasted_iota(jnp.int32, (3, width), 1) + tile * width
        shift_ref[:, tile * width : (tile + 1) * width] = jnp.where(slot < live, total[:3] + total[8:11], 0.0)


def near_body(place, tile_blocks, near_count, mine, other, mine_power, other_power, near_nodes):
    size = mine.shape[2]
    width = min(512, near_nodes.shape[1])
    return pl.pallas_call(
        near_kernel,
        out_shape=(
            jax.ShapeDtypeStruct((3, size), F32),
            jax.ShapeDtypeStruct(near_nodes.shape, F32),
        ),
        in_specs=[SMEM, SMEM, SMEM] + [VMEM] * 5,
        out_specs=(VMEM, VMEM),
        scratch_shapes=[
            pltpu.VMEM((tile_blocks.shape[1], size, 8), F32),
            pltpu.VMEM((2, 2 * size, width), BF16),
        ],
        name="near_body",
    )(place, tile_blocks, near_count, mine, other, mine_power, other_power, near_nodes)


def gathered(values, count, partner):
    chips = count // 2
    mine = lax.all_to_all(jnp.broadcast_to(values[None], (chips,) + values.shape), "chip", 0, 0)
    return mine, lax.ppermute(mine, SLAB, partner)


def shards(
    count,
    flow_state,
    flow_speed,
    wall_cell,
    base_shift,
    normals,
    centres,
    tile_blocks,
    near_count,
    near_nodes,
):
    place = jnp.stack([lax.axis_index("chip"), lax.axis_index("core")]).astype(jnp.int32)
    partner = [(i, i ^ 1) for i in range(count)]
    across = [(i, i + 1) for i in range(1, count - 1, 2)]
    across = across + [(j, i) for i, j in across]
    send_a, send_b = edge_rows(place, flow_state, flow_speed)
    from_a = lax.ppermute(send_a, SLAB, partner)
    from_b = lax.ppermute(send_b, SLAB, across)
    new_flow, packed = flux_and_right_side(
        place, flow_state, flow_speed, from_a, from_b, wall_cell, base_shift, normals, centres
    )
    mine, other = gathered(packed, count, partner)
    mine_power, other_power = gathered(powers(place, mine, other, count), count, partner)
    coefficients, node_shift = near_body(
        place, tile_blocks, near_count, mine, other, mine_power, other_power, near_nodes
    )
    return new_flow, coefficients, node_shift


def solution(mesh):
    groups, count = mesh.shape["groups"], mesh.shape["slab"]
    split = Mesh(mesh.devices.reshape(groups, count // 2, 2), ("groups",) + SLAB)
    in_specs = (
        P("groups", SLAB, None),
        P("groups", SLAB, None),
        P(("groups",) + SLAB),
        P("groups", SLAB),
        P("groups", SLAB),
        P("groups", SLAB),
        P("groups", None),
        P("groups"),
        P("groups", SLAB),
    )
    out_specs = (P("groups", SLAB, None), P("groups", SLAB), P("groups", SLAB))
    return jax.shard_map(
        functools.partial(shards, count), mesh=split, in_specs=in_specs, out_specs=out_specs, check_vma=False
    )
```

```python
import functools

import jax
import jax.numpy as jnp
from jax import lax
from jax.experimental import pallas as pl
from jax.experimental.pallas import tpu as pltpu
from jax.sharding import Mesh
from jax.sharding import PartitionSpec as P

FLUX_STEP = 0.2
SUPPORT = 0.15
DIAG_SHIFT = 0.5
CENTRE_SHIFT = DIAG_SHIFT + 1.0
TINY = 1e-12
DEPTH = 0.4
CHUNK = 128
MARGIN = 1e-3
BIG_LIMIT = 48 * 1024 * 1024
SMALL_LIMIT = 16 * 1024 * 1024
F32 = jnp.float32
BF16 = jnp.bfloat16
SLAB = ("chip", "core")
VMEM = pl.BlockSpec(memory_space=pltpu.VMEM)
SMEM = pl.BlockSpec(memory_space=pltpu.SMEM)
ANY = pl.BlockSpec(memory_space=pl.ANY)


def parts(values):
    first = values.astype(BF16).astype(F32)
    rest = values - first
    second = rest.astype(BF16).astype(F32)
    return first, second, rest - second


def doubled(values):
    high = values.astype(BF16)
    return jnp.concatenate([high, (values - high.astype(F32)).astype(BF16)], axis=0)


def sides(points):
    count = points.shape[1]
    squares = jnp.sum(points * points, axis=0, keepdims=True)
    one = jnp.ones((1, count), F32)
    zero = jnp.zeros((3, count), F32)
    a, b, c = parts(jnp.concatenate([points, squares, one, zero], axis=0))
    d, e, f = parts(jnp.concatenate([-2.0 * points, one, squares, zero], axis=0))
    return jnp.concatenate([a, a, b, a, c, b], axis=0), jnp.concatenate([d, e, d, f, d, e], axis=0)


def quarter_kernel(sources, targets):
    squared = jnp.maximum(jnp.dot(sources, targets, preferred_element_type=F32), TINY)
    inside = jnp.maximum(1.0 - squared * lax.rsqrt(squared), 0.0)
    square_in = inside * inside
    return square_in * square_in * (1.25 - inside)


def local_points(raw, origin):
    x = (raw[0:2] - 0.5) * (1.0 / SUPPORT)
    return jnp.concatenate([x, (raw[2:3] - origin) * (1.0 / SUPPORT)], axis=0)


def rank_of(values):
    count = values.shape[1]
    column = jnp.broadcast_to(values, (8, count)).T[:, 0:1]
    result = []
    for tile in range(count // CHUNK):
        mine = values[:, tile * CHUNK : (tile + 1) * CHUNK]
        total = jnp.zeros((8, CHUNK), F32)
        for chunk in range(count // CHUNK):
            other = column[chunk * CHUNK : (chunk + 1) * CHUNK]
            if chunk < tile:
                before = other <= mine
            elif chunk > tile:
                before = other < mine
            else:
                above = lax.broadcasted_iota(jnp.int32, (CHUNK, CHUNK), 0) < lax.broadcasted_iota(
                    jnp.int32, (CHUNK, CHUNK), 1
                )
                before = jnp.logical_or(other < mine, jnp.logical_and(other == mine, above))
            ones = jnp.where(before, 1.0, 0.0)
            for group in range(CHUNK // 8):
                total = total + ones[group * 8 : group * 8 + 8]
        result.append(jnp.sum(total, axis=0, keepdims=True))
    return jnp.concatenate(result, axis=1)


def moved(values, table, back):
    rows = values.shape[0]
    stacked = jnp.concatenate(parts(values), axis=0).astype(BF16)
    both = lax.dot_general(
        stacked, table, (((1,), (0 if back else 1,)), ((), ())), preferred_element_type=F32
    )
    return (both[:rows] + both[rows : 2 * rows]) + both[2 * rows :]


def chunk_bounds(source_z, target_z, width, low_ref, high_ref):
    chunks = source_z.shape[1] // CHUNK
    tiles = target_z.shape[1] // width

    def edges(values, size, pieces):
        rows = jnp.concatenate([values[:, i * size : (i + 1) * size] for i in range(pieces)], axis=0)
        return jnp.min(rows, axis=1, keepdims=True), jnp.max(rows, axis=1, keepdims=True)

    source_low, source_high = edges(source_z, CHUNK, chunks)
    target_low, target_high = edges(target_z, width, tiles)
    index = lax.broadcasted_iota(jnp.int32, (chunks, 1), 0).astype(F32)
    for tile in range(tiles):
        near = jnp.logical_and(
            source_high >= target_low[tile : tile + 1] - (1.0 + MARGIN),
            source_low <= target_high[tile : tile + 1] + (1.0 + MARGIN),
        )
        low_ref[tile] = jnp.min(jnp.where(near, index, float(chunks))).astype(jnp.int32)
        high_ref[tile] = jnp.max(jnp.where(near, index + 1.0, 0.0)).astype(jnp.int32)


def order_kernel(base_ref, normal_ref, centre_ref, cell_ref, nodes_ref, out_ref, centre_table, nodes_out, node_table):
    def table_of(ref, rank):
        count = rank.shape[1]
        rows = 128
        for start in range(0, count, rows):
            row = lax.broadcasted_iota(jnp.int32, (rows, count), 0).astype(F32) + float(start)
            ref[start : start + rows] = jnp.where(row == rank, 1.0, 0.0).astype(BF16)

    count = centre_ref.shape[1]
    table_of(centre_table, rank_of(centre_ref[2:3]))
    values = jnp.concatenate(
        [
            base_ref[...],
            normal_ref[...],
            centre_ref[...],
            cell_ref[...].astype(F32),
            jnp.zeros((6, count), F32),
        ],
        axis=0,
    )
    out_ref[...] = moved(values, centre_table[...], False)
    table_of(node_table, rank_of(nodes_ref[2:3]))
    nodes = jnp.concatenate([nodes_ref[...], jnp.zeros((5, nodes_ref.shape[1]), F32)], axis=0)
    nodes_out[...] = moved(nodes, node_table[...], False)


def ordered(base_shift, normals, centres, wall_cell, near_nodes):
    count, slots = centres.shape[1], near_nodes.shape[1]
    return pl.pallas_call(
        order_kernel,
        out_shape=(
            jax.ShapeDtypeStruct((16, count), F32),
            jax.ShapeDtypeStruct((count, count), BF16),
            jax.ShapeDtypeStruct((8, slots), F32),
            jax.ShapeDtypeStruct((slots, slots), BF16),
        ),
        in_specs=[VMEM] * 5,
        out_specs=(VMEM,) * 4,
        compiler_params=pltpu.CompilerParams(vmem_limit_bytes=SMALL_LIMIT),
        cost_estimate=pl.CostEstimate(flops=8_000_000, bytes_accessed=4_000_000, transcendentals=0),
        name="order",
    )(base_shift, normals, centres, wall_cell.reshape(1, -1), near_nodes)


def edge_kernel(q_ref, w_ref, a_ref, b_ref, sems):
    count = q_ref.shape[0]
    last = q_ref.shape[1] - 1
    core = lax.axis_index("core")

    def move(row_a, row_b):
        copies = [
            pltpu.make_async_copy(q_ref.at[:, row_a], a_ref.at[pl.ds(0, count)], sems.at[0]),
            pltpu.make_async_copy(q_ref.at[:, row_b], b_ref.at[pl.ds(0, count)], sems.at[1]),
            pltpu.make_async_copy(w_ref.at[pl.ds(0, 1), row_a], a_ref.at[pl.ds(count, 1)], sems.at[2]),
            pltpu.make_async_copy(w_ref.at[pl.ds(0, 1), row_b], b_ref.at[pl.ds(count, 1)], sems.at[3]),
        ]
        for copy in copies:
            copy.start()
        for copy in copies:
            copy.wait()

    @pl.when(core == 0)
    def _():
        move(last, 0)

    @pl.when(core != 0)
    def _():
        move(0, last)


def edge_rows(flow_state, flow_speed):
    count, _, plane = flow_state.shape
    rows = jax.ShapeDtypeStruct((count + 1, plane), F32)
    return pl.pallas_call(
        edge_kernel,
        out_shape=(rows, rows),
        in_specs=[ANY, ANY],
        out_specs=(VMEM, VMEM),
        scratch_shapes=[pltpu.SemaphoreType.DMA((4,))],
        compiler_params=pltpu.CompilerParams(vmem_limit_bytes=SMALL_LIMIT),
        name="edge_rows",
    )(flow_state, flow_speed)


def flux_kernel(
    q_ref, w_ref, a_ref, b_ref, sorted_ref, new_ref, out_ref
):
    count, rows, plane = q_ref.shape
    width = 512
    even = lax.axis_index("core") == 0
    pressure = 4
    rate = 0.5 * FLUX_STEP

    def chunk(step, _):
        here = pl.multiple_of(step * width, 128)
        left = pl.multiple_of(lax.rem(here + plane - 128, plane), 128)
        right = pl.multiple_of(lax.rem(here + width, plane), 128)
        below = jnp.where(even, b_ref[:, pl.ds(here, width)], a_ref[:, pl.ds(here, width)])
        above = jnp.where(even, a_ref[:, pl.ds(here, width)], b_ref[:, pl.ds(here, width)])
        row = lax.broadcasted_iota(jnp.int32, (rows, width), 0)

        def axial(values, index):
            down = jnp.where(row == 0, below[index : index + 1], pltpu.roll(values, 1, 0))
            up = jnp.where(row == rows - 1, above[index : index + 1], pltpu.roll(values, rows - 1, 0))
            return down, up

        def cyclic(ref, index):
            values = ref[index, :, pl.ds(here, width)]
            wide = jnp.concatenate(
                [ref[index, :, pl.ds(left, 128)], values, ref[index, :, pl.ds(right, 128)]], axis=1
            )
            before = pltpu.roll(wide, 1, 1)[:, 128 : 128 + width]
            after = pltpu.roll(wide, width + 255, 1)[:, 128 : 128 + width]
            return values, before, after

        w = w_ref[0, :, pl.ds(here, width)]
        w_down, w_up = axial(w, count)
        face_low = rate * (w_down + w)
        face_high = rate * (w + w_up)
        speed, speed_before, speed_after = cyclic(w_ref, 1)
        face_left = rate * (speed_before + speed)
        face_right = rate * (speed + speed_after)
        low_in = jnp.maximum(face_low, 0.0)
        high_out = jnp.minimum(face_high, 0.0)
        left_in = jnp.maximum(face_left, 0.0)
        right_out = jnp.minimum(face_right, 0.0)
        keep = 1.0 - (
            (jnp.maximum(face_high, 0.0) - jnp.minimum(face_low, 0.0))
            + (jnp.maximum(face_right, 0.0) - jnp.minimum(face_left, 0.0))
        )
        for index in range(count):
            values, before, after = cyclic(q_ref, index)
            down, up = axial(values, index)
            new_ref[index, :, pl.ds(here, width)] = (
                keep * values + low_in * down - high_out * up + left_in * before - right_out * after
            )
        return 0

    lax.fori_loop(0, plane // width, chunk, 0)

    cells = sorted_ref[9:10].astype(jnp.int32)
    lanes = plane // 128
    cell_row = cells // plane
    column = cells - cell_row * plane
    group = column // 128
    lane = column - group * 128
    stacked = jnp.concatenate(
        [new_ref[pressure, :, index * 128 : index * 128 + 128] for index in range(lanes)], axis=0
    )
    place = group * rows + cell_row
    centres = cells.shape[1]
    chosen = (lax.broadcasted_iota(jnp.int32, (rows * lanes, centres), 0) == place).astype(F32).astype(BF16)
    pieces = jnp.concatenate(parts(stacked), axis=1).astype(BF16)
    both = lax.dot_general(pieces, chosen, (((0,), (0,)), ((), ())), preferred_element_type=F32)
    picked = (both[:128] + both[128:256]) + both[256:]
    load = jnp.sum(
        jnp.where(lax.broadcasted_iota(jnp.int32, (128, centres), 0) == lane, picked, 0.0), axis=0, keepdims=True
    )
    packed = jnp.concatenate(
        [sorted_ref[0:3] + sorted_ref[3:6] * load, sorted_ref[6:9], jnp.zeros((2, centres), F32)], axis=0
    )
    for chip in range(out_ref.shape[0]):
        out_ref[chip] = packed


def flux_and_right_side(chips, flow_state, flow_speed, from_a, from_b, in_order):
    return pl.pallas_call(
        flux_kernel,
        out_shape=(
            jax.ShapeDtypeStruct(flow_state.shape, F32),
            jax.ShapeDtypeStruct((chips, 8, in_order.shape[1]), F32),
        ),
        in_specs=[VMEM] * 5,
        out_specs=(VMEM, VMEM),
        compiler_params=pltpu.CompilerParams(vmem_limit_bytes=SMALL_LIMIT),
        name="flux",
    )(flow_state, flow_speed, from_a, from_b, in_order)


def block_of(mine_ref, other_ref, block, core):
    chip = lax.div(block, 2)
    own = lax.rem(block, 2) == core
    return jnp.where(own, mine_ref[chip], other_ref[chip])


def powers_kernel(
    count, mine_ref, other_ref, out_ref, source_side, target_side, vector, tables, low_ref, high_ref
):
    size = mine_ref.shape[2]
    chip, core = lax.axis_index("chip"), lax.axis_index("core")
    me = chip * 2 + core
    slots, width, reach = 6, 256, 6
    span = reach * CHUNK
    total = slots * size
    origin = lax.div(me * 2, 5).astype(F32)
    value_row = lax.broadcasted_iota(jnp.int32, (8, size), 0) < 3

    live, zeroth, third = [], [], []
    for slot in range(slots):
        block = me + slot - 2
        valid = jnp.logical_and(block >= 0, block < count)
        live.append(valid)
        data = block_of(mine_ref, other_ref, jnp.clip(block, 0, count - 1), core)
        zeroth.append(jnp.where(jnp.logical_and(value_row, valid), data, 0.0))
        middle = (block.astype(F32) + 0.5) * DEPTH
        raw = jnp.concatenate([data[3:5], jnp.where(valid, data[5:6], middle)], axis=0)
        points = local_points(raw, origin)
        third.append(points[2:3])
        source, target = sides(points)
        source_side[slot * size : (slot + 1) * size] = source.T.astype(BF16)
        target_side[:, slot * size : (slot + 1) * size] = target.astype(BF16)
    far = (lax.broadcasted_iota(jnp.int32, (span, 48), 1) == 3).astype(F32) * 4096.0
    source_side[total:] = far.astype(BF16)
    vector[:, total:] = jnp.zeros((16, span), BF16)
    heights = jnp.concatenate(third, axis=1)
    chunk_bounds(heights, heights[:, size : 5 * size], width, low_ref, high_ref)
    tiles = 4 * size // width

    def steps_of(tile):
        return lax.div(high_ref[tile] - low_ref[tile] + (reach - 1), reach)

    def build_tile(tile, _):
        lanes = pl.ds(pl.multiple_of(tile * width + size, width), width)
        targets = target_side[:, lanes]

        def build(step, _):
            chunk = low_ref[tile] + step * reach
            rows = pl.ds(pl.multiple_of(chunk * CHUNK, CHUNK), span)
            table = quarter_kernel(source_side[rows], targets)
            high = table.astype(BF16)
            tables[tile, step, :span] = high
            tables[tile, step, span:] = (table - high.astype(F32)).astype(BF16)
            for piece in range(width // CHUNK):
                place = (tile * width + size) // CHUNK + piece - chunk

                @pl.when(jnp.logical_and(place >= 0, place < reach))
                def _(place=place, piece=piece):
                    same = lax.broadcasted_iota(jnp.int32, (CHUNK, CHUNK), 0) == lax.broadcasted_iota(
                        jnp.int32, (CHUNK, CHUNK), 1
                    )
                    for half in range(2):
                        at = pl.ds(pl.multiple_of(place * CHUNK + half * span, CHUNK), CHUNK)
                        columns = slice(piece * CHUNK, (piece + 1) * CHUNK)
                        old = tables[tile, step, at, columns].astype(F32)
                        tables[tile, step, at, columns] = jnp.where(same, 0.0, old).astype(BF16)

            return 0

        lax.fori_loop(0, steps_of(tile), build, 0)
        return 0

    lax.fori_loop(0, tiles, build_tile, 0)

    def applied(tile):
        def one(step):
            lanes = pl.ds(pl.multiple_of((low_ref[tile] + step * reach) * CHUNK, CHUNK), span)
            window = vector[:, lanes]
            return jnp.dot(
                jnp.concatenate([window, window], axis=1), tables[tile, step], preferred_element_type=F32
            )

        both = lax.fori_loop(1, steps_of(tile), lambda step, old: old + one(step), one(0))
        return 4.0 * (both[:8] + both[8:])

    def power(slot):
        first = (slot - 1) * size // width
        values = jnp.concatenate([applied(first + i) for i in range(size // width)], axis=1)
        return jnp.where(live[slot], values, 0.0)

    def hold(values, slot):
        vector[:, slot * size : (slot + 1) * size] = doubled(values)

    for slot in range(slots):
        hold(zeroth[slot], slot)
    first = {slot: power(slot) for slot in range(1, 5)}
    for slot in range(1, 5):
        hold(first[slot], slot)
    second = {slot: power(slot) for slot in range(2, 4)}
    hold(jnp.zeros((8, size), F32), 1)
    hold(second[2], 2)
    hold(2.0 * second[3], 3)
    last = power(2)

    def inner(left, right):
        return jnp.sum(left * right, axis=1, keepdims=True)

    moments = [
        inner(zeroth[2], zeroth[2]),
        inner(zeroth[2], first[2]),
        inner(first[2], first[2]),
        inner(first[2], second[2]),
        inner(second[2], second[2]),
        inner(second[2], last),
    ]
    lane = lax.broadcasted_iota(jnp.int32, (8, 128), 1)
    packed = jnp.zeros((8, 128), F32)
    for index, moment in enumerate(moments):
        packed = jnp.where(lane == index, moment, packed)
    values = jnp.concatenate([first[2][:3], second[2][:3], jnp.zeros((2, size), F32)], axis=0)
    for index in range(out_ref.shape[0]):
        out_ref[index, :, :size] = values
        out_ref[index, :, size:] = packed


def powers(mine, other, count):
    chips, _, size = mine.shape
    tiles = 4 * size // 256
    steps = (6 * size // CHUNK + 5) // 6
    return pl.pallas_call(
        functools.partial(powers_kernel, count),
        out_shape=jax.ShapeDtypeStruct((chips, 8, size + 128), F32),
        in_specs=[VMEM, VMEM],
        out_specs=VMEM,
        scratch_shapes=[
            pltpu.VMEM((6 * size + 6 * CHUNK, 48), BF16),
            pltpu.VMEM((48, 6 * size), BF16),
            pltpu.VMEM((16, 6 * size + 6 * CHUNK), BF16),
            pltpu.VMEM((tiles, steps, 12 * CHUNK, 256), BF16),
            pltpu.SMEM((tiles,), jnp.int32),
            pltpu.SMEM((tiles,), jnp.int32),
        ],
        compiler_params=pltpu.CompilerParams(vmem_limit_bytes=BIG_LIMIT),
        name="powers",
    )(mine, other)


def ratio(top, bottom):
    safe = bottom > 0.0
    return jnp.where(safe, top / jnp.where(safe, bottom, 1.0), 0.0)


def weights_of(moments):
    def inner(left, right):
        total = None
        for i, a in enumerate(left):
            for j, c in enumerate(right):
                term = a * c * moments[i + j]
                total = term if total is None else total + term
        return total

    one = jnp.ones_like(moments[0])
    residual, search = [one], [one]
    coefficients = [0.0 * one] * 3
    energy = moments[0]
    for step in range(3):
        image = [CENTRE_SHIFT * value for value in search] + [0.0 * one]
        for index, value in enumerate(search):
            image[index + 1] = image[index + 1] + value
        length = ratio(energy, inner(search, image))
        for index, value in enumerate(search):
            coefficients[index] = coefficients[index] + length * value
        if step == 2:
            break
        longer = residual + [0.0 * one]
        residual = [value - length * other for value, other in zip(longer, image)]
        fresh = jnp.maximum(inner(residual, residual), 0.0)
        scale = ratio(fresh, energy)
        search = [
            value + scale * (search[index] if index < len(search) else 0.0)
            for index, value in enumerate(residual)
        ]
        energy = fresh
    return coefficients


def near_kernel(
    tile_ref, count_ref, mine_ref, other_ref, mine_power, other_power, nodes_ref, centre_hbm, node_hbm,
    coef_ref, shift_ref,
    source_side, target_side, vector, result, centre_table, node_table, sems, low_ref, high_ref,
):
    size = mine_ref.shape[2]
    slots = nodes_ref.shape[1]
    chips = mine_ref.shape[0]
    core = lax.axis_index("core")
    me = lax.axis_index("chip") * 2 + core
    listed = tile_ref.shape[0] // count_ref.shape[0]
    width, reach = 256, 4
    span = reach * CHUNK
    total = listed * size
    copies = [
        pltpu.make_async_copy(centre_hbm, centre_table, sems.at[0]),
        pltpu.make_async_copy(node_hbm, node_table, sems.at[1]),
    ]
    for copy in copies:
        copy.start()

    summed = mine_power[0, :, size:] + other_power[0, :, size:]
    for index in range(1, chips):
        summed = summed + (mine_power[index, :, size:] + other_power[index, :, size:])
    weights = weights_of([summed[:, index : index + 1] for index in range(6)])

    def coefficients_of(block):
        data = block_of(mine_ref, other_ref, block, core)
        power = block_of(mine_power, other_power, block, core)[:, :size]
        values = weights[0] * data + weights[1] * power + weights[2] * pltpu.roll(power, 5, 0)
        keep = lax.broadcasted_iota(jnp.int32, (8, size), 0) < 3
        return data, jnp.where(keep, values, 0.0)

    origin = lax.div((tile_ref[me * listed] + 2) * 2, 5).astype(F32)
    third = []
    for index in range(listed):
        data, values = coefficients_of(tile_ref[me * listed + index])
        points = local_points(data[3:6], origin)
        third.append(points[2:3])
        source, _ = sides(points)
        source_side[index * size : (index + 1) * size] = source.T.astype(BF16)
        vector[:, index * size : (index + 1) * size] = doubled(values)
    far = (lax.broadcasted_iota(jnp.int32, (span, 48), 1) == 3).astype(F32) * 4096.0
    source_side[total:] = far.astype(BF16)
    vector[:, total:] = jnp.zeros((16, span), BF16)
    points = local_points(nodes_ref[0:3], origin)
    _, target = sides(points)
    target_side[...] = target.astype(BF16)
    chunk_bounds(jnp.concatenate(third, axis=1), points[2:3], width, low_ref, high_ref)

    def node_tile(tile, _):
        lanes = pl.ds(pl.multiple_of(tile * width, width), width)
        targets = target_side[:, lanes]

        def one(step, old):
            start = pl.multiple_of((low_ref[tile] + step * reach) * CHUNK, CHUNK)
            table = quarter_kernel(source_side[pl.ds(start, span)], targets)
            window = vector[:, pl.ds(start, span)]
            return old + jnp.dot(
                jnp.concatenate([window, window], axis=1), doubled(table), preferred_element_type=F32
            )

        steps = lax.div(high_ref[tile] - low_ref[tile] + (reach - 1), reach)
        both = lax.fori_loop(0, steps, one, jnp.zeros((16, width), F32))
        result[:, lanes] = 4.0 * (both[:8] + both[8:])
        return 0

    lax.fori_loop(0, slots // width, node_tile, 0)
    for copy in copies:
        copy.wait()
    coef_ref[...] = moved(coefficients_of(me)[1], centre_table[...], True)[:3]
    slot = lax.broadcasted_iota(jnp.int32, (3, slots), 1)
    shift_ref[...] = jnp.where(slot < count_ref[me], moved(result[...], node_table[...], True)[:3], 0.0)


def near_body(tile_blocks, near_count, mine, other, mine_power, other_power, nodes, centre_table, node_table):
    size = mine.shape[2]
    slots = nodes.shape[1]
    total = tile_blocks.shape[1] * size
    return pl.pallas_call(
        near_kernel,
        out_shape=(
            jax.ShapeDtypeStruct((3, size), F32),
            jax.ShapeDtypeStruct((3, slots), F32),
        ),
        in_specs=[SMEM, SMEM] + [VMEM] * 5 + [ANY, ANY],
        out_specs=(VMEM, VMEM),
        scratch_shapes=[
            pltpu.VMEM((total + 4 * CHUNK, 48), BF16),
            pltpu.VMEM((48, slots), BF16),
            pltpu.VMEM((16, total + 4 * CHUNK), BF16),
            pltpu.VMEM((8, slots), F32),
            pltpu.VMEM((size, size), BF16),
            pltpu.VMEM((slots, slots), BF16),
            pltpu.SemaphoreType.DMA((2,)),
            pltpu.SMEM((slots // 256,), jnp.int32),
            pltpu.SMEM((slots // 256,), jnp.int32),
        ],
        compiler_params=pltpu.CompilerParams(vmem_limit_bytes=SMALL_LIMIT),
        name="near_body",
    )(tile_blocks.reshape(-1), near_count, mine, other, mine_power, other_power, nodes, centre_table, node_table)


def gathered(values, count, partner):
    mine = lax.all_to_all(values, "chip", 0, 0)
    return mine, lax.ppermute(mine, SLAB, partner)


def shards(
    count,
    flow_state,
    flow_speed,
    wall_cell,
    base_shift,
    normals,
    centres,
    tile_blocks,
    near_count,
    near_nodes,
):
    partner = [(i, i ^ 1) for i in range(count)]
    across = [(i, i + 1) for i in range(1, count - 1, 2)]
    across = across + [(j, i) for i, j in across]
    send_a, send_b = edge_rows(flow_state, flow_speed)
    from_a = lax.ppermute(send_a, SLAB, partner)
    from_b = lax.ppermute(send_b, SLAB, across)
    in_order, centre_table, nodes, node_table = ordered(base_shift, normals, centres, wall_cell, near_nodes)
    new_flow, packed = flux_and_right_side(count // 2, flow_state, flow_speed, from_a, from_b, in_order)
    mine, other = gathered(packed, count, partner)
    mine_power, other_power = gathered(powers(mine, other, count), count, partner)
    coefficients, node_shift = near_body(
        tile_blocks, near_count, mine, other, mine_power, other_power, nodes, centre_table, node_table
    )
    return new_flow, coefficients, node_shift


def solution(mesh):
    groups, count = mesh.shape["groups"], mesh.shape["slab"]
    split = Mesh(mesh.devices.reshape(groups, count // 2, 2), ("groups",) + SLAB)
    in_specs = (
        P("groups", SLAB, None),
        P("groups", SLAB, None),
        P(("groups",) + SLAB),
        P("groups", SLAB),
        P("groups", SLAB),
        P("groups", SLAB),
        P("groups", None),
        P("groups"),
        P("groups", SLAB),
    )
    out_specs = (P("groups", SLAB, None), P("groups", SLAB), P("groups", SLAB))
    return jax.shard_map(
        functools.partial(shards, count), mesh=split, in_specs=in_specs, out_specs=out_specs, check_vma=False
    )
```

```python
import functools

import jax
import jax.numpy as jnp
from jax import lax
from jax.experimental import pallas as pl
from jax.experimental.pallas import tpu as pltpu
from jax.sharding import Mesh
from jax.sharding import PartitionSpec as P

FLUX_STEP = 0.2
SUPPORT = 0.15
DIAG_SHIFT = 0.5
CENTRE_SHIFT = DIAG_SHIFT + 1.0
TINY = 1e-12
DEPTH = 0.4
CHUNK = 128
MARGIN = 1e-3
BIG_LIMIT = 48 * 1024 * 1024
SMALL_LIMIT = 16 * 1024 * 1024
F32 = jnp.float32
BF16 = jnp.bfloat16
SLAB = ("chip", "core")
VMEM = pl.BlockSpec(memory_space=pltpu.VMEM)
SMEM = pl.BlockSpec(memory_space=pltpu.SMEM)
HBM = pl.BlockSpec(memory_space=pltpu.HBM)


def parts(values):
    first = values.astype(BF16).astype(F32)
    rest = values - first
    second = rest.astype(BF16).astype(F32)
    return first, second, rest - second


def doubled(values):
    high = values.astype(BF16)
    return jnp.concatenate([high, (values - high.astype(F32)).astype(BF16)], axis=0)


def sides(points):
    count = points.shape[1]
    squares = jnp.sum(points * points, axis=0, keepdims=True)
    one = jnp.ones((1, count), F32)
    zero = jnp.zeros((3, count), F32)
    a, b, c = parts(jnp.concatenate([points, squares, one, zero], axis=0))
    d, e, f = parts(jnp.concatenate([-2.0 * points, one, squares, zero], axis=0))
    return jnp.concatenate([a, a, b, a, c, b], axis=0), jnp.concatenate([d, e, d, f, d, e], axis=0)


def quarter_kernel(sources, targets):
    squared = jnp.maximum(jnp.dot(sources, targets, preferred_element_type=F32), TINY)
    inside = jnp.maximum(1.0 - squared * lax.rsqrt(squared), 0.0)
    square_in = inside * inside
    return square_in * square_in * (1.25 - inside)


def local_points(raw, origin):
    x = (raw[0:2] - 0.5) * (1.0 / SUPPORT)
    return jnp.concatenate([x, (raw[2:3] - origin) * (1.0 / SUPPORT)], axis=0)


def rank_of(values):
    count = values.shape[1]
    column = jnp.broadcast_to(values, (8, count)).T[:, 0:1]
    result = []
    for tile in range(count // CHUNK):
        mine = values[:, tile * CHUNK : (tile + 1) * CHUNK]
        total = jnp.zeros((8, CHUNK), F32)
        for chunk in range(count // CHUNK):
            other = column[chunk * CHUNK : (chunk + 1) * CHUNK]
            if chunk < tile:
                before = other <= mine
            elif chunk > tile:
                before = other < mine
            else:
                above = lax.broadcasted_iota(jnp.int32, (CHUNK, CHUNK), 0) < lax.broadcasted_iota(
                    jnp.int32, (CHUNK, CHUNK), 1
                )
                before = jnp.logical_or(other < mine, jnp.logical_and(other == mine, above))
            ones = jnp.where(before, 1.0, 0.0)
            for group in range(CHUNK // 8):
                total = total + ones[group * 8 : group * 8 + 8]
        result.append(jnp.sum(total, axis=0, keepdims=True))
    return jnp.concatenate(result, axis=1)


def moved(values, table, back):
    rows = values.shape[0]
    stacked = jnp.concatenate(parts(values), axis=0).astype(BF16)
    both = lax.dot_general(
        stacked, table, (((1,), (0 if back else 1,)), ((), ())), preferred_element_type=F32
    )
    return (both[:rows] + both[rows : 2 * rows]) + both[2 * rows :]


def chunk_bounds(source_z, target_z, width, low_ref, high_ref):
    chunks = source_z.shape[1] // CHUNK
    tiles = target_z.shape[1] // width

    def edges(values, size, pieces):
        rows = jnp.concatenate([values[:, i * size : (i + 1) * size] for i in range(pieces)], axis=0)
        return jnp.min(rows, axis=1, keepdims=True), jnp.max(rows, axis=1, keepdims=True)

    source_low, source_high = edges(source_z, CHUNK, chunks)
    target_low, target_high = edges(target_z, width, tiles)
    index = lax.broadcasted_iota(jnp.int32, (chunks, 1), 0).astype(F32)
    for tile in range(tiles):
        near = jnp.logical_and(
            source_high >= target_low[tile : tile + 1] - (1.0 + MARGIN),
            source_low <= target_high[tile : tile + 1] + (1.0 + MARGIN),
        )
        low_ref[tile] = jnp.min(jnp.where(near, index, float(chunks))).astype(jnp.int32)
        high_ref[tile] = jnp.max(jnp.where(near, index + 1.0, 0.0)).astype(jnp.int32)


def order_kernel(base_ref, normal_ref, centre_ref, cell_ref, nodes_ref, out_ref, centre_table, nodes_out, node_table):
    def table_of(ref, rank):
        count = rank.shape[1]
        rows = 128
        for start in range(0, count, rows):
            row = lax.broadcasted_iota(jnp.int32, (rows, count), 0).astype(F32) + float(start)
            ref[start : start + rows] = jnp.where(row == rank, 1.0, 0.0).astype(BF16)

    count = centre_ref.shape[1]
    table_of(centre_table, rank_of(centre_ref[2:3]))
    values = jnp.concatenate(
        [
            base_ref[...],
            normal_ref[...],
            centre_ref[...],
            cell_ref[...].astype(F32),
            jnp.zeros((6, count), F32),
        ],
        axis=0,
    )
    out_ref[...] = moved(values, centre_table[...], False)
    table_of(node_table, rank_of(nodes_ref[2:3]))
    nodes = jnp.concatenate([nodes_ref[...], jnp.zeros((5, nodes_ref.shape[1]), F32)], axis=0)
    nodes_out[...] = moved(nodes, node_table[...], False)


def ordered(base_shift, normals, centres, wall_cell, near_nodes):
    count, slots = centres.shape[1], near_nodes.shape[1]
    return pl.pallas_call(
        order_kernel,
        out_shape=(
            jax.ShapeDtypeStruct((16, count), F32),
            jax.ShapeDtypeStruct((count, count), BF16),
            jax.ShapeDtypeStruct((8, slots), F32),
            jax.ShapeDtypeStruct((slots, slots), BF16),
        ),
        in_specs=[VMEM] * 5,
        out_specs=(VMEM,) * 4,
        compiler_params=pltpu.CompilerParams(vmem_limit_bytes=SMALL_LIMIT),
        cost_estimate=pl.CostEstimate(flops=8_000_000, bytes_accessed=4_000_000, transcendentals=0),
        name="order",
    )(base_shift, normals, centres, wall_cell.reshape(1, -1), near_nodes)


def edge_kernel(q_hbm, w_hbm, a_ref, b_ref, q_ref, w_ref, sems):
    count, rows, _ = q_ref.shape
    copies = [pltpu.make_async_copy(w_hbm.at[index], w_ref.at[index], sems.at[index]) for index in range(2)]
    copies += [
        pltpu.make_async_copy(q_hbm.at[index], q_ref.at[index], sems.at[2 + index]) for index in range(count)
    ]
    for copy in copies:
        copy.start()
    core = lax.axis_index("core")
    for copy in copies:
        copy.wait()

    def move(row_a, row_b):
        for target, row in ((a_ref, row_a), (b_ref, row_b)):
            for index in range(count):
                target[index : index + 1] = q_ref[index, row : row + 1]
            target[count : count + 1] = w_ref[0, row : row + 1]

    @pl.when(core == 0)
    def _():
        move(rows - 1, 0)

    @pl.when(core != 0)
    def _():
        move(0, rows - 1)


def edge_rows(flow_state, flow_speed):
    count, _, plane = flow_state.shape
    rows = jax.ShapeDtypeStruct((count + 1, plane), F32)
    return pl.pallas_call(
        edge_kernel,
        out_shape=(
            rows,
            rows,
            jax.ShapeDtypeStruct(flow_state.shape, F32),
            jax.ShapeDtypeStruct(flow_speed.shape, F32),
        ),
        in_specs=[HBM, HBM],
        out_specs=(VMEM,) * 4,
        scratch_shapes=[pltpu.SemaphoreType.DMA((count + 2,))],
        compiler_params=pltpu.CompilerParams(vmem_limit_bytes=SMALL_LIMIT),
        name="edge_rows",
    )(flow_state, flow_speed)


RATE = 0.5 * FLUX_STEP
PRESSURE = 4


def picked(stacked, chosen, lane):
    high, middle, low = parts(stacked)
    pieces = jnp.concatenate([high, middle, low], axis=1).astype(BF16)
    both = lax.dot_general(pieces, chosen, (((0,), (0,)), ((), ())), preferred_element_type=F32)
    value = (both[:128] + both[128:256]) + both[256:]
    here = lax.broadcasted_iota(jnp.int32, value.shape, 0) == lane
    return jnp.sum(jnp.where(here, value, 0.0), axis=0, keepdims=True)


def stacked_lanes(values):
    return jnp.concatenate([values[:, i : i + 128] for i in range(0, values.shape[1], 128)], axis=0)


def inner_kernel(q_ref, w_ref, sorted_ref, new_hbm, low_ref, high_ref, out_ref, chosen_ref, new_ref, sems):
    count, rows, plane = q_ref.shape
    width = 512
    steps = plane // width
    row = lax.broadcasted_iota(jnp.int32, (rows, width), 0)

    def copy_of(step):
        lanes = pl.ds(pl.multiple_of(step * width, width), width)
        return pltpu.make_async_copy(new_ref.at[:, :, lanes], new_hbm.at[:, :, lanes], sems.at[step])

    def chunk(step, _):
        here = pl.multiple_of(step * width, 128)
        left = pl.multiple_of(lax.rem(here + plane - 128, plane), 128)
        right = pl.multiple_of(lax.rem(here + width, plane), 128)

        def cyclic(ref, index):
            values = ref[index, :, pl.ds(here, width)]
            wide = jnp.concatenate(
                [ref[index, :, pl.ds(left, 128)], values, ref[index, :, pl.ds(right, 128)]], axis=1
            )
            before = pltpu.roll(wide, 1, 1)[:, 128 : 128 + width]
            after = pltpu.roll(wide, width + 255, 1)[:, 128 : 128 + width]
            return values, before, after

        w = w_ref[0, :, pl.ds(here, width)]
        face_low = jnp.where(row == 0, 0.0, RATE * (pltpu.roll(w, 1, 0) + w))
        face_high = jnp.where(row == rows - 1, 0.0, RATE * (w + pltpu.roll(w, rows - 1, 0)))
        speed, speed_before, speed_after = cyclic(w_ref, 1)
        face_left = RATE * (speed_before + speed)
        face_right = RATE * (speed + speed_after)
        low_in = jnp.maximum(face_low, 0.0)
        high_out = jnp.minimum(face_high, 0.0)
        left_in = jnp.maximum(face_left, 0.0)
        right_out = jnp.minimum(face_right, 0.0)
        keep = 1.0 - (
            (jnp.maximum(face_high, 0.0) - jnp.minimum(face_low, 0.0))
            + (jnp.maximum(face_right, 0.0) - jnp.minimum(face_left, 0.0))
        )
        for index in range(count):
            values, before, after = cyclic(q_ref, index)
            new = (
                keep * values
                + low_in * pltpu.roll(values, 1, 0)
                - high_out * pltpu.roll(values, rows - 1, 0)
                + left_in * before
                - right_out * after
            )
            new_ref[index, :, pl.ds(here, width)] = new
            low_ref[index : index + 1, pl.ds(here, width)] = new[0:1]
            high_ref[index : index + 1, pl.ds(here, width)] = new[rows - 1 : rows]
        copy_of(step).start()
        return 0

    lax.fori_loop(0, steps, chunk, 0)

    cells = sorted_ref[9:10].astype(jnp.int32)
    cell_row = cells // plane
    column = cells - cell_row * plane
    group = column // 128
    lane = column - group * 128
    place = group * rows + cell_row
    centres = cells.shape[1]
    lanes = plane // 128
    chosen = (lax.broadcasted_iota(jnp.int32, (rows * lanes, centres), 0) == place).astype(F32).astype(BF16)
    chosen_ref[...] = chosen
    load = picked(stacked_lanes(new_ref[PRESSURE]), chosen, lane)
    out_ref[...] = jnp.concatenate(
        [
            sorted_ref[0:3] + sorted_ref[3:6] * load,
            sorted_ref[3:9],
            lane.astype(F32),
            jnp.zeros((6, centres), F32),
        ],
        axis=0,
    )
    for step in range(steps):
        copy_of(step).wait()


def inner_flux(flow_state, flow_speed, in_order):
    count, rows, plane = flow_state.shape
    centres = in_order.shape[1]
    edge = jax.ShapeDtypeStruct((count, plane), F32)
    return pl.pallas_call(
        inner_kernel,
        out_shape=(
            jax.ShapeDtypeStruct(flow_state.shape, F32),
            edge,
            edge,
            jax.ShapeDtypeStruct((16, centres), F32),
            jax.ShapeDtypeStruct((rows * plane // 128, centres), BF16),
        ),
        in_specs=[VMEM] * 3,
        out_specs=(HBM, VMEM, VMEM, VMEM, VMEM),
        scratch_shapes=[pltpu.VMEM(flow_state.shape, F32), pltpu.SemaphoreType.DMA((plane // 512,))],
        compiler_params=pltpu.CompilerParams(vmem_limit_bytes=SMALL_LIMIT),
        cost_estimate=pl.CostEstimate(flops=20_000_000, bytes_accessed=4_000_000, transcendentals=0),
        name="inner_flux",
    )(flow_state, flow_speed, in_order)


def outer_kernel(
    send_a, send_b, from_a, from_b, low_ref, high_ref, base_ref, chosen_ref, out_ref, new_low, new_high, both_ref
):
    count, plane = low_ref.shape
    rows = both_ref.shape[0]
    even = lax.axis_index("core") == 0
    own_low = jnp.where(even, send_b[...], send_a[...])
    own_high = jnp.where(even, send_a[...], send_b[...])
    below = jnp.where(even, from_b[...], from_a[...])
    above = jnp.where(even, from_a[...], from_b[...])

    def flux(first, second):
        face = RATE * (first[count : count + 1] + second[count : count + 1])
        return jnp.maximum(face, 0.0) * first[:count] + jnp.minimum(face, 0.0) * second[:count]

    low = flux(below, own_low)
    high = flux(own_high, above)
    new_low[...] = low_ref[...] + low
    new_high[...] = high_ref[...] - high
    row = lax.broadcasted_iota(jnp.int32, (rows, plane), 0)
    zero = jnp.zeros((rows, plane), F32)
    added = jnp.where(row == 0, low[PRESSURE : PRESSURE + 1], zero)
    added = added - jnp.where(row == rows - 1, high[PRESSURE : PRESSURE + 1], zero)
    both_ref[...] = added
    base = base_ref[...]
    load = picked(stacked_lanes(both_ref[...]), chosen_ref[...], base[9:10].astype(jnp.int32))
    centres = base.shape[1]
    packed = jnp.concatenate([base[0:3] + base[3:6] * load, base[6:9], jnp.zeros((2, centres), F32)], axis=0)
    for chip in range(out_ref.shape[0]):
        out_ref[chip] = packed


def right_side(chips, rows, send_a, send_b, from_a, from_b, low, high, base, chosen):
    edge = jax.ShapeDtypeStruct(low.shape, F32)
    return pl.pallas_call(
        outer_kernel,
        out_shape=(jax.ShapeDtypeStruct((chips, 8, base.shape[1]), F32), edge, edge),
        in_specs=[VMEM] * 8,
        out_specs=(VMEM,) * 3,
        scratch_shapes=[pltpu.VMEM((rows, low.shape[1]), F32)],
        compiler_params=pltpu.CompilerParams(vmem_limit_bytes=SMALL_LIMIT),
        name="outer_flux",
    )(send_a, send_b, from_a, from_b, low, high, base, chosen)


def block_of(mine_ref, other_ref, block, core):
    chip = lax.div(block, 2)
    own = lax.rem(block, 2) == core
    return jnp.where(own, mine_ref[chip], other_ref[chip])


def powers_kernel(
    count, mine_ref, other_ref, new_low, new_high, new_in, out_ref, new_out,
    source_side, target_side, vector, image, tables, low_ref, high_ref, sems,
):
    del new_in
    rows_per_block = new_out.shape[1]
    copies = [
        pltpu.make_async_copy(new_low, new_out.at[:, 0], sems.at[0]),
        pltpu.make_async_copy(new_high, new_out.at[:, rows_per_block - 1], sems.at[1]),
    ]
    for copy in copies:
        copy.start()
    size = mine_ref.shape[2]
    chip, core = lax.axis_index("chip"), lax.axis_index("core")
    me = chip * 2 + core
    slots, width, reach = 6, 256, 6
    span = reach * CHUNK
    total = slots * size
    origin = lax.div(me * 2, 5).astype(F32)
    value_row = lax.broadcasted_iota(jnp.int32, (8, size), 0) < 3

    live, zeroth, third = [], [], []
    for slot in range(slots):
        block = me + slot - 2
        valid = jnp.logical_and(block >= 0, block < count)
        live.append(valid)
        data = block_of(mine_ref, other_ref, jnp.clip(block, 0, count - 1), core)
        zeroth.append(jnp.where(jnp.logical_and(value_row, valid), data, 0.0))
        middle = (block.astype(F32) + 0.5) * DEPTH
        raw = jnp.concatenate([data[3:5], jnp.where(valid, data[5:6], middle)], axis=0)
        points = local_points(raw, origin)
        third.append(points[2:3])
        source, target = sides(points)
        source_side[slot * size : (slot + 1) * size] = source.T.astype(BF16)
        target_side[:, slot * size : (slot + 1) * size] = target.astype(BF16)
    far = (lax.broadcasted_iota(jnp.int32, (span, 48), 1) == 3).astype(F32) * 4096.0
    source_side[total:] = far.astype(BF16)
    vector[:, total:] = jnp.zeros((16, span), BF16)
    heights = jnp.concatenate(third, axis=1)
    chunk_bounds(heights, heights[:, size : 5 * size], width, low_ref, high_ref)
    tiles = 4 * size // width

    def steps_of(tile):
        return lax.div(high_ref[tile] - low_ref[tile] + (reach - 1), reach)

    most = steps_of(0)
    for tile in range(1, tiles):
        most = jnp.maximum(most, steps_of(tile))
    same = lax.broadcasted_iota(jnp.int32, (CHUNK, CHUNK), 0) == lax.broadcasted_iota(
        jnp.int32, (CHUNK, CHUNK), 1
    )

    def build(tile, step):
        lanes = pl.ds(pl.multiple_of(tile * width + size, width), width)
        chunk = low_ref[tile] + step * reach
        rows = pl.ds(pl.multiple_of(chunk * CHUNK, CHUNK), span)
        table = quarter_kernel(source_side[rows], target_side[:, lanes])
        high = table.astype(BF16)
        tables[tile, step, :span] = high
        tables[tile, step, span:] = (table - high.astype(F32)).astype(BF16)
        for piece in range(width // CHUNK):
            place = (tile * width + size) // CHUNK + piece - chunk
            inside = jnp.logical_and(place >= 0, place < reach)
            place = jnp.clip(place, 0, reach - 1)
            for half in range(2):
                at = pl.ds(pl.multiple_of(place * CHUNK + half * span, CHUNK), CHUNK)
                columns = slice(piece * CHUNK, (piece + 1) * CHUNK)
                old = tables[tile, step, at, columns]
                tables[tile, step, at, columns] = jnp.where(jnp.logical_and(same, inside), 0.0, old.astype(F32)).astype(BF16)

    def one(tile, step):
        lanes = pl.ds(pl.multiple_of((low_ref[tile] + step * reach) * CHUNK, CHUNK), span)
        window = vector[:, lanes]
        return jnp.dot(jnp.concatenate([window, window], axis=1), tables[tile, step], preferred_element_type=F32)

    def lanes_of(tile):
        return pl.ds(pl.multiple_of(tile * width, width), width)

    def further(first, last):
        @pl.when(most > 1)
        def _():
            def of_tile(tile, _):
                def add(step, _):
                    image[:, lanes_of(tile)] += one(tile, step)
                    return 0

                return lax.fori_loop(1, steps_of(tile), add, 0)

            lax.fori_loop(first, last, of_tile, 0)

    def image_of(slot):
        both = image[:, (slot - 1) * size : slot * size]
        return jnp.where(live[slot], 4.0 * (both[:8] + both[8:]), 0.0)

    def power(slots):
        first, last = (slots[0] - 1) * size // width, slots[-1] * size // width
        for tile in range(first, last):
            image[:, tile * width : (tile + 1) * width] = one(tile, 0)
        further(first, last)
        return {slot: image_of(slot) for slot in slots}

    def hold(values, slot):
        vector[:, slot * size : (slot + 1) * size] = doubled(values)

    for slot in range(slots):
        hold(zeroth[slot], slot)

    def tile_step(tile, _):
        before = jnp.maximum(tile - 1, 0)
        image[:, lanes_of(before)] = one(before, 0)
        build(tile, 0)
        return 0

    build(0, 0)
    lax.fori_loop(1, tiles, tile_step, 0)
    image[:, (tiles - 1) * width : tiles * width] = one(tiles - 1, 0)

    @pl.when(most > 1)
    def _():
        def of_tile(tile, _):
            def more(step, _):
                build(tile, step)
                return 0

            return lax.fori_loop(1, steps_of(tile), more, 0)

        lax.fori_loop(0, tiles, of_tile, 0)

    further(0, tiles)
    first = {slot: image_of(slot) for slot in range(1, 5)}
    for slot in range(1, 5):
        hold(first[slot], slot)
    second = power([2, 3])
    hold(jnp.zeros((8, size), F32), 1)
    hold(second[2], 2)
    hold(2.0 * second[3], 3)
    last = power([2])[2]

    def inner(left, right):
        return jnp.sum(left * right, axis=1, keepdims=True)

    moments = [
        inner(zeroth[2], zeroth[2]),
        inner(zeroth[2], first[2]),
        inner(first[2], first[2]),
        inner(first[2], second[2]),
        inner(second[2], second[2]),
        inner(second[2], last),
    ]
    lane = lax.broadcasted_iota(jnp.int32, (8, 128), 1)
    packed = jnp.zeros((8, 128), F32)
    for index, moment in enumerate(moments):
        packed = jnp.where(lane == index, moment, packed)
    values = jnp.concatenate([first[2][:3], second[2][:3], jnp.zeros((2, size), F32)], axis=0)
    for index in range(out_ref.shape[0]):
        out_ref[index, :, :size] = values
        out_ref[index, :, size:] = packed
    for copy in copies:
        copy.wait()


def powers(mine, other, new_low, new_high, new_flow, count):
    chips, _, size = mine.shape
    tiles = 4 * size // 256
    steps = (6 * size // CHUNK + 5) // 6
    return pl.pallas_call(
        functools.partial(powers_kernel, count),
        out_shape=(
            jax.ShapeDtypeStruct((chips, 8, size + 128), F32),
            jax.ShapeDtypeStruct(new_flow.shape, F32),
        ),
        in_specs=[VMEM] * 4 + [HBM],
        out_specs=(VMEM, HBM),
        scratch_shapes=[
            pltpu.VMEM((6 * size + 6 * CHUNK, 48), BF16),
            pltpu.VMEM((48, 6 * size), BF16),
            pltpu.VMEM((16, 6 * size + 6 * CHUNK), BF16),
            pltpu.VMEM((16, 4 * size), F32),
            pltpu.VMEM((tiles, steps, 12 * CHUNK, 256), BF16),
            pltpu.SMEM((tiles,), jnp.int32),
            pltpu.SMEM((tiles,), jnp.int32),
            pltpu.SemaphoreType.DMA((2,)),
        ],
        input_output_aliases={4: 1},
        compiler_params=pltpu.CompilerParams(vmem_limit_bytes=BIG_LIMIT),
        name="powers",
    )(mine, other, new_low, new_high, new_flow)


def ratio(top, bottom):
    safe = bottom > 0.0
    return jnp.where(safe, top / jnp.where(safe, bottom, 1.0), 0.0)


def weights_of(moments):
    def inner(left, right):
        total = None
        for i, a in enumerate(left):
            for j, c in enumerate(right):
                term = a * c * moments[i + j]
                total = term if total is None else total + term
        return total

    one = jnp.ones_like(moments[0])
    residual, search = [one], [one]
    coefficients = [0.0 * one] * 3
    energy = moments[0]
    for step in range(3):
        image = [CENTRE_SHIFT * value for value in search] + [0.0 * one]
        for index, value in enumerate(search):
            image[index + 1] = image[index + 1] + value
        length = ratio(energy, inner(search, image))
        for index, value in enumerate(search):
            coefficients[index] = coefficients[index] + length * value
        if step == 2:
            break
        longer = residual + [0.0 * one]
        residual = [value - length * other for value, other in zip(longer, image)]
        fresh = jnp.maximum(inner(residual, residual), 0.0)
        scale = ratio(fresh, energy)
        search = [
            value + scale * (search[index] if index < len(search) else 0.0)
            for index, value in enumerate(residual)
        ]
        energy = fresh
    return coefficients


REACH = 7


def points_kernel(tile_ref, mine_ref, other_ref, nodes_ref, source_ref, target_ref, low_ref, high_ref):
    size = mine_ref.shape[2]
    core = lax.axis_index("core")
    me = lax.axis_index("chip") * 2 + core
    listed = tile_ref.shape[0] // (2 * mine_ref.shape[0])
    origin = lax.div((tile_ref[me * listed] + 2) * 2, 5).astype(F32)
    third = []
    for index in range(listed):
        data = block_of(mine_ref, other_ref, tile_ref[me * listed + index], core)
        points = local_points(data[3:6], origin)
        third.append(points[2:3])
        source, _ = sides(points)
        source_ref[index * size : (index + 1) * size] = source.T.astype(BF16)
    span = REACH * CHUNK
    far = (lax.broadcasted_iota(jnp.int32, (span, 48), 1) == 3).astype(F32) * 4096.0
    source_ref[listed * size :] = far.astype(BF16)
    points = local_points(nodes_ref[0:3], origin)
    _, target = sides(points)
    target_ref[...] = target.astype(BF16)
    chunk_bounds(jnp.concatenate(third, axis=1), points[2:3], CHUNK, low_ref, high_ref)


def near_points(tiles, listed, mine, other, nodes):
    size = mine.shape[2]
    slots = nodes.shape[1]
    bounds = jax.ShapeDtypeStruct((slots // CHUNK,), jnp.int32)
    return pl.pallas_call(
        points_kernel,
        out_shape=(
            jax.ShapeDtypeStruct((listed * size + REACH * CHUNK, 48), BF16),
            jax.ShapeDtypeStruct((48, slots), BF16),
            bounds,
            bounds,
        ),
        in_specs=[SMEM] + [VMEM] * 3,
        out_specs=(VMEM, VMEM, SMEM, SMEM),
        compiler_params=pltpu.CompilerParams(vmem_limit_bytes=SMALL_LIMIT),
        cost_estimate=pl.CostEstimate(flops=1_000_000, bytes_accessed=1_000_000, transcendentals=0),
        name="near_points",
    )(tiles, mine, other, nodes)


def near_kernel(
    tile_ref, count_ref, low_ref, high_ref, mine_ref, other_ref, mine_power, other_power, source_side, target_side,
    centre_table, node_table, coef_ref, shift_ref, vector, result,
):
    size = mine_ref.shape[2]
    slots = target_side.shape[1]
    chips = mine_ref.shape[0]
    core = lax.axis_index("core")
    me = lax.axis_index("chip") * 2 + core
    listed = tile_ref.shape[0] // count_ref.shape[0]
    width = CHUNK
    span = REACH * CHUNK
    total = listed * size

    summed = mine_power[0, :, size:] + other_power[0, :, size:]
    for index in range(1, chips):
        summed = summed + (mine_power[index, :, size:] + other_power[index, :, size:])
    weights = weights_of([summed[:, index : index + 1] for index in range(6)])

    def coefficients_of(block):
        data = block_of(mine_ref, other_ref, block, core)
        power = block_of(mine_power, other_power, block, core)[:, :size]
        values = weights[0] * data + weights[1] * power + weights[2] * pltpu.roll(power, 5, 0)
        keep = lax.broadcasted_iota(jnp.int32, (8, size), 0) < 3
        return jnp.where(keep, values, 0.0)

    for index in range(listed):
        values = coefficients_of(tile_ref[me * listed + index])
        vector[:, index * size : (index + 1) * size] = doubled(values)
    vector[:, total:] = jnp.zeros((16, span), BF16)

    def node_tile(tile, _):
        lanes = pl.ds(pl.multiple_of(tile * width, width), width)
        targets = target_side[:, lanes]

        def one(step, old):
            start = pl.multiple_of((low_ref[tile] + step * REACH) * CHUNK, CHUNK)
            table = quarter_kernel(source_side[pl.ds(start, span)], targets)
            window = vector[:, pl.ds(start, span)]
            return old + jnp.dot(
                jnp.concatenate([window, window], axis=1), doubled(table), preferred_element_type=F32
            )

        steps = lax.div(high_ref[tile] - low_ref[tile] + (REACH - 1), REACH)
        both = lax.fori_loop(0, steps, one, jnp.zeros((16, width), F32))
        result[:, lanes] = 4.0 * (both[:8] + both[8:])
        return 0

    lax.fori_loop(0, slots // width, node_tile, 0)
    coef_ref[...] = moved(coefficients_of(me), centre_table[...], True)[:3]
    slot = lax.broadcasted_iota(jnp.int32, (3, slots), 1)
    shift_ref[...] = jnp.where(slot < count_ref[me], moved(result[...], node_table[...], True)[:3], 0.0)


def near_body(tiles, listed, near_count, low, high, mine, other, mine_power, other_power, sources, targets, centre_table, node_table):
    size = mine.shape[2]
    slots = targets.shape[1]
    total = listed * size
    return pl.pallas_call(
        near_kernel,
        out_shape=(
            jax.ShapeDtypeStruct((3, size), F32),
            jax.ShapeDtypeStruct((3, slots), F32),
        ),
        in_specs=[SMEM] * 4 + [VMEM] * 8,
        out_specs=(VMEM, VMEM),
        scratch_shapes=[
            pltpu.VMEM((16, total + REACH * CHUNK), BF16),
            pltpu.VMEM((8, slots), F32),
        ],
        compiler_params=pltpu.CompilerParams(vmem_limit_bytes=SMALL_LIMIT),
        name="near_body",
    )(tiles, near_count, low, high, mine, other, mine_power, other_power, sources, targets, centre_table, node_table)


def gathered(values, count, partner):
    mine = lax.all_to_all(values, "chip", 0, 0)
    return mine, lax.ppermute(mine, SLAB, partner)


def shards(
    count,
    flow_state,
    flow_speed,
    wall_cell,
    base_shift,
    normals,
    centres,
    tile_blocks,
    near_count,
    near_nodes,
):
    partner = [(i, i ^ 1) for i in range(count)]
    across = [(i, i + 1) for i in range(1, count - 1, 2)]
    across = across + [(j, i) for i, j in across]
    chips, rows = count // 2, flow_state.shape[1]
    send_a, send_b, state, speed = edge_rows(flow_state, flow_speed)
    from_a = lax.ppermute(send_a, SLAB, partner)
    from_b = lax.ppermute(send_b, SLAB, across)
    in_order, centre_table, nodes, node_table = ordered(base_shift, normals, centres, wall_cell, near_nodes)
    new_flow, low, high, base, chosen = inner_flux(state, speed, in_order)
    packed, low, high = right_side(chips, rows, send_a, send_b, from_a, from_b, low, high, base, chosen)
    mine, other = gathered(packed, count, partner)
    power, new_flow = powers(mine, other, low, high, new_flow, count)
    mine_power, other_power = gathered(power, count, partner)
    tiles, listed = tile_blocks.reshape(-1), tile_blocks.shape[1]
    sources, targets, first, last = near_points(tiles, listed, mine, other, nodes)
    coefficients, node_shift = near_body(
        tiles, listed, near_count, first, last, mine, other, mine_power, other_power, sources, targets,
        centre_table, node_table,
    )
    return new_flow, coefficients, node_shift


def solution(mesh):
    groups, count = mesh.shape["groups"], mesh.shape["slab"]
    split = Mesh(mesh.devices.reshape(groups, count // 2, 2), ("groups",) + SLAB)
    in_specs = (
        P("groups", SLAB, None),
        P("groups", SLAB, None),
        P(("groups",) + SLAB),
        P("groups", SLAB),
        P("groups", SLAB),
        P("groups", SLAB),
        P("groups", None),
        P("groups"),
        P("groups", SLAB),
    )
    out_specs = (P("groups", SLAB, None), P("groups", SLAB), P("groups", SLAB))
    return jax.shard_map(
        functools.partial(shards, count), mesh=split, in_specs=in_specs, out_specs=out_specs, check_vma=False
    )
```

```python
import functools

import jax
import jax.numpy as jnp
from jax import lax
from jax.experimental import pallas as pl
from jax.experimental.pallas import tpu as pltpu
from jax.sharding import Mesh
from jax.sharding import PartitionSpec as P

FLUX_STEP = 0.2
SUPPORT = 0.15
DIAG_SHIFT = 0.5
CENTRE_SHIFT = DIAG_SHIFT + 1.0
TINY = 1e-12
DEPTH = 0.4
CHUNK = 128
MARGIN = 1e-3
BIG_LIMIT = 48 * 1024 * 1024
SMALL_LIMIT = 16 * 1024 * 1024
FULL_LIMIT = 62 * 1024 * 1024 + 768 * 1024
F32 = jnp.float32
BF16 = jnp.bfloat16
SLAB = ("chip", "core")
VMEM = pl.BlockSpec(memory_space=pltpu.VMEM)
SMEM = pl.BlockSpec(memory_space=pltpu.SMEM)
HBM = pl.BlockSpec(memory_space=pltpu.HBM)


def parts(values):
    first = values.astype(BF16).astype(F32)
    rest = values - first
    second = rest.astype(BF16).astype(F32)
    return first, second, rest - second


def doubled(values):
    high = values.astype(BF16)
    return jnp.concatenate([high, (values - high.astype(F32)).astype(BF16)], axis=0)


def sides(points):
    count = points.shape[1]
    squares = jnp.sum(points * points, axis=0, keepdims=True)
    one = jnp.ones((1, count), F32)
    zero = jnp.zeros((3, count), F32)
    a, b, c = parts(jnp.concatenate([points, squares, one, zero], axis=0))
    d, e, f = parts(jnp.concatenate([-2.0 * points, one, squares, zero], axis=0))
    return jnp.concatenate([a, a, b, a, c, b], axis=0), jnp.concatenate([d, e, d, f, d, e], axis=0)


def quarter_kernel(sources, targets):
    squared = jnp.maximum(jnp.dot(sources, targets, preferred_element_type=F32), TINY)
    inside = jnp.maximum(1.0 - squared * lax.rsqrt(squared), 0.0)
    square_in = inside * inside
    return square_in * square_in * (1.25 - inside)


def local_points(raw, origin):
    x = (raw[0:2] - 0.5) * (1.0 / SUPPORT)
    return jnp.concatenate([x, (raw[2:3] - origin) * (1.0 / SUPPORT)], axis=0)


def rank_of(values):
    count = values.shape[1]
    column = jnp.broadcast_to(values, (8, count)).T[:, 0:1]
    result = []
    for tile in range(count // CHUNK):
        mine = values[:, tile * CHUNK : (tile + 1) * CHUNK]
        total = jnp.zeros((8, CHUNK), F32)
        for chunk in range(count // CHUNK):
            other = column[chunk * CHUNK : (chunk + 1) * CHUNK]
            if chunk < tile:
                before = other <= mine
            elif chunk > tile:
                before = other < mine
            else:
                above = lax.broadcasted_iota(jnp.int32, (CHUNK, CHUNK), 0) < lax.broadcasted_iota(
                    jnp.int32, (CHUNK, CHUNK), 1
                )
                before = jnp.logical_or(other < mine, jnp.logical_and(other == mine, above))
            ones = jnp.where(before, 1.0, 0.0)
            for group in range(CHUNK // 8):
                total = total + ones[group * 8 : group * 8 + 8]
        result.append(jnp.sum(total, axis=0, keepdims=True))
    return jnp.concatenate(result, axis=1)


def moved(values, table):
    rows = values.shape[0]
    stacked = jnp.concatenate(parts(values), axis=0).astype(BF16)
    both = lax.dot_general(
        stacked, table, (((1,), (1,)), ((), ())), preferred_element_type=F32
    )
    return (both[:rows] + both[rows : 2 * rows]) + both[2 * rows :]


def moved_back(values, table):
    both = jnp.dot(doubled(values), table, preferred_element_type=F32)
    return both[:3] + both[8:11]


def chunk_bounds(source_z, target_z, width, low_ref, high_ref):
    chunks = source_z.shape[1] // CHUNK
    tiles = target_z.shape[1] // width

    def edges(values, size, pieces):
        rows = jnp.concatenate([values[:, i * size : (i + 1) * size] for i in range(pieces)], axis=0)
        return jnp.min(rows, axis=1, keepdims=True), jnp.max(rows, axis=1, keepdims=True)

    source_low, source_high = edges(source_z, CHUNK, chunks)
    target_low, target_high = edges(target_z, width, tiles)
    index = lax.broadcasted_iota(jnp.int32, (chunks, 1), 0).astype(F32)
    for tile in range(tiles):
        near = jnp.logical_and(
            source_high >= target_low[tile : tile + 1] - (1.0 + MARGIN),
            source_low <= target_high[tile : tile + 1] + (1.0 + MARGIN),
        )
        low_ref[tile] = jnp.min(jnp.where(near, index, float(chunks))).astype(jnp.int32)
        high_ref[tile] = jnp.max(jnp.where(near, index + 1.0, 0.0)).astype(jnp.int32)


def order_kernel(base_ref, normal_ref, centre_ref, cell_ref, nodes_ref, out_ref, centre_table, nodes_out, node_table):
    def table_of(ref, rank):
        count = rank.shape[1]
        rows = 128
        for start in range(0, count, rows):
            row = lax.broadcasted_iota(jnp.int32, (rows, count), 0).astype(F32) + float(start)
            ref[start : start + rows] = jnp.where(row == rank, 1.0, 0.0).astype(BF16)

    count = centre_ref.shape[1]
    table_of(centre_table, rank_of(centre_ref[2:3]))
    values = jnp.concatenate(
        [
            base_ref[...],
            normal_ref[...],
            centre_ref[...],
            cell_ref[...].astype(F32),
            jnp.zeros((6, count), F32),
        ],
        axis=0,
    )
    out_ref[...] = moved(values, centre_table[...])
    table_of(node_table, rank_of(nodes_ref[2:3]))
    nodes = jnp.concatenate([nodes_ref[...], jnp.zeros((5, nodes_ref.shape[1]), F32)], axis=0)
    nodes_out[...] = moved(nodes, node_table[...])


def ordered(base_shift, normals, centres, wall_cell, near_nodes):
    count, slots = centres.shape[1], near_nodes.shape[1]
    return pl.pallas_call(
        order_kernel,
        out_shape=(
            jax.ShapeDtypeStruct((16, count), F32),
            jax.ShapeDtypeStruct((count, count), BF16),
            jax.ShapeDtypeStruct((8, slots), F32),
            jax.ShapeDtypeStruct((slots, slots), BF16),
        ),
        in_specs=[VMEM] * 5,
        out_specs=(VMEM,) * 4,
        compiler_params=pltpu.CompilerParams(vmem_limit_bytes=SMALL_LIMIT),
        cost_estimate=pl.CostEstimate(flops=8_000_000, bytes_accessed=4_000_000, transcendentals=0),
        name="order",
    )(base_shift, normals, centres, wall_cell.reshape(1, -1), near_nodes)


def edge_kernel(q_ref, w_ref, a_ref, b_ref, sems):
    count, rows, _ = q_ref.shape

    def move(row_a, row_b):
        copies = []
        for target, row in ((a_ref, row_a), (b_ref, row_b)):
            for index in range(count + 1):
                source = q_ref.at[index] if index < count else w_ref.at[0]
                copies.append(
                    pltpu.make_async_copy(
                        source.at[pl.ds(row, 1)], target.at[pl.ds(index, 1)], sems.at[len(copies)]
                    )
                )
        for copy in copies:
            copy.start()
        for copy in copies:
            copy.wait()

    core = lax.axis_index("core")

    @pl.when(core == 0)
    def _():
        move(rows - 1, 0)

    @pl.when(core != 0)
    def _():
        move(0, rows - 1)


def edge_rows(flow_state, flow_speed):
    count, _, plane = flow_state.shape
    rows = jax.ShapeDtypeStruct((count + 1, plane), F32)
    return pl.pallas_call(
        edge_kernel,
        out_shape=(rows, rows),
        in_specs=[HBM, HBM],
        out_specs=(VMEM, VMEM),
        scratch_shapes=[pltpu.SemaphoreType.DMA((2 * count + 2,))],
        compiler_params=pltpu.CompilerParams(vmem_limit_bytes=FULL_LIMIT),
        name="edge_rows",
    )(flow_state, flow_speed)


RATE = 0.5 * FLUX_STEP
PRESSURE = 4


def picked(stacked, chosen, lane):
    high, middle, low = parts(stacked)
    pieces = jnp.concatenate([high, middle, low], axis=1).astype(BF16)
    both = lax.dot_general(pieces, chosen, (((0,), (0,)), ((), ())), preferred_element_type=F32)
    value = (both[:128] + both[128:256]) + both[256:]
    here = lax.broadcasted_iota(jnp.int32, value.shape, 0) == lane
    return jnp.sum(jnp.where(here, value, 0.0), axis=0, keepdims=True)


def stacked_lanes(values):
    return jnp.concatenate([values[:, i : i + 128] for i in range(0, values.shape[1], 128)], axis=0)


def inner_kernel(q_ref, w_ref, sorted_ref, new_hbm, low_ref, high_ref, out_ref, chosen_ref, new_ref, sems):
    count, rows, plane = q_ref.shape
    width = 512
    steps = plane // width
    row = lax.broadcasted_iota(jnp.int32, (rows, width), 0)

    def copy_of(step):
        lanes = pl.ds(pl.multiple_of(step * width, width), width)
        return pltpu.make_async_copy(new_ref.at[:, :, lanes], new_hbm.at[:, :, lanes], sems.at[step])

    def chunk(step, _):
        here = pl.multiple_of(step * width, 128)
        left = pl.multiple_of(lax.rem(here + plane - 128, plane), 128)
        right = pl.multiple_of(lax.rem(here + width, plane), 128)

        def cyclic(ref, index):
            values = ref[index, :, pl.ds(here, width)]
            wide = jnp.concatenate(
                [ref[index, :, pl.ds(left, 128)], values, ref[index, :, pl.ds(right, 128)]], axis=1
            )
            before = pltpu.roll(wide, 1, 1)[:, 128 : 128 + width]
            after = pltpu.roll(wide, width + 255, 1)[:, 128 : 128 + width]
            return values, before, after

        w = w_ref[0, :, pl.ds(here, width)]
        face_low = jnp.where(row == 0, 0.0, RATE * (pltpu.roll(w, 1, 0) + w))
        face_high = jnp.where(row == rows - 1, 0.0, RATE * (w + pltpu.roll(w, rows - 1, 0)))
        speed, speed_before, speed_after = cyclic(w_ref, 1)
        face_left = RATE * (speed_before + speed)
        face_right = RATE * (speed + speed_after)
        low_in = jnp.maximum(face_low, 0.0)
        high_out = jnp.minimum(face_high, 0.0)
        left_in = jnp.maximum(face_left, 0.0)
        right_out = jnp.minimum(face_right, 0.0)
        keep = 1.0 - (
            (jnp.maximum(face_high, 0.0) - jnp.minimum(face_low, 0.0))
            + (jnp.maximum(face_right, 0.0) - jnp.minimum(face_left, 0.0))
        )
        for index in range(count):
            values, before, after = cyclic(q_ref, index)
            new = (
                keep * values
                + low_in * pltpu.roll(values, 1, 0)
                - high_out * pltpu.roll(values, rows - 1, 0)
                + left_in * before
                - right_out * after
            )
            new_ref[index, :, pl.ds(here, width)] = new
            low_ref[index : index + 1, pl.ds(here, width)] = new[0:1]
            high_ref[index : index + 1, pl.ds(here, width)] = new[rows - 1 : rows]
        copy_of(step).start()
        return 0

    lax.fori_loop(0, steps, chunk, 0)

    cells = sorted_ref[9:10].astype(jnp.int32)
    cell_row = cells // plane
    column = cells - cell_row * plane
    group = column // 128
    lane = column - group * 128
    place = group * rows + cell_row
    centres = cells.shape[1]
    lanes = plane // 128
    chosen = (lax.broadcasted_iota(jnp.int32, (rows * lanes, centres), 0) == place).astype(F32).astype(BF16)
    chosen_ref[...] = chosen
    load = picked(stacked_lanes(new_ref[PRESSURE]), chosen, lane)
    out_ref[...] = jnp.concatenate(
        [
            sorted_ref[0:3] + sorted_ref[3:6] * load,
            sorted_ref[3:9],
            lane.astype(F32),
            jnp.zeros((6, centres), F32),
        ],
        axis=0,
    )
    for step in range(steps):
        copy_of(step).wait()


def inner_flux(flow_state, flow_speed, in_order):
    count, rows, plane = flow_state.shape
    centres = in_order.shape[1]
    edge = jax.ShapeDtypeStruct((count, plane), F32)
    return pl.pallas_call(
        inner_kernel,
        out_shape=(
            jax.ShapeDtypeStruct(flow_state.shape, F32),
            edge,
            edge,
            jax.ShapeDtypeStruct((16, centres), F32),
            jax.ShapeDtypeStruct((rows * plane // 128, centres), BF16),
        ),
        in_specs=[VMEM] * 3,
        out_specs=(HBM, VMEM, VMEM, VMEM, VMEM),
        scratch_shapes=[pltpu.VMEM(flow_state.shape, F32), pltpu.SemaphoreType.DMA((plane // 512,))],
        compiler_params=pltpu.CompilerParams(vmem_limit_bytes=SMALL_LIMIT),
        cost_estimate=pl.CostEstimate(flops=20_000_000, bytes_accessed=4_000_000, transcendentals=0),
        name="inner_flux",
    )(flow_state, flow_speed, in_order)


def outer_kernel(
    send_a, send_b, from_a, from_b, low_ref, high_ref, base_ref, chosen_ref, out_ref, new_low, new_high, both_ref
):
    count, plane = low_ref.shape
    rows = both_ref.shape[0]
    even = lax.axis_index("core") == 0
    own_low = jnp.where(even, send_b[...], send_a[...])
    own_high = jnp.where(even, send_a[...], send_b[...])
    below = jnp.where(even, from_b[...], from_a[...])
    above = jnp.where(even, from_a[...], from_b[...])

    def flux(first, second):
        face = RATE * (first[count : count + 1] + second[count : count + 1])
        return jnp.maximum(face, 0.0) * first[:count] + jnp.minimum(face, 0.0) * second[:count]

    low = flux(below, own_low)
    high = flux(own_high, above)
    new_low[...] = low_ref[...] + low
    new_high[...] = high_ref[...] - high
    row = lax.broadcasted_iota(jnp.int32, (rows, plane), 0)
    zero = jnp.zeros((rows, plane), F32)
    added = jnp.where(row == 0, low[PRESSURE : PRESSURE + 1], zero)
    added = added - jnp.where(row == rows - 1, high[PRESSURE : PRESSURE + 1], zero)
    both_ref[...] = added
    base = base_ref[...]
    load = picked(stacked_lanes(both_ref[...]), chosen_ref[...], base[9:10].astype(jnp.int32))
    centres = base.shape[1]
    packed = jnp.concatenate([base[0:3] + base[3:6] * load, base[6:9], jnp.zeros((2, centres), F32)], axis=0)
    for chip in range(out_ref.shape[0]):
        out_ref[chip] = packed


def right_side(chips, rows, send_a, send_b, from_a, from_b, low, high, base, chosen):
    edge = jax.ShapeDtypeStruct(low.shape, F32)
    return pl.pallas_call(
        outer_kernel,
        out_shape=(jax.ShapeDtypeStruct((chips, 8, base.shape[1]), F32), edge, edge),
        in_specs=[VMEM] * 8,
        out_specs=(VMEM,) * 3,
        scratch_shapes=[pltpu.VMEM((rows, low.shape[1]), F32)],
        compiler_params=pltpu.CompilerParams(vmem_limit_bytes=SMALL_LIMIT),
        name="outer_flux",
    )(send_a, send_b, from_a, from_b, low, high, base, chosen)


def block_of(mine_ref, other_ref, block, core):
    chip = lax.div(block, 2)
    own = lax.rem(block, 2) == core
    return jnp.where(own, mine_ref[chip], other_ref[chip])


def powers_kernel(
    count, mine_ref, other_ref, new_low, new_high, new_in, out_ref, new_out,
    source_side, target_side, vector, image, tables, low_ref, high_ref, sems,
):
    del new_in
    rows_per_block = new_out.shape[1]
    copies = [
        pltpu.make_async_copy(new_low, new_out.at[:, 0], sems.at[0]),
        pltpu.make_async_copy(new_high, new_out.at[:, rows_per_block - 1], sems.at[1]),
    ]
    for copy in copies:
        copy.start()
    size = mine_ref.shape[2]
    chip, core = lax.axis_index("chip"), lax.axis_index("core")
    me = chip * 2 + core
    slots, width, reach = 6, 256, 6
    span = reach * CHUNK
    total = slots * size
    origin = lax.div(me * 2, 5).astype(F32)
    value_row = lax.broadcasted_iota(jnp.int32, (8, size), 0) < 3

    live, zeroth, third = [], [], []
    for slot in range(slots):
        block = me + slot - 2
        valid = jnp.logical_and(block >= 0, block < count)
        live.append(valid)
        data = block_of(mine_ref, other_ref, jnp.clip(block, 0, count - 1), core)
        zeroth.append(jnp.where(jnp.logical_and(value_row, valid), data, 0.0))
        middle = (block.astype(F32) + 0.5) * DEPTH
        raw = jnp.concatenate([data[3:5], jnp.where(valid, data[5:6], middle)], axis=0)
        points = local_points(raw, origin)
        third.append(points[2:3])
        source, target = sides(points)
        source_side[slot * size : (slot + 1) * size] = source.T.astype(BF16)
        target_side[:, slot * size : (slot + 1) * size] = target.astype(BF16)
    far = (lax.broadcasted_iota(jnp.int32, (span, 48), 1) == 3).astype(F32) * 4096.0
    source_side[total:] = far.astype(BF16)
    vector[:, total:] = jnp.zeros((16, span), BF16)
    heights = jnp.concatenate(third, axis=1)
    chunk_bounds(heights, heights[:, size : 5 * size], width, low_ref, high_ref)
    tiles = 4 * size // width

    def steps_of(tile):
        return lax.div(high_ref[tile] - low_ref[tile] + (reach - 1), reach)

    most = steps_of(0)
    for tile in range(1, tiles):
        most = jnp.maximum(most, steps_of(tile))
    same = lax.broadcasted_iota(jnp.int32, (CHUNK, CHUNK), 0) == lax.broadcasted_iota(
        jnp.int32, (CHUNK, CHUNK), 1
    )

    def build(tile, step):
        lanes = pl.ds(pl.multiple_of(tile * width + size, width), width)
        chunk = low_ref[tile] + step * reach
        rows = pl.ds(pl.multiple_of(chunk * CHUNK, CHUNK), span)
        table = quarter_kernel(source_side[rows], target_side[:, lanes])
        high = table.astype(BF16)
        tables[tile, step, :span] = high
        tables[tile, step, span:] = (table - high.astype(F32)).astype(BF16)
        for piece in range(width // CHUNK):
            place = (tile * width + size) // CHUNK + piece - chunk
            inside = jnp.logical_and(place >= 0, place < reach)
            place = jnp.clip(place, 0, reach - 1)
            for half in range(2):
                at = pl.ds(pl.multiple_of(place * CHUNK + half * span, CHUNK), CHUNK)
                columns = slice(piece * CHUNK, (piece + 1) * CHUNK)
                old = tables[tile, step, at, columns]
                tables[tile, step, at, columns] = jnp.where(jnp.logical_and(same, inside), 0.0, old.astype(F32)).astype(BF16)

    def one(tile, step):
        lanes = pl.ds(pl.multiple_of((low_ref[tile] + step * reach) * CHUNK, CHUNK), span)
        window = vector[:, lanes]
        return jnp.dot(jnp.concatenate([window, window], axis=1), tables[tile, step], preferred_element_type=F32)

    def lanes_of(tile):
        return pl.ds(pl.multiple_of(tile * width, width), width)

    def further(first, last):
        @pl.when(most > 1)
        def _():
            def of_tile(tile, _):
                def add(step, _):
                    image[:, lanes_of(tile)] += one(tile, step)
                    return 0

                return lax.fori_loop(1, steps_of(tile), add, 0)

            lax.fori_loop(first, last, of_tile, 0)

    def image_of(slot):
        both = image[:, (slot - 1) * size : slot * size]
        return jnp.where(live[slot], 4.0 * (both[:8] + both[8:]), 0.0)

    def power(slots):
        first, last = (slots[0] - 1) * size // width, slots[-1] * size // width
        for tile in range(first, last):
            image[:, tile * width : (tile + 1) * width] = one(tile, 0)
        further(first, last)
        return {slot: image_of(slot) for slot in slots}

    def hold(values, slot):
        vector[:, slot * size : (slot + 1) * size] = doubled(values)

    for slot in range(slots):
        hold(zeroth[slot], slot)

    def two_tiles(step, _):
        before = jnp.maximum(2 * step - 2, 0)
        for piece in range(2):
            image[:, lanes_of(before + piece)] = one(before + piece, 0)
        for piece in range(2):
            build(2 * step + piece, 0)
        return 0

    lax.fori_loop(0, tiles // 2, two_tiles, 0)
    for tile in range(tiles - 2, tiles):
        image[:, tile * width : (tile + 1) * width] = one(tile, 0)

    @pl.when(most > 1)
    def _():
        def of_tile(tile, _):
            def more(step, _):
                build(tile, step)
                return 0

            return lax.fori_loop(1, steps_of(tile), more, 0)

        lax.fori_loop(0, tiles, of_tile, 0)

    further(0, tiles)
    first = {slot: image_of(slot) for slot in range(1, 5)}
    for slot in range(1, 5):
        hold(first[slot], slot)
    second = power([2, 3])
    hold(jnp.zeros((8, size), F32), 1)
    hold(second[2], 2)
    hold(2.0 * second[3], 3)
    last = power([2])[2]

    def inner(left, right):
        return jnp.sum(left * right, axis=1, keepdims=True)

    moments = [
        inner(zeroth[2], zeroth[2]),
        inner(zeroth[2], first[2]),
        inner(first[2], first[2]),
        inner(first[2], second[2]),
        inner(second[2], second[2]),
        inner(second[2], last),
    ]
    lane = lax.broadcasted_iota(jnp.int32, (8, 128), 1)
    packed = jnp.zeros((8, 128), F32)
    for index, moment in enumerate(moments):
        packed = jnp.where(lane == index, moment, packed)
    values = jnp.concatenate([first[2][:3], second[2][:3], jnp.zeros((2, size), F32)], axis=0)
    for index in range(out_ref.shape[0]):
        out_ref[index, :, :size] = values
        out_ref[index, :, size:] = packed
    for copy in copies:
        copy.wait()


def powers(mine, other, new_low, new_high, new_flow, count):
    chips, _, size = mine.shape
    tiles = 4 * size // 256
    steps = (6 * size // CHUNK + 5) // 6
    return pl.pallas_call(
        functools.partial(powers_kernel, count),
        out_shape=(
            jax.ShapeDtypeStruct((chips, 8, size + 128), F32),
            jax.ShapeDtypeStruct(new_flow.shape, F32),
        ),
        in_specs=[VMEM] * 4 + [HBM],
        out_specs=(VMEM, HBM),
        scratch_shapes=[
            pltpu.VMEM((6 * size + 6 * CHUNK, 48), BF16),
            pltpu.VMEM((48, 6 * size), BF16),
            pltpu.VMEM((16, 6 * size + 6 * CHUNK), BF16),
            pltpu.VMEM((16, 4 * size), F32),
            pltpu.VMEM((tiles, steps, 12 * CHUNK, 256), BF16),
            pltpu.SMEM((tiles,), jnp.int32),
            pltpu.SMEM((tiles,), jnp.int32),
            pltpu.SemaphoreType.DMA((2,)),
        ],
        input_output_aliases={4: 1},
        compiler_params=pltpu.CompilerParams(vmem_limit_bytes=BIG_LIMIT),
        name="powers",
    )(mine, other, new_low, new_high, new_flow)


def ratio(top, bottom):
    safe = bottom > 0.0
    return jnp.where(safe, top / jnp.where(safe, bottom, 1.0), 0.0)


def weights_of(moments):
    def inner(left, right):
        total = None
        for i, a in enumerate(left):
            for j, c in enumerate(right):
                term = a * c * moments[i + j]
                total = term if total is None else total + term
        return total

    one = jnp.ones_like(moments[0])
    residual, search = [one], [one]
    coefficients = [0.0 * one] * 3
    energy = moments[0]
    for step in range(3):
        image = [CENTRE_SHIFT * value for value in search] + [0.0 * one]
        for index, value in enumerate(search):
            image[index + 1] = image[index + 1] + value
        length = ratio(energy, inner(search, image))
        for index, value in enumerate(search):
            coefficients[index] = coefficients[index] + length * value
        if step == 2:
            break
        longer = residual + [0.0 * one]
        residual = [value - length * other for value, other in zip(longer, image)]
        fresh = jnp.maximum(inner(residual, residual), 0.0)
        scale = ratio(fresh, energy)
        search = [
            value + scale * (search[index] if index < len(search) else 0.0)
            for index, value in enumerate(residual)
        ]
        energy = fresh
    return coefficients


REACH = 7


def bounds_of(source_z, target_z):
    chunks = source_z.shape[1] // CHUNK
    tiles = target_z.shape[1] // CHUNK

    def edges(values, pieces):
        rows = jnp.concatenate([values[:, i * CHUNK : (i + 1) * CHUNK] for i in range(pieces)], axis=0)
        return jnp.min(rows, axis=1, keepdims=True), jnp.max(rows, axis=1, keepdims=True)

    def across(values):
        return jnp.broadcast_to(values, (tiles, 128)).T[0:1]

    source_low, source_high = edges(source_z, chunks)
    target_low, target_high = edges(target_z, tiles)
    near = jnp.logical_and(
        source_high >= across(target_low) - (1.0 + MARGIN), source_low <= across(target_high) + (1.0 + MARGIN)
    )
    index = lax.broadcasted_iota(jnp.int32, (chunks, tiles), 0).astype(F32)
    low = jnp.min(jnp.where(near, index, float(chunks)), axis=0, keepdims=True)
    high = jnp.max(jnp.where(near, index + 1.0, 0.0), axis=0, keepdims=True)
    return jnp.concatenate([low, high], axis=0)


def first_listed(tile_ref, me):
    return tile_ref[pl.ds(me, 1), :][0, 0]


def points_kernel(tile_ref, mine_ref, other_ref, nodes_ref, source_ref, target_ref, bound_ref):
    size = mine_ref.shape[2]
    core = lax.axis_index("core")
    me = lax.axis_index("chip") * 2 + core
    listed = tile_ref.shape[1]
    start = first_listed(tile_ref, me)
    origin = lax.div((start + 2) * 2, 5).astype(F32)
    third = []
    for index in range(listed):
        data = block_of(mine_ref, other_ref, start + index, core)
        points = local_points(data[3:6], origin)
        third.append(points[2:3])
        source, _ = sides(points)
        source_ref[index * size : (index + 1) * size] = source.T.astype(BF16)
    span = REACH * CHUNK
    far = (lax.broadcasted_iota(jnp.int32, (span, 48), 1) == 3).astype(F32) * 4096.0
    source_ref[listed * size :] = far.astype(BF16)
    points = local_points(nodes_ref[0:3], origin)
    _, target = sides(points)
    target_ref[...] = target.astype(BF16)
    bound_ref[...] = bounds_of(jnp.concatenate(third, axis=1), points[2:3])


def near_points(tile_blocks, mine, other, nodes):
    size = mine.shape[2]
    slots = nodes.shape[1]
    listed = tile_blocks.shape[1]
    return pl.pallas_call(
        points_kernel,
        out_shape=(
            jax.ShapeDtypeStruct((listed * size + REACH * CHUNK, 48), BF16),
            jax.ShapeDtypeStruct((48, slots), BF16),
            jax.ShapeDtypeStruct((2, slots // CHUNK), F32),
        ),
        in_specs=[VMEM] * 4,
        out_specs=(VMEM,) * 3,
        compiler_params=pltpu.CompilerParams(vmem_limit_bytes=SMALL_LIMIT),
        cost_estimate=pl.CostEstimate(flops=1_000_000, bytes_accessed=1_000_000, transcendentals=0),
        name="near_points",
    )(tile_blocks, mine, other, nodes)


def near_kernel(
    tile_ref, count_ref, bound_ref, mine_ref, other_ref, mine_power, other_power, source_side, target_side,
    centre_table, node_table, coef_ref, shift_ref, vector, result, low_ref, step_ref,
):
    size = mine_ref.shape[2]
    slots = target_side.shape[1]
    chips = mine_ref.shape[0]
    core = lax.axis_index("core")
    me = lax.axis_index("chip") * 2 + core
    listed = tile_ref.shape[1]
    start_block = first_listed(tile_ref, me)
    width = CHUNK
    tiles = slots // width
    span = REACH * CHUNK
    total = listed * size

    bounds = bound_ref[...].astype(jnp.int32)
    most = 0
    for tile in range(tiles):
        low = bounds[0, tile]
        steps = lax.div(bounds[1, tile] - low + (REACH - 1), REACH)
        low_ref[tile] = low
        step_ref[tile] = steps
        most = jnp.maximum(most, steps)

    summed = mine_power[0, :, size:] + other_power[0, :, size:]
    for index in range(1, chips):
        summed = summed + (mine_power[index, :, size:] + other_power[index, :, size:])
    weights = weights_of([summed[:, index : index + 1] for index in range(6)])

    def coefficients_of(block):
        data = block_of(mine_ref, other_ref, block, core)
        power = block_of(mine_power, other_power, block, core)[:, :size]
        values = weights[0] * data + weights[1] * power + weights[2] * pltpu.roll(power, 5, 0)
        keep = lax.broadcasted_iota(jnp.int32, (8, size), 0) < 3
        return jnp.where(keep, values, 0.0)

    for index in range(listed):
        vector[:, index * size : (index + 1) * size] = doubled(coefficients_of(start_block + index))
    vector[:, total:] = jnp.zeros((16, span), BF16)
    coef_ref[...] = moved_back(coefficients_of(me), centre_table[...])

    def lanes_of(tile):
        return pl.ds(pl.multiple_of(tile * width, width), width)

    def one(tile, step):
        start = pl.multiple_of((low_ref[tile] + step * REACH) * CHUNK, CHUNK)
        table = quarter_kernel(source_side[pl.ds(start, span)], target_side[:, lanes_of(tile)])
        window = vector[:, pl.ds(start, span)]
        return jnp.dot(jnp.concatenate([window, window], axis=1), doubled(table), preferred_element_type=F32)

    def two_tiles(step, _):
        for piece in range(2):
            result[:, lanes_of(2 * step + piece)] = one(2 * step + piece, 0)
        return 0

    lax.fori_loop(0, tiles // 2, two_tiles, 0)

    @pl.when(most > 1)
    def _():
        def of_tile(tile, _):
            def add(step, _):
                result[:, lanes_of(tile)] += one(tile, step)
                return 0

            return lax.fori_loop(1, step_ref[tile], add, 0)

        lax.fori_loop(0, tiles, of_tile, 0)

    lane = lax.broadcasted_iota(jnp.int32, count_ref.shape, 1)
    live = jnp.sum(jnp.where(lane == me, count_ref[...], 0).astype(F32), axis=1, keepdims=True)
    slot = lax.broadcasted_iota(jnp.int32, (3, slots), 1).astype(F32)
    both = result[...]
    shift = moved_back(4.0 * (both[:8] + both[8:]), node_table[...])
    shift_ref[...] = jnp.where(slot < live, shift, 0.0)


def near_body(tile_blocks, near_count, bounds, mine, other, mine_power, other_power, sources, targets, centre_table, node_table):
    size = mine.shape[2]
    slots = targets.shape[1]
    total = tile_blocks.shape[1] * size
    return pl.pallas_call(
        near_kernel,
        out_shape=(
            jax.ShapeDtypeStruct((3, size), F32),
            jax.ShapeDtypeStruct((3, slots), F32),
        ),
        in_specs=[VMEM] * 11,
        out_specs=(VMEM, VMEM),
        scratch_shapes=[
            pltpu.VMEM((16, total + REACH * CHUNK), BF16),
            pltpu.VMEM((16, slots), F32),
            pltpu.SMEM((slots // CHUNK,), jnp.int32),
            pltpu.SMEM((slots // CHUNK,), jnp.int32),
        ],
        compiler_params=pltpu.CompilerParams(vmem_limit_bytes=SMALL_LIMIT),
        name="near_body",
    )(
        tile_blocks, near_count.reshape(1, -1), bounds, mine, other, mine_power, other_power, sources, targets,
        centre_table, node_table,
    )


def gathered(values, count, partner):
    mine = lax.all_to_all(values, "chip", 0, 0)
    return mine, lax.ppermute(mine, SLAB, partner)


def shards(
    count,
    flow_state,
    flow_speed,
    wall_cell,
    base_shift,
    normals,
    centres,
    tile_blocks,
    near_count,
    near_nodes,
):
    partner = [(i, i ^ 1) for i in range(count)]
    across = [(i, i + 1) for i in range(1, count - 1, 2)]
    across = across + [(j, i) for i, j in across]
    chips, rows = count // 2, flow_state.shape[1]
    send_a, send_b = edge_rows(flow_state, flow_speed)
    from_b = lax.ppermute(send_b, SLAB, across)
    from_a = lax.ppermute(send_a, SLAB, partner)
    in_order, centre_table, nodes, node_table = ordered(base_shift, normals, centres, wall_cell, near_nodes)
    new_flow, low, high, base, chosen = inner_flux(flow_state, flow_speed, in_order)
    packed, low, high = right_side(chips, rows, send_a, send_b, from_a, from_b, low, high, base, chosen)
    mine, other = gathered(packed, count, partner)
    power, new_flow = powers(mine, other, low, high, new_flow, count)
    mine_power, other_power = gathered(power, count, partner)
    sources, targets, bounds = near_points(tile_blocks, mine, other, nodes)
    coefficients, node_shift = near_body(
        tile_blocks, near_count, bounds, mine, other, mine_power, other_power, sources, targets,
        centre_table, node_table,
    )
    return new_flow, coefficients, node_shift


def solution(mesh):
    groups, count = mesh.shape["groups"], mesh.shape["slab"]
    split = Mesh(mesh.devices.reshape(groups, count // 2, 2), ("groups",) + SLAB)
    in_specs = (
        P("groups", SLAB, None),
        P("groups", SLAB, None),
        P(("groups",) + SLAB),
        P("groups", SLAB),
        P("groups", SLAB),
        P("groups", SLAB),
        P("groups", None),
        P("groups"),
        P("groups", SLAB),
    )
    out_specs = (P("groups", SLAB, None), P("groups", SLAB), P("groups", SLAB))
    return jax.shard_map(
        functools.partial(shards, count), mesh=split, in_specs=in_specs, out_specs=out_specs, check_vma=False
    )
```

```python
import functools

import jax
import jax.numpy as jnp
from jax import lax
from jax.experimental import pallas as pl
from jax.experimental.pallas import tpu as pltpu
from jax.sharding import Mesh
from jax.sharding import PartitionSpec as P


FLUX_STEP = 0.2
SUPPORT = 0.15
DIAG_SHIFT = 0.5
CENTRE_SHIFT = DIAG_SHIFT + 1.0
TINY = 1e-12
DEPTH = 0.4
CHUNK = 128
MARGIN = 1e-3
ORDER_FLOPS = 2_000_000_000
BIG_LIMIT = 48 * 1024 * 1024
SMALL_LIMIT = 16 * 1024 * 1024
FULL_LIMIT = 62 * 1024 * 1024 + 768 * 1024
F32 = jnp.float32
BF16 = jnp.bfloat16
SLAB = ("chip", "core")
VMEM = pl.BlockSpec(memory_space=pltpu.VMEM)
SMEM = pl.BlockSpec(memory_space=pltpu.SMEM)
HBM = pl.BlockSpec(memory_space=pltpu.HBM)


def parts(values):
    first = values.astype(BF16).astype(F32)
    rest = values - first
    second = rest.astype(BF16).astype(F32)
    return first, second, rest - second


def doubled(values):
    high = values.astype(BF16)
    return jnp.concatenate([high, (values - high.astype(F32)).astype(BF16)], axis=0)


def sides(points):
    count = points.shape[1]
    squares = jnp.sum(points * points, axis=0, keepdims=True)
    one = jnp.ones((1, count), F32)
    zero = jnp.zeros((3, count), F32)
    a, b, c = parts(jnp.concatenate([points, squares, one, zero], axis=0))
    d, e, f = parts(jnp.concatenate([-2.0 * points, one, squares, zero], axis=0))
    return jnp.concatenate([a, a, b, a, c, b], axis=0), jnp.concatenate([d, e, d, f, d, e], axis=0)


def quarter_kernel(sources, targets):
    squared = jnp.maximum(jnp.dot(sources, targets, preferred_element_type=F32), TINY)
    inside = jnp.maximum(1.0 - squared * lax.rsqrt(squared), 0.0)
    square_in = inside * inside
    return square_in * square_in * (1.25 - inside)


def local_points(raw, origin):
    x = (raw[0:2] - 0.5) * (1.0 / SUPPORT)
    return jnp.concatenate([x, (raw[2:3] - origin) * (1.0 / SUPPORT)], axis=0)


def rank_of(values):
    count = values.shape[1]
    column = jnp.broadcast_to(values, (8, count)).T[:, 0:1]
    result = []
    for tile in range(count // CHUNK):
        mine = values[:, tile * CHUNK : (tile + 1) * CHUNK]
        total = jnp.zeros((8, CHUNK), F32)
        for chunk in range(count // CHUNK):
            other = column[chunk * CHUNK : (chunk + 1) * CHUNK]
            if chunk < tile:
                before = other <= mine
            elif chunk > tile:
                before = other < mine
            else:
                above = lax.broadcasted_iota(jnp.int32, (CHUNK, CHUNK), 0) < lax.broadcasted_iota(
                    jnp.int32, (CHUNK, CHUNK), 1
                )
                before = jnp.logical_or(other < mine, jnp.logical_and(other == mine, above))
            ones = jnp.where(before, 1.0, 0.0)
            for group in range(CHUNK // 8):
                total = total + ones[group * 8 : group * 8 + 8]
        result.append(jnp.sum(total, axis=0, keepdims=True))
    return jnp.concatenate(result, axis=1)


def moved(values, table):
    rows = values.shape[0]
    stacked = jnp.concatenate(parts(values), axis=0).astype(BF16)
    both = lax.dot_general(
        stacked, table, (((1,), (1,)), ((), ())), preferred_element_type=F32
    )
    return (both[:rows] + both[rows : 2 * rows]) + both[2 * rows :]


def moved_back(values, table):
    both = jnp.dot(doubled(values), table, preferred_element_type=F32)
    return both[:3] + both[8:11]


def chunk_bounds(source_z, target_z, width, low_ref, high_ref):
    chunks = source_z.shape[1] // CHUNK
    tiles = target_z.shape[1] // width

    def edges(values, size, pieces):
        rows = jnp.concatenate([values[:, i * size : (i + 1) * size] for i in range(pieces)], axis=0)
        return jnp.min(rows, axis=1, keepdims=True), jnp.max(rows, axis=1, keepdims=True)

    source_low, source_high = edges(source_z, CHUNK, chunks)
    target_low, target_high = edges(target_z, width, tiles)
    index = lax.broadcasted_iota(jnp.int32, (chunks, 1), 0).astype(F32)
    for tile in range(tiles):
        near = jnp.logical_and(
            source_high >= target_low[tile : tile + 1] - (1.0 + MARGIN),
            source_low <= target_high[tile : tile + 1] + (1.0 + MARGIN),
        )
        low_ref[tile] = jnp.min(jnp.where(near, index, float(chunks))).astype(jnp.int32)
        high_ref[tile] = jnp.max(jnp.where(near, index + 1.0, 0.0)).astype(jnp.int32)


def order_kernel(base_ref, normal_ref, centre_ref, cell_ref, nodes_ref, out_ref, centre_table, nodes_out, node_table):
    def table_of(ref, rank):
        count = rank.shape[1]
        rows = 128
        for start in range(0, count, rows):
            row = lax.broadcasted_iota(jnp.int32, (rows, count), 0).astype(F32) + float(start)
            ref[start : start + rows] = jnp.where(row == rank, 1.0, 0.0).astype(BF16)

    count = centre_ref.shape[1]
    table_of(centre_table, rank_of(centre_ref[2:3]))
    values = jnp.concatenate(
        [
            base_ref[...],
            normal_ref[...],
            centre_ref[...],
            cell_ref[...].astype(F32),
            jnp.zeros((6, count), F32),
        ],
        axis=0,
    )
    out_ref[...] = moved(values, centre_table[...])
    table_of(node_table, rank_of(nodes_ref[2:3]))
    nodes = jnp.concatenate([nodes_ref[...], jnp.zeros((5, nodes_ref.shape[1]), F32)], axis=0)
    nodes_out[...] = moved(nodes, node_table[...])


def ordered(base_shift, normals, centres, wall_cell, near_nodes):
    count, slots = centres.shape[1], near_nodes.shape[1]
    return pl.pallas_call(
        order_kernel,
        out_shape=(
            jax.ShapeDtypeStruct((16, count), F32),
            jax.ShapeDtypeStruct((count, count), BF16),
            jax.ShapeDtypeStruct((8, slots), F32),
            jax.ShapeDtypeStruct((slots, slots), BF16),
        ),
        in_specs=[VMEM] * 5,
        out_specs=(VMEM,) * 4,
        compiler_params=pltpu.CompilerParams(vmem_limit_bytes=SMALL_LIMIT),
        cost_estimate=pl.CostEstimate(flops=ORDER_FLOPS, bytes_accessed=4_000_000, transcendentals=0),
        name="order",
    )(base_shift, normals, centres, wall_cell.reshape(1, -1), near_nodes)


def edge_kernel(even_last, q_ref, w_ref, *rest):
    target, sems = rest[-2:]
    count, rows, _ = q_ref.shape

    def move(row):
        copies = []
        for index in range(count + 1):
            source = q_ref.at[index] if index < count else w_ref.at[0]
            copies.append(
                pltpu.make_async_copy(source.at[pl.ds(row, 1)], target.at[pl.ds(index, 1)], sems.at[index])
            )
        for copy in copies:
            copy.start()
        for copy in copies:
            copy.wait()

    core = lax.axis_index("core")

    @pl.when(core == 0)
    def _():
        move(rows - 1 if even_last else 0)

    @pl.when(core != 0)
    def _():
        move(0 if even_last else rows - 1)


def edge_rows(even_last, flow_state, flow_speed, *after):
    count, _, plane = flow_state.shape
    return pl.pallas_call(
        functools.partial(edge_kernel, even_last),
        out_shape=jax.ShapeDtypeStruct((count + 1, plane), F32),
        in_specs=[HBM, HBM] + [HBM] * len(after),
        out_specs=VMEM,
        scratch_shapes=[pltpu.SemaphoreType.DMA((count + 1,))],
        compiler_params=pltpu.CompilerParams(vmem_limit_bytes=FULL_LIMIT),
        name="edge_rows",
    )(flow_state, flow_speed, *after)


RATE = 0.5 * FLUX_STEP
PRESSURE = 4


def picked(stacked, chosen, lane):
    high, middle, low = parts(stacked)
    pieces = jnp.concatenate([high, middle, low], axis=1).astype(BF16)
    both = lax.dot_general(pieces, chosen, (((0,), (0,)), ((), ())), preferred_element_type=F32)
    value = (both[:128] + both[128:256]) + both[256:]
    here = lax.broadcasted_iota(jnp.int32, value.shape, 0) == lane
    return jnp.sum(jnp.where(here, value, 0.0), axis=0, keepdims=True)


def stacked_lanes(values):
    return jnp.concatenate([values[:, i : i + 128] for i in range(0, values.shape[1], 128)], axis=0)


def inner_kernel(q_ref, w_ref, sorted_ref, new_hbm, low_ref, high_ref, out_ref, chosen_ref, new_ref, sems):
    count, rows, plane = q_ref.shape
    width = 512
    steps = plane // width
    row = lax.broadcasted_iota(jnp.int32, (rows, width), 0)

    def copy_of(step):
        lanes = pl.ds(pl.multiple_of(step * width, width), width)
        return pltpu.make_async_copy(new_ref.at[:, :, lanes], new_hbm.at[:, :, lanes], sems.at[step])

    def chunk(step, _):
        here = pl.multiple_of(step * width, 128)
        left = pl.multiple_of(lax.rem(here + plane - 128, plane), 128)
        right = pl.multiple_of(lax.rem(here + width, plane), 128)

        def cyclic(ref, index):
            values = ref[index, :, pl.ds(here, width)]
            wide = jnp.concatenate(
                [ref[index, :, pl.ds(left, 128)], values, ref[index, :, pl.ds(right, 128)]], axis=1
            )
            before = pltpu.roll(wide, 1, 1)[:, 128 : 128 + width]
            after = pltpu.roll(wide, width + 255, 1)[:, 128 : 128 + width]
            return values, before, after

        w = w_ref[0, :, pl.ds(here, width)]
        face_low = jnp.where(row == 0, 0.0, RATE * (pltpu.roll(w, 1, 0) + w))
        face_high = jnp.where(row == rows - 1, 0.0, RATE * (w + pltpu.roll(w, rows - 1, 0)))
        speed, speed_before, speed_after = cyclic(w_ref, 1)
        face_left = RATE * (speed_before + speed)
        face_right = RATE * (speed + speed_after)
        low_in = jnp.maximum(face_low, 0.0)
        high_out = jnp.minimum(face_high, 0.0)
        left_in = jnp.maximum(face_left, 0.0)
        right_out = jnp.minimum(face_right, 0.0)
        keep = 1.0 - (
            (jnp.maximum(face_high, 0.0) - jnp.minimum(face_low, 0.0))
            + (jnp.maximum(face_right, 0.0) - jnp.minimum(face_left, 0.0))
        )
        for index in range(count):
            values, before, after = cyclic(q_ref, index)
            new = (
                keep * values
                + low_in * pltpu.roll(values, 1, 0)
                - high_out * pltpu.roll(values, rows - 1, 0)
                + left_in * before
                - right_out * after
            )
            new_ref[index, :, pl.ds(here, width)] = new
            low_ref[index : index + 1, pl.ds(here, width)] = new[0:1]
            high_ref[index : index + 1, pl.ds(here, width)] = new[rows - 1 : rows]
        copy_of(step).start()
        return 0

    lax.fori_loop(0, steps, chunk, 0)

    cells = sorted_ref[9:10].astype(jnp.int32)
    cell_row = cells // plane
    column = cells - cell_row * plane
    group = column // 128
    lane = column - group * 128
    place = group * rows + cell_row
    centres = cells.shape[1]
    lanes = plane // 128
    chosen = (lax.broadcasted_iota(jnp.int32, (rows * lanes, centres), 0) == place).astype(F32).astype(BF16)
    chosen_ref[...] = chosen
    load = picked(stacked_lanes(new_ref[PRESSURE]), chosen, lane)
    out_ref[...] = jnp.concatenate(
        [
            sorted_ref[0:3] + sorted_ref[3:6] * load,
            sorted_ref[3:9],
            lane.astype(F32),
            jnp.zeros((6, centres), F32),
        ],
        axis=0,
    )
    for step in range(steps):
        copy_of(step).wait()


def inner_flux(flow_state, flow_speed, in_order):
    count, rows, plane = flow_state.shape
    centres = in_order.shape[1]
    edge = jax.ShapeDtypeStruct((count, plane), F32)
    return pl.pallas_call(
        inner_kernel,
        out_shape=(
            jax.ShapeDtypeStruct(flow_state.shape, F32),
            edge,
            edge,
            jax.ShapeDtypeStruct((16, centres), F32),
            jax.ShapeDtypeStruct((rows * plane // 128, centres), BF16),
        ),
        in_specs=[VMEM] * 3,
        out_specs=(HBM, VMEM, VMEM, VMEM, VMEM),
        scratch_shapes=[pltpu.VMEM(flow_state.shape, F32), pltpu.SemaphoreType.DMA((plane // 512,))],
        compiler_params=pltpu.CompilerParams(vmem_limit_bytes=SMALL_LIMIT),
        cost_estimate=pl.CostEstimate(flops=20_000_000, bytes_accessed=4_000_000, transcendentals=0),
        name="inner_flux",
    )(flow_state, flow_speed, in_order)


def outer_kernel(
    send_a, send_b, from_a, from_b, low_ref, high_ref, base_ref, chosen_ref, out_ref, new_low, new_high, both_ref
):
    count, plane = low_ref.shape
    rows = both_ref.shape[0]
    even = lax.axis_index("core") == 0
    own_low = jnp.where(even, send_b[...], send_a[...])
    own_high = jnp.where(even, send_a[...], send_b[...])
    below = jnp.where(even, from_b[...], from_a[...])
    above = jnp.where(even, from_a[...], from_b[...])

    def flux(first, second):
        face = RATE * (first[count : count + 1] + second[count : count + 1])
        return jnp.maximum(face, 0.0) * first[:count] + jnp.minimum(face, 0.0) * second[:count]

    low = flux(below, own_low)
    high = flux(own_high, above)
    new_low[...] = low_ref[...] + low
    new_high[...] = high_ref[...] - high
    row = lax.broadcasted_iota(jnp.int32, (rows, plane), 0)
    zero = jnp.zeros((rows, plane), F32)
    added = jnp.where(row == 0, low[PRESSURE : PRESSURE + 1], zero)
    added = added - jnp.where(row == rows - 1, high[PRESSURE : PRESSURE + 1], zero)
    both_ref[...] = added
    base = base_ref[...]
    load = picked(stacked_lanes(both_ref[...]), chosen_ref[...], base[9:10].astype(jnp.int32))
    centres = base.shape[1]
    packed = jnp.concatenate([base[0:3] + base[3:6] * load, base[6:9], jnp.zeros((2, centres), F32)], axis=0)
    for chip in range(out_ref.shape[0]):
        out_ref[chip] = packed


def right_side(chips, rows, send_a, send_b, from_a, from_b, low, high, base, chosen):
    edge = jax.ShapeDtypeStruct(low.shape, F32)
    return pl.pallas_call(
        outer_kernel,
        out_shape=(jax.ShapeDtypeStruct((chips, 8, base.shape[1]), F32), edge, edge),
        in_specs=[VMEM] * 8,
        out_specs=(VMEM,) * 3,
        scratch_shapes=[pltpu.VMEM((rows, low.shape[1]), F32)],
        compiler_params=pltpu.CompilerParams(vmem_limit_bytes=SMALL_LIMIT),
        name="outer_flux",
    )(send_a, send_b, from_a, from_b, low, high, base, chosen)


def block_of(mine_ref, other_ref, block, core):
    chip = lax.div(block, 2)
    own = lax.rem(block, 2) == core
    return jnp.where(own, mine_ref[chip], other_ref[chip])


def powers_kernel(
    count, mine_ref, other_ref, new_low, new_high, new_in, out_ref, new_out,
    source_side, target_side, vector, image, tables, low_ref, high_ref, sems,
):
    del new_in
    rows_per_block = new_out.shape[1]
    copies = [
        pltpu.make_async_copy(new_low, new_out.at[:, 0], sems.at[0]),
        pltpu.make_async_copy(new_high, new_out.at[:, rows_per_block - 1], sems.at[1]),
    ]
    for copy in copies:
        copy.start()
    size = mine_ref.shape[2]
    chip, core = lax.axis_index("chip"), lax.axis_index("core")
    me = chip * 2 + core
    slots, width, reach = 6, 256, 6
    span = reach * CHUNK
    total = slots * size
    origin = lax.div(me * 2, 5).astype(F32)
    value_row = lax.broadcasted_iota(jnp.int32, (8, size), 0) < 3

    live, zeroth, third = [], [], []
    for slot in range(slots):
        block = me + slot - 2
        valid = jnp.logical_and(block >= 0, block < count)
        live.append(valid)
        data = block_of(mine_ref, other_ref, jnp.clip(block, 0, count - 1), core)
        zeroth.append(jnp.where(jnp.logical_and(value_row, valid), data, 0.0))
        middle = (block.astype(F32) + 0.5) * DEPTH
        raw = jnp.concatenate([data[3:5], jnp.where(valid, data[5:6], middle)], axis=0)
        points = local_points(raw, origin)
        third.append(points[2:3])
        source, target = sides(points)
        source_side[slot * size : (slot + 1) * size] = source.T.astype(BF16)
        target_side[:, slot * size : (slot + 1) * size] = target.astype(BF16)
    far = (lax.broadcasted_iota(jnp.int32, (span, 48), 1) == 3).astype(F32) * 4096.0
    source_side[total:] = far.astype(BF16)
    vector[:, total:] = jnp.zeros((16, span), BF16)
    heights = jnp.concatenate(third, axis=1)
    chunk_bounds(heights, heights[:, size : 5 * size], width, low_ref, high_ref)
    tiles = 4 * size // width

    def steps_of(tile):
        return lax.div(high_ref[tile] - low_ref[tile] + (reach - 1), reach)

    most = steps_of(0)
    for tile in range(1, tiles):
        most = jnp.maximum(most, steps_of(tile))
    same = lax.broadcasted_iota(jnp.int32, (CHUNK, CHUNK), 0) == lax.broadcasted_iota(
        jnp.int32, (CHUNK, CHUNK), 1
    )

    def build(tile, step):
        lanes = pl.ds(pl.multiple_of(tile * width + size, width), width)
        chunk = low_ref[tile] + step * reach
        rows = pl.ds(pl.multiple_of(chunk * CHUNK, CHUNK), span)
        table = quarter_kernel(source_side[rows], target_side[:, lanes])
        high = table.astype(BF16)
        tables[tile, step, :span] = high
        tables[tile, step, span:] = (table - high.astype(F32)).astype(BF16)
        for piece in range(width // CHUNK):
            place = (tile * width + size) // CHUNK + piece - chunk
            inside = jnp.logical_and(place >= 0, place < reach)
            place = jnp.clip(place, 0, reach - 1)
            for half in range(2):
                at = pl.ds(pl.multiple_of(place * CHUNK + half * span, CHUNK), CHUNK)
                columns = slice(piece * CHUNK, (piece + 1) * CHUNK)
                old = tables[tile, step, at, columns]
                tables[tile, step, at, columns] = jnp.where(jnp.logical_and(same, inside), 0.0, old.astype(F32)).astype(BF16)

    def one(tile, step):
        lanes = pl.ds(pl.multiple_of((low_ref[tile] + step * reach) * CHUNK, CHUNK), span)
        window = vector[:, lanes]
        return jnp.dot(jnp.concatenate([window, window], axis=1), tables[tile, step], preferred_element_type=F32)

    def lanes_of(tile):
        return pl.ds(pl.multiple_of(tile * width, width), width)

    def further(first, last):
        @pl.when(most > 1)
        def _():
            def of_tile(tile, _):
                def add(step, _):
                    image[:, lanes_of(tile)] += one(tile, step)
                    return 0

                return lax.fori_loop(1, steps_of(tile), add, 0)

            lax.fori_loop(first, last, of_tile, 0)

    def image_of(slot):
        both = image[:, (slot - 1) * size : slot * size]
        return jnp.where(live[slot], 4.0 * (both[:8] + both[8:]), 0.0)

    def power(slots):
        first, last = (slots[0] - 1) * size // width, slots[-1] * size // width
        for tile in range(first, last):
            image[:, tile * width : (tile + 1) * width] = one(tile, 0)
        further(first, last)
        return {slot: image_of(slot) for slot in slots}

    def hold(values, slot):
        vector[:, slot * size : (slot + 1) * size] = doubled(values)

    for slot in range(slots):
        hold(zeroth[slot], slot)

    def tile_step(tile, _):
        before = jnp.maximum(tile - 1, 0)
        image[:, lanes_of(before)] = one(before, 0)
        build(tile, 0)
        return 0

    lax.fori_loop(0, tiles, tile_step, 0)
    image[:, (tiles - 1) * width : tiles * width] = one(tiles - 1, 0)

    @pl.when(most > 1)
    def _():
        def of_tile(tile, _):
            def more(step, _):
                build(tile, step)
                return 0

            return lax.fori_loop(1, steps_of(tile), more, 0)

        lax.fori_loop(0, tiles, of_tile, 0)

    further(0, tiles)
    first = {slot: image_of(slot) for slot in range(1, 5)}
    for slot in range(1, 5):
        hold(first[slot], slot)
    second = power([2, 3])
    hold(jnp.zeros((8, size), F32), 1)
    hold(second[2], 2)
    hold(2.0 * second[3], 3)
    last = power([2])[2]

    def inner(left, right):
        return jnp.sum(left * right, axis=1, keepdims=True)

    moments = [
        inner(zeroth[2], zeroth[2]),
        inner(zeroth[2], first[2]),
        inner(first[2], first[2]),
        inner(first[2], second[2]),
        inner(second[2], second[2]),
        inner(second[2], last),
    ]
    lane = lax.broadcasted_iota(jnp.int32, (8, 128), 1)
    packed = jnp.zeros((8, 128), F32)
    for index, moment in enumerate(moments):
        packed = jnp.where(lane == index, moment, packed)
    values = jnp.concatenate([first[2][:3], second[2][:3], jnp.zeros((2, size), F32)], axis=0)
    for index in range(out_ref.shape[0]):
        out_ref[index, :, :size] = values
        out_ref[index, :, size:] = packed
    for copy in copies:
        copy.wait()


def powers(mine, other, new_low, new_high, new_flow, count):
    chips, _, size = mine.shape
    tiles = 4 * size // 256
    steps = (6 * size // CHUNK + 5) // 6
    return pl.pallas_call(
        functools.partial(powers_kernel, count),
        out_shape=(
            jax.ShapeDtypeStruct((chips, 8, size + 128), F32),
            jax.ShapeDtypeStruct(new_flow.shape, F32),
        ),
        in_specs=[VMEM] * 4 + [HBM],
        out_specs=(VMEM, HBM),
        scratch_shapes=[
            pltpu.VMEM((6 * size + 6 * CHUNK, 48), BF16),
            pltpu.VMEM((48, 6 * size), BF16),
            pltpu.VMEM((16, 6 * size + 6 * CHUNK), BF16),
            pltpu.VMEM((16, 4 * size), F32),
            pltpu.VMEM((tiles, steps, 12 * CHUNK, 256), BF16),
            pltpu.SMEM((tiles,), jnp.int32),
            pltpu.SMEM((tiles,), jnp.int32),
            pltpu.SemaphoreType.DMA((2,)),
        ],
        input_output_aliases={4: 1},
        compiler_params=pltpu.CompilerParams(vmem_limit_bytes=BIG_LIMIT),
        name="powers",
    )(mine, other, new_low, new_high, new_flow)


def ratio(top, bottom):
    safe = bottom > 0.0
    return jnp.where(safe, top / jnp.where(safe, bottom, 1.0), 0.0)


def weights_of(moments):
    def inner(left, right):
        total = None
        for i, a in enumerate(left):
            for j, c in enumerate(right):
                term = a * c * moments[i + j]
                total = term if total is None else total + term
        return total

    one = jnp.ones_like(moments[0])
    residual, search = [one], [one]
    coefficients = [0.0 * one] * 3
    energy = moments[0]
    for step in range(3):
        image = [CENTRE_SHIFT * value for value in search] + [0.0 * one]
        for index, value in enumerate(search):
            image[index + 1] = image[index + 1] + value
        length = ratio(energy, inner(search, image))
        for index, value in enumerate(search):
            coefficients[index] = coefficients[index] + length * value
        if step == 2:
            break
        longer = residual + [0.0 * one]
        residual = [value - length * other for value, other in zip(longer, image)]
        fresh = jnp.maximum(inner(residual, residual), 0.0)
        scale = ratio(fresh, energy)
        search = [
            value + scale * (search[index] if index < len(search) else 0.0)
            for index, value in enumerate(residual)
        ]
        energy = fresh
    return coefficients


REACH = 7


def bounds_of(source_z, target_z):
    chunks = source_z.shape[1] // CHUNK
    tiles = target_z.shape[1] // CHUNK

    def edges(values, pieces):
        rows = jnp.concatenate([values[:, i * CHUNK : (i + 1) * CHUNK] for i in range(pieces)], axis=0)
        return jnp.min(rows, axis=1, keepdims=True), jnp.max(rows, axis=1, keepdims=True)

    def across(values):
        return jnp.broadcast_to(values, (tiles, 128)).T[0:1]

    source_low, source_high = edges(source_z, chunks)
    target_low, target_high = edges(target_z, tiles)
    near = jnp.logical_and(
        source_high >= across(target_low) - (1.0 + MARGIN), source_low <= across(target_high) + (1.0 + MARGIN)
    )
    index = lax.broadcasted_iota(jnp.int32, (chunks, tiles), 0).astype(F32)
    low = jnp.min(jnp.where(near, index, float(chunks)), axis=0, keepdims=True)
    high = jnp.max(jnp.where(near, index + 1.0, 0.0), axis=0, keepdims=True)
    return jnp.concatenate([low, high], axis=0)


def first_listed(tile_ref, me):
    return tile_ref[pl.ds(me, 1), :][0, 0]


def points_kernel(tile_ref, mine_ref, other_ref, nodes_ref, source_ref, target_ref, bound_ref):
    size = mine_ref.shape[2]
    core = lax.axis_index("core")
    me = lax.axis_index("chip") * 2 + core
    listed = tile_ref.shape[1]
    start = first_listed(tile_ref, me)
    origin = lax.div((start + 2) * 2, 5).astype(F32)
    third = []
    for index in range(listed):
        data = block_of(mine_ref, other_ref, start + index, core)
        points = local_points(data[3:6], origin)
        third.append(points[2:3])
        source, _ = sides(points)
        source_ref[index * size : (index + 1) * size] = source.T.astype(BF16)
    span = REACH * CHUNK
    far = (lax.broadcasted_iota(jnp.int32, (span, 48), 1) == 3).astype(F32) * 4096.0
    source_ref[listed * size :] = far.astype(BF16)
    points = local_points(nodes_ref[0:3], origin)
    _, target = sides(points)
    target_ref[...] = target.astype(BF16)
    bound_ref[...] = bounds_of(jnp.concatenate(third, axis=1), points[2:3])


def near_points(tile_blocks, mine, other, nodes):
    size = mine.shape[2]
    slots = nodes.shape[1]
    listed = tile_blocks.shape[1]
    return pl.pallas_call(
        points_kernel,
        out_shape=(
            jax.ShapeDtypeStruct((listed * size + REACH * CHUNK, 48), BF16),
            jax.ShapeDtypeStruct((48, slots), BF16),
            jax.ShapeDtypeStruct((2, slots // CHUNK), F32),
        ),
        in_specs=[VMEM] * 4,
        out_specs=(VMEM,) * 3,
        compiler_params=pltpu.CompilerParams(vmem_limit_bytes=SMALL_LIMIT),
        cost_estimate=pl.CostEstimate(flops=1_000_000, bytes_accessed=1_000_000, transcendentals=0),
        name="near_points",
    )(tile_blocks, mine, other, nodes)


def near_kernel(
    tile_ref, count_ref, bound_ref, mine_ref, other_ref, mine_power, other_power, source_side, target_side,
    centre_table, node_table, coef_ref, shift_ref, vector, result, low_ref, step_ref,
):
    size = mine_ref.shape[2]
    slots = target_side.shape[1]
    chips = mine_ref.shape[0]
    core = lax.axis_index("core")
    me = lax.axis_index("chip") * 2 + core
    listed = tile_ref.shape[1]
    start_block = first_listed(tile_ref, me)
    width = CHUNK
    tiles = slots // width
    span = REACH * CHUNK
    total = listed * size

    bounds = bound_ref[...].astype(jnp.int32)
    most = 0
    for tile in range(tiles):
        low = bounds[0, tile]
        steps = lax.div(bounds[1, tile] - low + (REACH - 1), REACH)
        low_ref[tile] = low
        step_ref[tile] = steps
        most = jnp.maximum(most, steps)

    summed = mine_power[0, :, size:] + other_power[0, :, size:]
    for index in range(1, chips):
        summed = summed + (mine_power[index, :, size:] + other_power[index, :, size:])
    weights = weights_of([summed[:, index : index + 1] for index in range(6)])

    def coefficients_of(block):
        data = block_of(mine_ref, other_ref, block, core)
        power = block_of(mine_power, other_power, block, core)[:, :size]
        values = weights[0] * data + weights[1] * power + weights[2] * pltpu.roll(power, 5, 0)
        keep = lax.broadcasted_iota(jnp.int32, (8, size), 0) < 3
        return jnp.where(keep, values, 0.0)

    for index in range(listed):
        vector[:, index * size : (index + 1) * size] = doubled(coefficients_of(start_block + index))
    vector[:, total:] = jnp.zeros((16, span), BF16)
    coef_ref[...] = moved_back(coefficients_of(me), centre_table[...])

    def lanes_of(tile):
        return pl.ds(pl.multiple_of(tile * width, width), width)

    def one(tile, step):
        start = pl.multiple_of((low_ref[tile] + step * REACH) * CHUNK, CHUNK)
        table = quarter_kernel(source_side[pl.ds(start, span)], target_side[:, lanes_of(tile)])
        window = vector[:, pl.ds(start, span)]
        return jnp.dot(jnp.concatenate([window, window], axis=1), doubled(table), preferred_element_type=F32)

    def two_tiles(step, _):
        for piece in range(2):
            result[:, lanes_of(2 * step + piece)] = one(2 * step + piece, 0)
        return 0

    lax.fori_loop(0, tiles // 2, two_tiles, 0)

    @pl.when(most > 1)
    def _():
        def of_tile(tile, _):
            def add(step, _):
                result[:, lanes_of(tile)] += one(tile, step)
                return 0

            return lax.fori_loop(1, step_ref[tile], add, 0)

        lax.fori_loop(0, tiles, of_tile, 0)

    lane = lax.broadcasted_iota(jnp.int32, count_ref.shape, 1)
    live = jnp.sum(jnp.where(lane == me, count_ref[...], 0).astype(F32), axis=1, keepdims=True)
    slot = lax.broadcasted_iota(jnp.int32, (3, slots), 1).astype(F32)
    both = result[...]
    shift = moved_back(4.0 * (both[:8] + both[8:]), node_table[...])
    shift_ref[...] = jnp.where(slot < live, shift, 0.0)


def near_body(tile_blocks, near_count, bounds, mine, other, mine_power, other_power, sources, targets, centre_table, node_table):
    size = mine.shape[2]
    slots = targets.shape[1]
    total = tile_blocks.shape[1] * size
    return pl.pallas_call(
        near_kernel,
        out_shape=(
            jax.ShapeDtypeStruct((3, size), F32),
            jax.ShapeDtypeStruct((3, slots), F32),
        ),
        in_specs=[VMEM] * 11,
        out_specs=(VMEM, VMEM),
        scratch_shapes=[
            pltpu.VMEM((16, total + REACH * CHUNK), BF16),
            pltpu.VMEM((16, slots), F32),
            pltpu.SMEM((slots // CHUNK,), jnp.int32),
            pltpu.SMEM((slots // CHUNK,), jnp.int32),
        ],
        compiler_params=pltpu.CompilerParams(vmem_limit_bytes=SMALL_LIMIT),
        name="near_body",
    )(
        tile_blocks, near_count.reshape(1, -1), bounds, mine, other, mine_power, other_power, sources, targets,
        centre_table, node_table,
    )


def gathered(values, partner):
    mine = lax.all_to_all(values, "chip", 0, 0)
    return mine, lax.ppermute(mine, SLAB, partner)


def shards(
    count,
    flow_state,
    flow_speed,
    wall_cell,
    base_shift,
    normals,
    centres,
    tile_blocks,
    near_count,
    near_nodes,
):
    partner = [(i, i ^ 1) for i in range(count)]
    across = [(i, i + 1) for i in range(1, count - 1, 2)]
    across = across + [(j, i) for i, j in across]
    chips, rows = count // 2, flow_state.shape[1]
    send_b = edge_rows(False, flow_state, flow_speed)
    from_b = lax.ppermute(send_b, SLAB, across)
    send_a = edge_rows(True, flow_state, flow_speed, send_b)
    from_a = lax.ppermute(send_a, SLAB, partner)
    in_order, centre_table, nodes, node_table = ordered(base_shift, normals, centres, wall_cell, near_nodes)
    new_flow, low, high, base, chosen = inner_flux(flow_state, flow_speed, in_order)
    packed, low, high = right_side(chips, rows, send_a, send_b, from_a, from_b, low, high, base, chosen)
    mine, other = gathered(packed, partner)
    power, new_flow = powers(mine, other, low, high, new_flow, count)
    mine_power, other_power = gathered(power, partner)
    sources, targets, bounds = near_points(tile_blocks, mine, other, nodes)
    coefficients, node_shift = near_body(
        tile_blocks, near_count, bounds, mine, other, mine_power, other_power, sources, targets,
        centre_table, node_table,
    )
    return new_flow, coefficients, node_shift


def solution(mesh):
    groups, count = mesh.shape["groups"], mesh.shape["slab"]
    split = Mesh(mesh.devices.reshape(groups, count // 2, 2), ("groups",) + SLAB)
    in_specs = (
        P("groups", SLAB, None),
        P("groups", SLAB, None),
        P(("groups",) + SLAB),
        P("groups", SLAB),
        P("groups", SLAB),
        P("groups", SLAB),
        P("groups", None),
        P("groups"),
        P("groups", SLAB),
    )
    out_specs = (P("groups", SLAB, None), P("groups", SLAB), P("groups", SLAB))
    return jax.shard_map(
        functools.partial(shards, count), mesh=split, in_specs=in_specs, out_specs=out_specs, check_vma=False
    )
```

```python
import functools

import jax
import jax.numpy as jnp
from jax import lax
from jax.experimental import pallas as pl
from jax.experimental.pallas import tpu as pltpu
from jax.sharding import Mesh
from jax.sharding import PartitionSpec as P


FLUX_STEP = 0.2
SUPPORT = 0.15
DIAG_SHIFT = 0.5
CENTRE_SHIFT = DIAG_SHIFT + 1.0
TINY = 1e-12
DEPTH = 0.4
CHUNK = 128
MARGIN = 1e-3
ORDER_FLOPS = 2_000_000_000
BIG_LIMIT = 48 * 1024 * 1024
SMALL_LIMIT = 16 * 1024 * 1024

F32 = jnp.float32
BF16 = jnp.bfloat16
SLAB = ("chip", "core")
VMEM = pl.BlockSpec(memory_space=pltpu.VMEM)
SMEM = pl.BlockSpec(memory_space=pltpu.SMEM)
HBM = pl.BlockSpec(memory_space=pltpu.HBM)


def parts(values):
    first = values.astype(BF16).astype(F32)
    rest = values - first
    second = rest.astype(BF16).astype(F32)
    return first, second, rest - second


def doubled(values):
    high = values.astype(BF16)
    return jnp.concatenate([high, (values - high.astype(F32)).astype(BF16)], axis=0)


def sides(points):
    count = points.shape[1]
    squares = jnp.sum(points * points, axis=0, keepdims=True)
    one = jnp.ones((1, count), F32)
    zero = jnp.zeros((3, count), F32)
    a, b, c = parts(jnp.concatenate([points, squares, one, zero], axis=0))
    d, e, f = parts(jnp.concatenate([-2.0 * points, one, squares, zero], axis=0))
    return jnp.concatenate([a, a, b, a, c, b], axis=0), jnp.concatenate([d, e, d, f, d, e], axis=0)


def quarter_kernel(sources, targets):
    squared = jnp.maximum(jnp.dot(sources, targets, preferred_element_type=F32), TINY)
    inside = jnp.maximum(1.0 - squared * lax.rsqrt(squared), 0.0)
    square_in = inside * inside
    return square_in * square_in * (1.25 - inside)


def local_points(raw, origin):
    x = (raw[0:2] - 0.5) * (1.0 / SUPPORT)
    return jnp.concatenate([x, (raw[2:3] - origin) * (1.0 / SUPPORT)], axis=0)


def rank_of(values):
    count = values.shape[1]
    column = jnp.broadcast_to(values, (8, count)).T[:, 0:1]
    result = []
    for tile in range(count // CHUNK):
        mine = values[:, tile * CHUNK : (tile + 1) * CHUNK]
        total = jnp.zeros((8, CHUNK), F32)
        for chunk in range(count // CHUNK):
            other = column[chunk * CHUNK : (chunk + 1) * CHUNK]
            if chunk < tile:
                before = other <= mine
            elif chunk > tile:
                before = other < mine
            else:
                above = lax.broadcasted_iota(jnp.int32, (CHUNK, CHUNK), 0) < lax.broadcasted_iota(
                    jnp.int32, (CHUNK, CHUNK), 1
                )
                before = jnp.logical_or(other < mine, jnp.logical_and(other == mine, above))
            ones = jnp.where(before, 1.0, 0.0)
            for group in range(CHUNK // 8):
                total = total + ones[group * 8 : group * 8 + 8]
        result.append(jnp.sum(total, axis=0, keepdims=True))
    return jnp.concatenate(result, axis=1)


def moved(values, table):
    rows = values.shape[0]
    stacked = jnp.concatenate(parts(values), axis=0).astype(BF16)
    both = lax.dot_general(
        stacked, table, (((1,), (1,)), ((), ())), preferred_element_type=F32
    )
    return (both[:rows] + both[rows : 2 * rows]) + both[2 * rows :]


def moved_back(values, table):
    both = jnp.dot(doubled(values), table, preferred_element_type=F32)
    return both[:3] + both[8:11]


def chunk_bounds(source_z, target_z, width, low_ref, high_ref):
    chunks = source_z.shape[1] // CHUNK
    tiles = target_z.shape[1] // width

    def edges(values, size, pieces):
        rows = jnp.concatenate([values[:, i * size : (i + 1) * size] for i in range(pieces)], axis=0)
        return jnp.min(rows, axis=1, keepdims=True), jnp.max(rows, axis=1, keepdims=True)

    source_low, source_high = edges(source_z, CHUNK, chunks)
    target_low, target_high = edges(target_z, width, tiles)
    index = lax.broadcasted_iota(jnp.int32, (chunks, 1), 0).astype(F32)
    for tile in range(tiles):
        near = jnp.logical_and(
            source_high >= target_low[tile : tile + 1] - (1.0 + MARGIN),
            source_low <= target_high[tile : tile + 1] + (1.0 + MARGIN),
        )
        low_ref[tile] = jnp.min(jnp.where(near, index, float(chunks))).astype(jnp.int32)
        high_ref[tile] = jnp.max(jnp.where(near, index + 1.0, 0.0)).astype(jnp.int32)


def order_kernel(base_ref, normal_ref, centre_ref, cell_ref, nodes_ref, out_ref, centre_table, nodes_out, node_table):
    def table_of(ref, rank):
        count = rank.shape[1]
        rows = 128
        for start in range(0, count, rows):
            row = lax.broadcasted_iota(jnp.int32, (rows, count), 0).astype(F32) + float(start)
            ref[start : start + rows] = jnp.where(row == rank, 1.0, 0.0).astype(BF16)

    count = centre_ref.shape[1]
    table_of(centre_table, rank_of(centre_ref[2:3]))
    values = jnp.concatenate(
        [
            base_ref[...],
            normal_ref[...],
            centre_ref[...],
            cell_ref[...].astype(F32),
            jnp.zeros((6, count), F32),
        ],
        axis=0,
    )
    out_ref[...] = moved(values, centre_table[...])
    table_of(node_table, rank_of(nodes_ref[2:3]))
    nodes = jnp.concatenate([nodes_ref[...], jnp.zeros((5, nodes_ref.shape[1]), F32)], axis=0)
    nodes_out[...] = moved(nodes, node_table[...])


def ordered(base_shift, normals, centres, wall_cell, near_nodes):
    count, slots = centres.shape[1], near_nodes.shape[1]
    return pl.pallas_call(
        order_kernel,
        out_shape=(
            jax.ShapeDtypeStruct((16, count), F32),
            jax.ShapeDtypeStruct((count, count), BF16),
            jax.ShapeDtypeStruct((8, slots), F32),
            jax.ShapeDtypeStruct((slots, slots), BF16),
        ),
        in_specs=[VMEM] * 5,
        out_specs=(VMEM,) * 4,
        compiler_params=pltpu.CompilerParams(vmem_limit_bytes=SMALL_LIMIT),
        cost_estimate=pl.CostEstimate(flops=ORDER_FLOPS, bytes_accessed=4_000_000, transcendentals=0),
        name="order",
    )(base_shift, normals, centres, wall_cell.reshape(1, -1), near_nodes)


def edge_kernel(even_last, q_ref, w_ref, target, sems):
    count, rows, _ = q_ref.shape

    def move(row):
        copies = []
        for index in range(count + 1):
            source = q_ref.at[index] if index < count else w_ref.at[0]
            copies.append(
                pltpu.make_async_copy(source.at[pl.ds(row, 1)], target.at[pl.ds(index, 1)], sems.at[index])
            )
        for copy in copies:
            copy.start()
        for copy in copies:
            copy.wait()

    core = lax.axis_index("core")

    @pl.when(core == 0)
    def _():
        move(rows - 1 if even_last else 0)

    @pl.when(core != 0)
    def _():
        move(0 if even_last else rows - 1)


def edge_rows(even_last, flow_state, flow_speed):
    count, _, plane = flow_state.shape
    return pl.pallas_call(
        functools.partial(edge_kernel, even_last),
        out_shape=jax.ShapeDtypeStruct((count + 1, plane), F32),
        in_specs=[HBM, HBM],
        out_specs=VMEM,
        scratch_shapes=[pltpu.SemaphoreType.DMA((count + 1,))],
        compiler_params=pltpu.CompilerParams(vmem_limit_bytes=SMALL_LIMIT),
        name="edge_rows",
    )(
        pltpu.with_memory_space_constraint(flow_state, pltpu.HBM),
        pltpu.with_memory_space_constraint(flow_speed, pltpu.HBM),
    )


RATE = 0.5 * FLUX_STEP
PRESSURE = 4


def picked(stacked, chosen, lane):
    high, middle, low = parts(stacked)
    pieces = jnp.concatenate([high, middle, low], axis=1).astype(BF16)
    both = lax.dot_general(pieces, chosen, (((0,), (0,)), ((), ())), preferred_element_type=F32)
    value = (both[:128] + both[128:256]) + both[256:]
    here = lax.broadcasted_iota(jnp.int32, value.shape, 0) == lane
    return jnp.sum(jnp.where(here, value, 0.0), axis=0, keepdims=True)


def stacked_lanes(values):
    return jnp.concatenate([values[:, i : i + 128] for i in range(0, values.shape[1], 128)], axis=0)


def inner_kernel(q_ref, w_ref, sorted_ref, new_hbm, low_ref, high_ref, out_ref, chosen_ref, new_ref, sems):
    count, rows, plane = q_ref.shape
    width = 512
    steps = plane // width
    row = lax.broadcasted_iota(jnp.int32, (rows, width), 0)

    def copy_of(step):
        lanes = pl.ds(pl.multiple_of(step * width, width), width)
        return pltpu.make_async_copy(new_ref.at[:, :, lanes], new_hbm.at[:, :, lanes], sems.at[step])

    def chunk(step, _):
        here = pl.multiple_of(step * width, 128)
        left = pl.multiple_of(lax.rem(here + plane - 128, plane), 128)
        right = pl.multiple_of(lax.rem(here + width, plane), 128)

        def cyclic(ref, index):
            values = ref[index, :, pl.ds(here, width)]
            wide = jnp.concatenate(
                [ref[index, :, pl.ds(left, 128)], values, ref[index, :, pl.ds(right, 128)]], axis=1
            )
            before = pltpu.roll(wide, 1, 1)[:, 128 : 128 + width]
            after = pltpu.roll(wide, width + 255, 1)[:, 128 : 128 + width]
            return values, before, after

        w = w_ref[0, :, pl.ds(here, width)]
        face_low = jnp.where(row == 0, 0.0, RATE * (pltpu.roll(w, 1, 0) + w))
        face_high = jnp.where(row == rows - 1, 0.0, RATE * (w + pltpu.roll(w, rows - 1, 0)))
        speed, speed_before, speed_after = cyclic(w_ref, 1)
        face_left = RATE * (speed_before + speed)
        face_right = RATE * (speed + speed_after)
        low_in = jnp.maximum(face_low, 0.0)
        high_out = jnp.minimum(face_high, 0.0)
        left_in = jnp.maximum(face_left, 0.0)
        right_out = jnp.minimum(face_right, 0.0)
        keep = 1.0 - (
            (jnp.maximum(face_high, 0.0) - jnp.minimum(face_low, 0.0))
            + (jnp.maximum(face_right, 0.0) - jnp.minimum(face_left, 0.0))
        )
        for index in range(count):
            values, before, after = cyclic(q_ref, index)
            new = (
                keep * values
                + low_in * pltpu.roll(values, 1, 0)
                - high_out * pltpu.roll(values, rows - 1, 0)
                + left_in * before
                - right_out * after
            )
            new_ref[index, :, pl.ds(here, width)] = new
            low_ref[index : index + 1, pl.ds(here, width)] = new[0:1]
            high_ref[index : index + 1, pl.ds(here, width)] = new[rows - 1 : rows]
        copy_of(step).start()
        return 0

    lax.fori_loop(0, steps, chunk, 0)

    cells = sorted_ref[9:10].astype(jnp.int32)
    cell_row = cells // plane
    column = cells - cell_row * plane
    group = column // 128
    lane = column - group * 128
    place = group * rows + cell_row
    centres = cells.shape[1]
    lanes = plane // 128
    chosen = (lax.broadcasted_iota(jnp.int32, (rows * lanes, centres), 0) == place).astype(F32).astype(BF16)
    chosen_ref[...] = chosen
    load = picked(stacked_lanes(new_ref[PRESSURE]), chosen, lane)
    out_ref[...] = jnp.concatenate(
        [
            sorted_ref[0:3] + sorted_ref[3:6] * load,
            sorted_ref[3:9],
            lane.astype(F32),
            jnp.zeros((6, centres), F32),
        ],
        axis=0,
    )
    for step in range(steps):
        copy_of(step).wait()


def inner_flux(flow_state, flow_speed, in_order):
    count, rows, plane = flow_state.shape
    centres = in_order.shape[1]
    edge = jax.ShapeDtypeStruct((count, plane), F32)
    return pl.pallas_call(
        inner_kernel,
        out_shape=(
            jax.ShapeDtypeStruct(flow_state.shape, F32),
            edge,
            edge,
            jax.ShapeDtypeStruct((16, centres), F32),
            jax.ShapeDtypeStruct((rows * plane // 128, centres), BF16),
        ),
        in_specs=[VMEM] * 3,
        out_specs=(HBM, VMEM, VMEM, VMEM, VMEM),
        scratch_shapes=[pltpu.VMEM(flow_state.shape, F32), pltpu.SemaphoreType.DMA((plane // 512,))],
        compiler_params=pltpu.CompilerParams(vmem_limit_bytes=SMALL_LIMIT),
        cost_estimate=pl.CostEstimate(flops=20_000_000, bytes_accessed=4_000_000, transcendentals=0),
        name="inner_flux",
    )(flow_state, flow_speed, in_order)


def outer_kernel(
    send_a, send_b, from_a, from_b, low_ref, high_ref, base_ref, chosen_ref, out_ref, new_low, new_high, both_ref
):
    count, plane = low_ref.shape
    rows = both_ref.shape[0]
    even = lax.axis_index("core") == 0
    own_low = jnp.where(even, send_b[...], send_a[...])
    own_high = jnp.where(even, send_a[...], send_b[...])
    below = jnp.where(even, from_b[...], from_a[...])
    above = jnp.where(even, from_a[...], from_b[...])

    def flux(first, second):
        face = RATE * (first[count : count + 1] + second[count : count + 1])
        return jnp.maximum(face, 0.0) * first[:count] + jnp.minimum(face, 0.0) * second[:count]

    low = flux(below, own_low)
    high = flux(own_high, above)
    new_low[...] = low_ref[...] + low
    new_high[...] = high_ref[...] - high
    row = lax.broadcasted_iota(jnp.int32, (rows, plane), 0)
    zero = jnp.zeros((rows, plane), F32)
    added = jnp.where(row == 0, low[PRESSURE : PRESSURE + 1], zero)
    added = added - jnp.where(row == rows - 1, high[PRESSURE : PRESSURE + 1], zero)
    both_ref[...] = added
    base = base_ref[...]
    load = picked(stacked_lanes(both_ref[...]), chosen_ref[...], base[9:10].astype(jnp.int32))
    centres = base.shape[1]
    packed = jnp.concatenate([base[0:3] + base[3:6] * load, base[6:9], jnp.zeros((2, centres), F32)], axis=0)
    for chip in range(out_ref.shape[0]):
        out_ref[chip] = packed


def right_side(chips, rows, send_a, send_b, from_a, from_b, low, high, base, chosen):
    edge = jax.ShapeDtypeStruct(low.shape, F32)
    return pl.pallas_call(
        outer_kernel,
        out_shape=(jax.ShapeDtypeStruct((chips, 8, base.shape[1]), F32), edge, edge),
        in_specs=[VMEM] * 8,
        out_specs=(VMEM,) * 3,
        scratch_shapes=[pltpu.VMEM((rows, low.shape[1]), F32)],
        compiler_params=pltpu.CompilerParams(vmem_limit_bytes=SMALL_LIMIT),
        name="outer_flux",
    )(send_a, send_b, from_a, from_b, low, high, base, chosen)


def block_of(mine_ref, other_ref, block, core):
    chip = lax.div(block, 2)
    own = lax.rem(block, 2) == core
    return jnp.where(own, mine_ref[chip], other_ref[chip])


def powers_kernel(
    count, mine_ref, other_ref, new_low, new_high, new_in, out_ref, new_out,
    source_side, target_side, vector, image, tables, low_ref, high_ref, sems,
):
    del new_in
    rows_per_block = new_out.shape[1]
    copies = [
        pltpu.make_async_copy(new_low, new_out.at[:, 0], sems.at[0]),
        pltpu.make_async_copy(new_high, new_out.at[:, rows_per_block - 1], sems.at[1]),
    ]
    for copy in copies:
        copy.start()
    size = mine_ref.shape[2]
    chip, core = lax.axis_index("chip"), lax.axis_index("core")
    me = chip * 2 + core
    slots, width, reach = 6, 256, 6
    span = reach * CHUNK
    total = slots * size
    origin = lax.div(me * 2, 5).astype(F32)
    value_row = lax.broadcasted_iota(jnp.int32, (8, size), 0) < 3

    live, zeroth, third = [], [], []
    for slot in range(slots):
        block = me + slot - 2
        valid = jnp.logical_and(block >= 0, block < count)
        live.append(valid)
        data = block_of(mine_ref, other_ref, jnp.clip(block, 0, count - 1), core)
        zeroth.append(jnp.where(jnp.logical_and(value_row, valid), data, 0.0))
        middle = (block.astype(F32) + 0.5) * DEPTH
        raw = jnp.concatenate([data[3:5], jnp.where(valid, data[5:6], middle)], axis=0)
        points = local_points(raw, origin)
        third.append(points[2:3])
        source, target = sides(points)
        source_side[slot * size : (slot + 1) * size] = source.T.astype(BF16)
        target_side[:, slot * size : (slot + 1) * size] = target.astype(BF16)
    far = (lax.broadcasted_iota(jnp.int32, (span, 48), 1) == 3).astype(F32) * 4096.0
    source_side[total:] = far.astype(BF16)
    vector[:, total:] = jnp.zeros((16, span), BF16)
    heights = jnp.concatenate(third, axis=1)
    chunk_bounds(heights, heights[:, size : 5 * size], width, low_ref, high_ref)
    tiles = 4 * size // width

    def steps_of(tile):
        return lax.div(high_ref[tile] - low_ref[tile] + (reach - 1), reach)

    most = steps_of(0)
    for tile in range(1, tiles):
        most = jnp.maximum(most, steps_of(tile))
    same = lax.broadcasted_iota(jnp.int32, (CHUNK, CHUNK), 0) == lax.broadcasted_iota(
        jnp.int32, (CHUNK, CHUNK), 1
    )

    def build(tile, step):
        lanes = pl.ds(pl.multiple_of(tile * width + size, width), width)
        chunk = low_ref[tile] + step * reach
        rows = pl.ds(pl.multiple_of(chunk * CHUNK, CHUNK), span)
        table = quarter_kernel(source_side[rows], target_side[:, lanes])
        high = table.astype(BF16)
        tables[tile, step, :span] = high
        tables[tile, step, span:] = (table - high.astype(F32)).astype(BF16)
        for piece in range(width // CHUNK):
            place = (tile * width + size) // CHUNK + piece - chunk
            inside = jnp.logical_and(place >= 0, place < reach)
            place = jnp.clip(place, 0, reach - 1)
            for half in range(2):
                at = pl.ds(pl.multiple_of(place * CHUNK + half * span, CHUNK), CHUNK)
                columns = slice(piece * CHUNK, (piece + 1) * CHUNK)
                old = tables[tile, step, at, columns]
                tables[tile, step, at, columns] = jnp.where(jnp.logical_and(same, inside), 0.0, old.astype(F32)).astype(BF16)

    def one(tile, step):
        lanes = pl.ds(pl.multiple_of((low_ref[tile] + step * reach) * CHUNK, CHUNK), span)
        window = vector[:, lanes]
        return jnp.dot(jnp.concatenate([window, window], axis=1), tables[tile, step], preferred_element_type=F32)

    def lanes_of(tile):
        return pl.ds(pl.multiple_of(tile * width, width), width)

    def further(first, last):
        @pl.when(most > 1)
        def _():
            def of_tile(tile, _):
                def add(step, _):
                    image[:, lanes_of(tile)] += one(tile, step)
                    return 0

                return lax.fori_loop(1, steps_of(tile), add, 0)

            lax.fori_loop(first, last, of_tile, 0)

    def image_of(slot):
        both = image[:, (slot - 1) * size : slot * size]
        return jnp.where(live[slot], 4.0 * (both[:8] + both[8:]), 0.0)

    def power(slots):
        first, last = (slots[0] - 1) * size // width, slots[-1] * size // width
        for tile in range(first, last):
            image[:, tile * width : (tile + 1) * width] = one(tile, 0)
        further(first, last)
        return {slot: image_of(slot) for slot in slots}

    def hold(values, slot):
        vector[:, slot * size : (slot + 1) * size] = doubled(values)

    for slot in range(slots):
        hold(zeroth[slot], slot)

    def tile_step(tile, _):
        before = jnp.maximum(tile - 1, 0)
        image[:, lanes_of(before)] = one(before, 0)
        build(tile, 0)
        return 0

    lax.fori_loop(0, tiles, tile_step, 0)
    image[:, (tiles - 1) * width : tiles * width] = one(tiles - 1, 0)

    @pl.when(most > 1)
    def _():
        def of_tile(tile, _):
            def more(step, _):
                build(tile, step)
                return 0

            return lax.fori_loop(1, steps_of(tile), more, 0)

        lax.fori_loop(0, tiles, of_tile, 0)

    further(0, tiles)
    first = {slot: image_of(slot) for slot in range(1, 5)}
    for slot in range(1, 5):
        hold(first[slot], slot)
    second = power([2, 3])
    hold(jnp.zeros((8, size), F32), 1)
    hold(second[2], 2)
    hold(2.0 * second[3], 3)
    last = power([2])[2]

    def inner(left, right):
        return jnp.sum(left * right, axis=1, keepdims=True)

    moments = [
        inner(zeroth[2], zeroth[2]),
        inner(zeroth[2], first[2]),
        inner(first[2], first[2]),
        inner(first[2], second[2]),
        inner(second[2], second[2]),
        inner(second[2], last),
    ]
    lane = lax.broadcasted_iota(jnp.int32, (8, 128), 1)
    packed = jnp.zeros((8, 128), F32)
    for index, moment in enumerate(moments):
        packed = jnp.where(lane == index, moment, packed)
    values = jnp.concatenate([first[2][:3], second[2][:3], jnp.zeros((2, size), F32)], axis=0)
    for index in range(out_ref.shape[0]):
        out_ref[index, :, :size] = values
        out_ref[index, :, size:] = packed
    for copy in copies:
        copy.wait()


def powers(mine, other, new_low, new_high, new_flow, count):
    chips, _, size = mine.shape
    tiles = 4 * size // 256
    steps = (6 * size // CHUNK + 5) // 6
    return pl.pallas_call(
        functools.partial(powers_kernel, count),
        out_shape=(
            jax.ShapeDtypeStruct((chips, 8, size + 128), F32),
            jax.ShapeDtypeStruct(new_flow.shape, F32),
        ),
        in_specs=[VMEM] * 4 + [HBM],
        out_specs=(VMEM, HBM),
        scratch_shapes=[
            pltpu.VMEM((6 * size + 6 * CHUNK, 48), BF16),
            pltpu.VMEM((48, 6 * size), BF16),
            pltpu.VMEM((16, 6 * size + 6 * CHUNK), BF16),
            pltpu.VMEM((16, 4 * size), F32),
            pltpu.VMEM((tiles, steps, 12 * CHUNK, 256), BF16),
            pltpu.SMEM((tiles,), jnp.int32),
            pltpu.SMEM((tiles,), jnp.int32),
            pltpu.SemaphoreType.DMA((2,)),
        ],
        input_output_aliases={4: 1},
        compiler_params=pltpu.CompilerParams(vmem_limit_bytes=BIG_LIMIT),
        name="powers",
    )(mine, other, new_low, new_high, new_flow)


def ratio(top, bottom):
    safe = bottom > 0.0
    return jnp.where(safe, top / jnp.where(safe, bottom, 1.0), 0.0)


def weights_of(moments):
    def inner(left, right):
        total = None
        for i, a in enumerate(left):
            for j, c in enumerate(right):
                term = a * c * moments[i + j]
                total = term if total is None else total + term
        return total

    one = jnp.ones_like(moments[0])
    residual, search = [one], [one]
    coefficients = [0.0 * one] * 3
    energy = moments[0]
    for step in range(3):
        image = [CENTRE_SHIFT * value for value in search] + [0.0 * one]
        for index, value in enumerate(search):
            image[index + 1] = image[index + 1] + value
        length = ratio(energy, inner(search, image))
        for index, value in enumerate(search):
            coefficients[index] = coefficients[index] + length * value
        if step == 2:
            break
        longer = residual + [0.0 * one]
        residual = [value - length * other for value, other in zip(longer, image)]
        fresh = jnp.maximum(inner(residual, residual), 0.0)
        scale = ratio(fresh, energy)
        search = [
            value + scale * (search[index] if index < len(search) else 0.0)
            for index, value in enumerate(residual)
        ]
        energy = fresh
    return coefficients


REACH = 7


def bounds_of(source_z, target_z):
    chunks = source_z.shape[1] // CHUNK
    tiles = target_z.shape[1] // CHUNK

    def edges(values, pieces):
        rows = jnp.concatenate([values[:, i * CHUNK : (i + 1) * CHUNK] for i in range(pieces)], axis=0)
        return jnp.min(rows, axis=1, keepdims=True), jnp.max(rows, axis=1, keepdims=True)

    def across(values):
        return jnp.broadcast_to(values, (tiles, 128)).T[0:1]

    source_low, source_high = edges(source_z, chunks)
    target_low, target_high = edges(target_z, tiles)
    near = jnp.logical_and(
        source_high >= across(target_low) - (1.0 + MARGIN), source_low <= across(target_high) + (1.0 + MARGIN)
    )
    index = lax.broadcasted_iota(jnp.int32, (chunks, tiles), 0).astype(F32)
    low = jnp.min(jnp.where(near, index, float(chunks)), axis=0, keepdims=True)
    high = jnp.max(jnp.where(near, index + 1.0, 0.0), axis=0, keepdims=True)
    return jnp.concatenate([low, high], axis=0)


def first_listed(tile_ref, me):
    return tile_ref[pl.ds(me, 1), :][0, 0]


def points_kernel(tile_ref, mine_ref, other_ref, nodes_ref, source_ref, target_ref, bound_ref):
    size = mine_ref.shape[2]
    core = lax.axis_index("core")
    me = lax.axis_index("chip") * 2 + core
    listed = tile_ref.shape[1]
    start = first_listed(tile_ref, me)
    origin = lax.div((start + 2) * 2, 5).astype(F32)
    third = []
    for index in range(listed):
        data = block_of(mine_ref, other_ref, start + index, core)
        points = local_points(data[3:6], origin)
        third.append(points[2:3])
        source, _ = sides(points)
        source_ref[index * size : (index + 1) * size] = source.T.astype(BF16)
    span = REACH * CHUNK
    far = (lax.broadcasted_iota(jnp.int32, (span, 48), 1) == 3).astype(F32) * 4096.0
    source_ref[listed * size :] = far.astype(BF16)
    points = local_points(nodes_ref[0:3], origin)
    _, target = sides(points)
    target_ref[...] = target.astype(BF16)
    bound_ref[...] = bounds_of(jnp.concatenate(third, axis=1), points[2:3])


def near_points(tile_blocks, mine, other, nodes):
    size = mine.shape[2]
    slots = nodes.shape[1]
    listed = tile_blocks.shape[1]
    return pl.pallas_call(
        points_kernel,
        out_shape=(
            jax.ShapeDtypeStruct((listed * size + REACH * CHUNK, 48), BF16),
            jax.ShapeDtypeStruct((48, slots), BF16),
            jax.ShapeDtypeStruct((2, slots // CHUNK), F32),
        ),
        in_specs=[VMEM] * 4,
        out_specs=(VMEM,) * 3,
        compiler_params=pltpu.CompilerParams(vmem_limit_bytes=SMALL_LIMIT),
        cost_estimate=pl.CostEstimate(flops=1_000_000, bytes_accessed=1_000_000, transcendentals=0),
        name="near_points",
    )(tile_blocks, mine, other, nodes)


def near_kernel(
    tile_ref, count_ref, bound_ref, mine_ref, other_ref, mine_power, other_power, source_side, target_side,
    centre_table, node_table, coef_ref, shift_ref, vector, result, low_ref, step_ref,
):
    size = mine_ref.shape[2]
    slots = target_side.shape[1]
    chips = mine_ref.shape[0]
    core = lax.axis_index("core")
    me = lax.axis_index("chip") * 2 + core
    listed = tile_ref.shape[1]
    start_block = first_listed(tile_ref, me)
    width = CHUNK
    tiles = slots // width
    span = REACH * CHUNK
    total = listed * size

    bounds = bound_ref[...].astype(jnp.int32)
    most = 0
    for tile in range(tiles):
        low = bounds[0, tile]
        steps = lax.div(bounds[1, tile] - low + (REACH - 1), REACH)
        low_ref[tile] = low
        step_ref[tile] = steps
        most = jnp.maximum(most, steps)

    summed = mine_power[0, :, size:] + other_power[0, :, size:]
    for index in range(1, chips):
        summed = summed + (mine_power[index, :, size:] + other_power[index, :, size:])
    weights = weights_of([summed[:, index : index + 1] for index in range(6)])

    def coefficients_of(block):
        data = block_of(mine_ref, other_ref, block, core)
        power = block_of(mine_power, other_power, block, core)[:, :size]
        values = weights[0] * data + weights[1] * power + weights[2] * pltpu.roll(power, 5, 0)
        keep = lax.broadcasted_iota(jnp.int32, (8, size), 0) < 3
        return jnp.where(keep, values, 0.0)

    for index in range(listed):
        vector[:, index * size : (index + 1) * size] = doubled(coefficients_of(start_block + index))
    vector[:, total:] = jnp.zeros((16, span), BF16)
    coef_ref[...] = moved_back(coefficients_of(me), centre_table[...])

    def lanes_of(tile):
        return pl.ds(pl.multiple_of(tile * width, width), width)

    def one(tile, step):
        start = pl.multiple_of((low_ref[tile] + step * REACH) * CHUNK, CHUNK)
        table = quarter_kernel(source_side[pl.ds(start, span)], target_side[:, lanes_of(tile)])
        window = vector[:, pl.ds(start, span)]
        return jnp.dot(jnp.concatenate([window, window], axis=1), doubled(table), preferred_element_type=F32)

    def two_tiles(step, _):
        for piece in range(2):
            result[:, lanes_of(2 * step + piece)] = one(2 * step + piece, 0)
        return 0

    lax.fori_loop(0, tiles // 2, two_tiles, 0)

    @pl.when(most > 1)
    def _():
        def of_tile(tile, _):
            def add(step, _):
                result[:, lanes_of(tile)] += one(tile, step)
                return 0

            return lax.fori_loop(1, step_ref[tile], add, 0)

        lax.fori_loop(0, tiles, of_tile, 0)

    lane = lax.broadcasted_iota(jnp.int32, count_ref.shape, 1)
    live = jnp.sum(jnp.where(lane == me, count_ref[...], 0).astype(F32), axis=1, keepdims=True)
    slot = lax.broadcasted_iota(jnp.int32, (3, slots), 1).astype(F32)
    both = result[...]
    shift = moved_back(4.0 * (both[:8] + both[8:]), node_table[...])
    shift_ref[...] = jnp.where(slot < live, shift, 0.0)


def near_body(tile_blocks, near_count, bounds, mine, other, mine_power, other_power, sources, targets, centre_table, node_table):
    size = mine.shape[2]
    slots = targets.shape[1]
    total = tile_blocks.shape[1] * size
    return pl.pallas_call(
        near_kernel,
        out_shape=(
            jax.ShapeDtypeStruct((3, size), F32),
            jax.ShapeDtypeStruct((3, slots), F32),
        ),
        in_specs=[VMEM] * 11,
        out_specs=(VMEM, VMEM),
        scratch_shapes=[
            pltpu.VMEM((16, total + REACH * CHUNK), BF16),
            pltpu.VMEM((16, slots), F32),
            pltpu.SMEM((slots // CHUNK,), jnp.int32),
            pltpu.SMEM((slots // CHUNK,), jnp.int32),
        ],
        compiler_params=pltpu.CompilerParams(vmem_limit_bytes=SMALL_LIMIT),
        name="near_body",
    )(
        tile_blocks, near_count.reshape(1, -1), bounds, mine, other, mine_power, other_power, sources, targets,
        centre_table, node_table,
    )


def gathered(values, partner):
    mine = lax.all_to_all(values, "chip", 0, 0)
    return mine, lax.ppermute(mine, SLAB, partner)


def shards(
    count,
    flow_state,
    flow_speed,
    wall_cell,
    base_shift,
    normals,
    centres,
    tile_blocks,
    near_count,
    near_nodes,
):
    partner = [(i, i ^ 1) for i in range(count)]
    across = [(i, i + 1) for i in range(1, count - 1, 2)]
    across = across + [(j, i) for i, j in across]
    chips, rows = count // 2, flow_state.shape[1]
    send_b = edge_rows(False, flow_state, flow_speed)
    from_b = lax.ppermute(send_b, SLAB, across)
    send_a = edge_rows(True, flow_state, flow_speed)
    from_a = lax.ppermute(send_a, SLAB, partner)
    in_order, centre_table, nodes, node_table = ordered(base_shift, normals, centres, wall_cell, near_nodes)
    new_flow, low, high, base, chosen = inner_flux(flow_state, flow_speed, in_order)
    packed, low, high = right_side(chips, rows, send_a, send_b, from_a, from_b, low, high, base, chosen)
    mine, other = gathered(packed, partner)
    power, new_flow = powers(mine, other, low, high, new_flow, count)
    mine_power, other_power = gathered(power, partner)
    sources, targets, bounds = near_points(tile_blocks, mine, other, nodes)
    coefficients, node_shift = near_body(
        tile_blocks, near_count, bounds, mine, other, mine_power, other_power, sources, targets,
        centre_table, node_table,
    )
    return new_flow, coefficients, node_shift


def solution(mesh):
    groups, count = mesh.shape["groups"], mesh.shape["slab"]
    split = Mesh(mesh.devices.reshape(groups, count // 2, 2), ("groups",) + SLAB)
    in_specs = (
        P("groups", SLAB, None),
        P("groups", SLAB, None),
        P(("groups",) + SLAB),
        P("groups", SLAB),
        P("groups", SLAB),
        P("groups", SLAB),
        P("groups", None),
        P("groups"),
        P("groups", SLAB),
    )
    out_specs = (P("groups", SLAB, None), P("groups", SLAB), P("groups", SLAB))
    return jax.shard_map(
        functools.partial(shards, count), mesh=split, in_specs=in_specs, out_specs=out_specs, check_vma=False
    )
```

```python
import functools

import jax
import jax.numpy as jnp
from jax import lax
from jax.experimental import pallas as pl
from jax.experimental.pallas import tpu as pltpu
from jax.sharding import Mesh
from jax.sharding import PartitionSpec as P


FLUX_STEP = 0.2
SUPPORT = 0.15
DIAG_SHIFT = 0.5
CENTRE_SHIFT = DIAG_SHIFT + 1.0
TINY = 1e-12
ITERS = 3
LOSS = 0.01
DEPTH = 0.4
CHUNK = 128
MARGIN = 1e-3
ORDER_FLOPS = 2_000_000_000
BIG_LIMIT = 48 * 1024 * 1024
SMALL_LIMIT = 16 * 1024 * 1024

F32 = jnp.float32
BF16 = jnp.bfloat16
SLAB = ("chip", "core")
VMEM = pl.BlockSpec(memory_space=pltpu.VMEM)
SMEM = pl.BlockSpec(memory_space=pltpu.SMEM)
HBM = pl.BlockSpec(memory_space=pltpu.HBM)


def parts(values):
    first = values.astype(BF16).astype(F32)
    rest = values - first
    second = rest.astype(BF16).astype(F32)
    return first, second, rest - second


def doubled(values):
    high = values.astype(BF16)
    return jnp.concatenate([high, (values - high.astype(F32)).astype(BF16)], axis=0)


def sides(points):
    count = points.shape[1]
    squares = jnp.sum(points * points, axis=0, keepdims=True)
    one = jnp.ones((1, count), F32)
    zero = jnp.zeros((3, count), F32)
    a, b, c = parts(jnp.concatenate([points, squares, one, zero], axis=0))
    d, e, f = parts(jnp.concatenate([-2.0 * points, one, squares, zero], axis=0))
    return jnp.concatenate([a, a, b, a, c, b], axis=0), jnp.concatenate([d, e, d, f, d, e], axis=0)


def quarter_kernel(sources, targets):
    squared = jnp.maximum(jnp.dot(sources, targets, preferred_element_type=F32), TINY)
    inside = jnp.maximum(1.0 - squared * lax.rsqrt(squared), 0.0)
    square_in = inside * inside
    return square_in * square_in * (1.25 - inside)


def local_points(raw, origin):
    x = (raw[0:2] - 0.5) * (1.0 / SUPPORT)
    return jnp.concatenate([x, (raw[2:3] - origin) * (1.0 / SUPPORT)], axis=0)


def rank_of(values):
    count = values.shape[1]
    column = jnp.broadcast_to(values, (8, count)).T[:, 0:1]
    result = []
    for tile in range(count // CHUNK):
        mine = values[:, tile * CHUNK : (tile + 1) * CHUNK]
        total = jnp.zeros((8, CHUNK), F32)
        for chunk in range(count // CHUNK):
            other = column[chunk * CHUNK : (chunk + 1) * CHUNK]
            if chunk < tile:
                before = other <= mine
            elif chunk > tile:
                before = other < mine
            else:
                above = lax.broadcasted_iota(jnp.int32, (CHUNK, CHUNK), 0) < lax.broadcasted_iota(
                    jnp.int32, (CHUNK, CHUNK), 1
                )
                before = jnp.logical_or(other < mine, jnp.logical_and(other == mine, above))
            ones = jnp.where(before, 1.0, 0.0)
            for group in range(CHUNK // 8):
                total = total + ones[group * 8 : group * 8 + 8]
        result.append(jnp.sum(total, axis=0, keepdims=True))
    return jnp.concatenate(result, axis=1)


def moved(values, table):
    rows = values.shape[0]
    stacked = jnp.concatenate(parts(values), axis=0).astype(BF16)
    both = lax.dot_general(
        stacked, table, (((1,), (1,)), ((), ())), preferred_element_type=F32
    )
    return (both[:rows] + both[rows : 2 * rows]) + both[2 * rows :]


def moved_back(values, table):
    both = jnp.dot(doubled(values), table, preferred_element_type=F32)
    return both[:3] + both[8:11]


def chunk_bounds(source_z, target_z, width, low_ref, high_ref):
    chunks = source_z.shape[1] // CHUNK
    tiles = target_z.shape[1] // width

    def edges(values, size, pieces):
        rows = jnp.concatenate([values[:, i * size : (i + 1) * size] for i in range(pieces)], axis=0)
        return jnp.min(rows, axis=1, keepdims=True), jnp.max(rows, axis=1, keepdims=True)

    source_low, source_high = edges(source_z, CHUNK, chunks)
    target_low, target_high = edges(target_z, width, tiles)
    index = lax.broadcasted_iota(jnp.int32, (chunks, 1), 0).astype(F32)
    for tile in range(tiles):
        near = jnp.logical_and(
            source_high >= target_low[tile : tile + 1] - (1.0 + MARGIN),
            source_low <= target_high[tile : tile + 1] + (1.0 + MARGIN),
        )
        low_ref[tile] = jnp.min(jnp.where(near, index, float(chunks))).astype(jnp.int32)
        high_ref[tile] = jnp.max(jnp.where(near, index + 1.0, 0.0)).astype(jnp.int32)


def order_kernel(base_ref, normal_ref, centre_ref, cell_ref, nodes_ref, out_ref, centre_table, nodes_out, node_table):
    def table_of(ref, rank):
        count = rank.shape[1]
        rows = 128
        for start in range(0, count, rows):
            row = lax.broadcasted_iota(jnp.int32, (rows, count), 0).astype(F32) + float(start)
            ref[start : start + rows] = jnp.where(row == rank, 1.0, 0.0).astype(BF16)

    count = centre_ref.shape[1]
    table_of(centre_table, rank_of(centre_ref[2:3]))
    values = jnp.concatenate(
        [
            base_ref[...],
            normal_ref[...],
            centre_ref[...],
            cell_ref[...].astype(F32),
            jnp.zeros((6, count), F32),
        ],
        axis=0,
    )
    out_ref[...] = moved(values, centre_table[...])
    table_of(node_table, rank_of(nodes_ref[2:3]))
    nodes = jnp.concatenate([nodes_ref[...], jnp.zeros((5, nodes_ref.shape[1]), F32)], axis=0)
    nodes_out[...] = moved(nodes, node_table[...])


def ordered(base_shift, normals, centres, wall_cell, near_nodes):
    count, slots = centres.shape[1], near_nodes.shape[1]
    return pl.pallas_call(
        order_kernel,
        out_shape=(
            jax.ShapeDtypeStruct((16, count), F32),
            jax.ShapeDtypeStruct((count, count), BF16),
            jax.ShapeDtypeStruct((8, slots), F32),
            jax.ShapeDtypeStruct((slots, slots), BF16),
        ),
        in_specs=[VMEM] * 5,
        out_specs=(VMEM,) * 4,
        compiler_params=pltpu.CompilerParams(vmem_limit_bytes=SMALL_LIMIT),
        cost_estimate=pl.CostEstimate(flops=ORDER_FLOPS, bytes_accessed=4_000_000, transcendentals=0),
        name="order",
    )(base_shift, normals, centres, wall_cell.reshape(1, -1), near_nodes)


def edge_kernel(even_last, q_ref, w_ref, target, sems):
    count, rows, _ = q_ref.shape

    def move(row):
        copies = []
        for index in range(count + 1):
            source = q_ref.at[index] if index < count else w_ref.at[0]
            copies.append(
                pltpu.make_async_copy(source.at[pl.ds(row, 1)], target.at[pl.ds(index, 1)], sems.at[index])
            )
        for copy in copies:
            copy.start()
        for copy in copies:
            copy.wait()

    core = lax.axis_index("core")

    @pl.when(core == 0)
    def _():
        move(rows - 1 if even_last else 0)

    @pl.when(core != 0)
    def _():
        move(0 if even_last else rows - 1)


def edge_rows(even_last, flow_state, flow_speed):
    count, _, plane = flow_state.shape
    return pl.pallas_call(
        functools.partial(edge_kernel, even_last),
        out_shape=jax.ShapeDtypeStruct((count + 1, plane), F32),
        in_specs=[HBM, HBM],
        out_specs=VMEM,
        scratch_shapes=[pltpu.SemaphoreType.DMA((count + 1,))],
        compiler_params=pltpu.CompilerParams(vmem_limit_bytes=SMALL_LIMIT),
        name="edge_rows",
    )(
        pltpu.with_memory_space_constraint(flow_state, pltpu.HBM),
        pltpu.with_memory_space_constraint(flow_speed, pltpu.HBM),
    )


RATE = 0.5 * FLUX_STEP
PRESSURE = 4


def picked(stacked, chosen, lane):
    high, middle, low = parts(stacked)
    pieces = jnp.concatenate([high, middle, low], axis=1).astype(BF16)
    both = lax.dot_general(pieces, chosen, (((0,), (0,)), ((), ())), preferred_element_type=F32)
    value = (both[:128] + both[128:256]) + both[256:]
    here = lax.broadcasted_iota(jnp.int32, value.shape, 0) == lane
    return jnp.sum(jnp.where(here, value, 0.0), axis=0, keepdims=True)


def stacked_lanes(values):
    return jnp.concatenate([values[:, i : i + 128] for i in range(0, values.shape[1], 128)], axis=0)


def inner_kernel(q_ref, w_ref, sorted_ref, new_hbm, low_ref, high_ref, out_ref, chosen_ref, new_ref, sems):
    count, rows, plane = q_ref.shape
    width = 512
    steps = plane // width
    row = lax.broadcasted_iota(jnp.int32, (rows, width), 0)

    def copy_of(step):
        lanes = pl.ds(pl.multiple_of(step * width, width), width)
        return pltpu.make_async_copy(new_ref.at[:, :, lanes], new_hbm.at[:, :, lanes], sems.at[step])

    def chunk(step, _):
        here = pl.multiple_of(step * width, 128)
        left = pl.multiple_of(lax.rem(here + plane - 128, plane), 128)
        right = pl.multiple_of(lax.rem(here + width, plane), 128)

        def cyclic(ref, index):
            values = ref[index, :, pl.ds(here, width)]
            wide = jnp.concatenate(
                [ref[index, :, pl.ds(left, 128)], values, ref[index, :, pl.ds(right, 128)]], axis=1
            )
            before = pltpu.roll(wide, 1, 1)[:, 128 : 128 + width]
            after = pltpu.roll(wide, width + 255, 1)[:, 128 : 128 + width]
            return values, before, after

        w = w_ref[0, :, pl.ds(here, width)]
        face_low = jnp.where(row == 0, 0.0, RATE * (pltpu.roll(w, 1, 0) + w))
        face_high = jnp.where(row == rows - 1, 0.0, RATE * (w + pltpu.roll(w, rows - 1, 0)))
        speed, speed_before, speed_after = cyclic(w_ref, 1)
        face_left = RATE * (speed_before + speed)
        face_right = RATE * (speed + speed_after)
        low_in = jnp.maximum(face_low, 0.0)
        high_out = jnp.minimum(face_high, 0.0)
        left_in = jnp.maximum(face_left, 0.0)
        right_out = jnp.minimum(face_right, 0.0)
        keep = 1.0 - (
            (jnp.maximum(face_high, 0.0) - jnp.minimum(face_low, 0.0))
            + (jnp.maximum(face_right, 0.0) - jnp.minimum(face_left, 0.0))
        )
        for index in range(count):
            values, before, after = cyclic(q_ref, index)
            new = (
                keep * values
                + low_in * pltpu.roll(values, 1, 0)
                - high_out * pltpu.roll(values, rows - 1, 0)
                + left_in * before
                - right_out * after
            )
            new_ref[index, :, pl.ds(here, width)] = new
            low_ref[index : index + 1, pl.ds(here, width)] = new[0:1]
            high_ref[index : index + 1, pl.ds(here, width)] = new[rows - 1 : rows]
        copy_of(step).start()
        return 0

    lax.fori_loop(0, steps, chunk, 0)

    cells = sorted_ref[9:10].astype(jnp.int32)
    cell_row = cells // plane
    column = cells - cell_row * plane
    group = column // 128
    lane = column - group * 128
    place = group * rows + cell_row
    centres = cells.shape[1]
    lanes = plane // 128
    chosen = (lax.broadcasted_iota(jnp.int32, (rows * lanes, centres), 0) == place).astype(F32).astype(BF16)
    chosen_ref[...] = chosen
    load = picked(stacked_lanes(new_ref[PRESSURE]), chosen, lane)
    out_ref[...] = jnp.concatenate(
        [
            sorted_ref[0:3] + sorted_ref[3:6] * load,
            sorted_ref[3:9],
            lane.astype(F32),
            jnp.zeros((6, centres), F32),
        ],
        axis=0,
    )
    for step in range(steps):
        copy_of(step).wait()


def inner_flux(flow_state, flow_speed, in_order):
    count, rows, plane = flow_state.shape
    centres = in_order.shape[1]
    edge = jax.ShapeDtypeStruct((count, plane), F32)
    return pl.pallas_call(
        inner_kernel,
        out_shape=(
            pltpu.HBM(flow_state.shape, F32),
            edge,
            edge,
            jax.ShapeDtypeStruct((16, centres), F32),
            jax.ShapeDtypeStruct((rows * plane // 128, centres), BF16),
        ),
        in_specs=[VMEM] * 3,
        out_specs=(HBM, VMEM, VMEM, VMEM, VMEM),
        scratch_shapes=[pltpu.VMEM(flow_state.shape, F32), pltpu.SemaphoreType.DMA((plane // 512,))],
        compiler_params=pltpu.CompilerParams(vmem_limit_bytes=SMALL_LIMIT),
        cost_estimate=pl.CostEstimate(flops=20_000_000, bytes_accessed=4_000_000, transcendentals=0),
        name="inner_flux",
    )(flow_state, flow_speed, in_order)


def outer_kernel(
    send_a, send_b, from_a, from_b, low_ref, high_ref, base_ref, chosen_ref, out_ref, new_low, new_high, both_ref
):
    count, plane = low_ref.shape
    rows = both_ref.shape[0]
    even = lax.axis_index("core") == 0
    own_low = jnp.where(even, send_b[...], send_a[...])
    own_high = jnp.where(even, send_a[...], send_b[...])
    below = jnp.where(even, from_b[...], from_a[...])
    above = jnp.where(even, from_a[...], from_b[...])

    def flux(first, second):
        face = RATE * (first[count : count + 1] + second[count : count + 1])
        return jnp.maximum(face, 0.0) * first[:count] + jnp.minimum(face, 0.0) * second[:count]

    low = flux(below, own_low)
    high = flux(own_high, above)
    new_low[...] = low_ref[...] + low
    new_high[...] = high_ref[...] - high
    row = lax.broadcasted_iota(jnp.int32, (rows, plane), 0)
    zero = jnp.zeros((rows, plane), F32)
    added = jnp.where(row == 0, low[PRESSURE : PRESSURE + 1], zero)
    added = added - jnp.where(row == rows - 1, high[PRESSURE : PRESSURE + 1], zero)
    both_ref[...] = added
    base = base_ref[...]
    load = picked(stacked_lanes(both_ref[...]), chosen_ref[...], base[9:10].astype(jnp.int32))
    centres = base.shape[1]
    packed = jnp.concatenate([base[0:3] + base[3:6] * load, base[6:9], jnp.zeros((2, centres), F32)], axis=0)
    for chip in range(out_ref.shape[0]):
        out_ref[chip] = packed


def right_side(chips, rows, send_a, send_b, from_a, from_b, low, high, base, chosen):
    edge = jax.ShapeDtypeStruct(low.shape, F32)
    return pl.pallas_call(
        outer_kernel,
        out_shape=(jax.ShapeDtypeStruct((chips, 8, base.shape[1]), F32), edge, edge),
        in_specs=[VMEM] * 8,
        out_specs=(VMEM,) * 3,
        scratch_shapes=[pltpu.VMEM((rows, low.shape[1]), F32)],
        compiler_params=pltpu.CompilerParams(vmem_limit_bytes=SMALL_LIMIT),
        name="outer_flux",
    )(send_a, send_b, from_a, from_b, low, high, base, chosen)


def block_of(mine_ref, other_ref, block, core):
    chip = lax.div(block, 2)
    own = lax.rem(block, 2) == core
    return jnp.where(own, mine_ref[chip], other_ref[chip])


def powers_kernel(
    count, mine_ref, other_ref, new_low, new_high, new_in, out_ref, new_out,
    source_side, target_side, vector, image, tables, low_ref, high_ref, sems,
):
    del new_in
    rows_per_block = new_out.shape[1]
    copies = [
        pltpu.make_async_copy(new_low, new_out.at[:, 0], sems.at[0]),
        pltpu.make_async_copy(new_high, new_out.at[:, rows_per_block - 1], sems.at[1]),
    ]
    for copy in copies:
        copy.start()
    size = mine_ref.shape[2]
    chip, core = lax.axis_index("chip"), lax.axis_index("core")
    me = chip * 2 + core
    slots, width, reach = 6, 256, 6
    span = reach * CHUNK
    total = slots * size
    origin = lax.div(me * 2, 5).astype(F32)
    value_row = lax.broadcasted_iota(jnp.int32, (8, size), 0) < 3

    live, zeroth, third = [], [], []
    for slot in range(slots):
        block = me + slot - 2
        valid = jnp.logical_and(block >= 0, block < count)
        live.append(valid)
        data = block_of(mine_ref, other_ref, jnp.clip(block, 0, count - 1), core)
        zeroth.append(jnp.where(jnp.logical_and(value_row, valid), data, 0.0))
        middle = (block.astype(F32) + 0.5) * DEPTH
        raw = jnp.concatenate([data[3:5], jnp.where(valid, data[5:6], middle)], axis=0)
        points = local_points(raw, origin)
        third.append(points[2:3])
        source, target = sides(points)
        source_side[slot * size : (slot + 1) * size] = source.T.astype(BF16)
        target_side[:, slot * size : (slot + 1) * size] = target.astype(BF16)
    far = (lax.broadcasted_iota(jnp.int32, (span, 48), 1) == 3).astype(F32) * 4096.0
    source_side[total:] = far.astype(BF16)
    vector[:, total:] = jnp.zeros((16, span), BF16)
    heights = jnp.concatenate(third, axis=1)
    chunk_bounds(heights, heights[:, size : 5 * size], width, low_ref, high_ref)
    tiles = 4 * size // width

    def steps_of(tile):
        return lax.div(high_ref[tile] - low_ref[tile] + (reach - 1), reach)

    most = steps_of(0)
    for tile in range(1, tiles):
        most = jnp.maximum(most, steps_of(tile))
    same = lax.broadcasted_iota(jnp.int32, (CHUNK, CHUNK), 0) == lax.broadcasted_iota(
        jnp.int32, (CHUNK, CHUNK), 1
    )

    def build(tile, step):
        lanes = pl.ds(pl.multiple_of(tile * width + size, width), width)
        chunk = low_ref[tile] + step * reach
        rows = pl.ds(pl.multiple_of(chunk * CHUNK, CHUNK), span)
        table = quarter_kernel(source_side[rows], target_side[:, lanes])
        high = table.astype(BF16)
        tables[tile, step, :span] = high
        tables[tile, step, span:] = (table - high.astype(F32)).astype(BF16)
        for piece in range(width // CHUNK):
            place = (tile * width + size) // CHUNK + piece - chunk
            inside = jnp.logical_and(place >= 0, place < reach)
            place = jnp.clip(place, 0, reach - 1)
            for half in range(2):
                at = pl.ds(pl.multiple_of(place * CHUNK + half * span, CHUNK), CHUNK)
                columns = slice(piece * CHUNK, (piece + 1) * CHUNK)
                old = tables[tile, step, at, columns]
                tables[tile, step, at, columns] = jnp.where(jnp.logical_and(same, inside), 0.0, old.astype(F32)).astype(BF16)

    def one(tile, step):
        lanes = pl.ds(pl.multiple_of((low_ref[tile] + step * reach) * CHUNK, CHUNK), span)
        window = vector[:, lanes]
        return jnp.dot(jnp.concatenate([window, window], axis=1), tables[tile, step], preferred_element_type=F32)

    def lanes_of(tile):
        return pl.ds(pl.multiple_of(tile * width, width), width)

    def further(first, last):
        @pl.when(most > 1)
        def _():
            def of_tile(tile, _):
                def add(step, _):
                    image[:, lanes_of(tile)] += one(tile, step)
                    return 0

                return lax.fori_loop(1, steps_of(tile), add, 0)

            lax.fori_loop(first, last, of_tile, 0)

    def image_of(slot):
        both = image[:, (slot - 1) * size : slot * size]
        return jnp.where(live[slot], 4.0 * (both[:8] + both[8:]), 0.0)

    def power(slots):
        first, last = (slots[0] - 1) * size // width, slots[-1] * size // width
        for tile in range(first, last):
            image[:, tile * width : (tile + 1) * width] = one(tile, 0)
        further(first, last)
        return {slot: image_of(slot) for slot in slots}

    def hold(values, slot):
        vector[:, slot * size : (slot + 1) * size] = doubled(values)

    for slot in range(slots):
        hold(zeroth[slot], slot)

    def tile_step(tile, _):
        before = jnp.maximum(tile - 1, 0)
        image[:, lanes_of(before)] = one(before, 0)
        build(tile, 0)
        return 0

    lax.fori_loop(0, tiles, tile_step, 0)
    image[:, (tiles - 1) * width : tiles * width] = one(tiles - 1, 0)

    @pl.when(most > 1)
    def _():
        def of_tile(tile, _):
            def more(step, _):
                build(tile, step)
                return 0

            return lax.fori_loop(1, steps_of(tile), more, 0)

        lax.fori_loop(0, tiles, of_tile, 0)

    further(0, tiles)
    first = {slot: image_of(slot) for slot in range(1, 5)}
    for slot in range(1, 5):
        hold(first[slot], slot)
    second = power([2, 3])
    hold(jnp.zeros((8, size), F32), 1)
    hold(second[2], 2)
    hold(2.0 * second[3], 3)
    last = power([2])[2]

    def inner(left, right):
        return jnp.sum(left * right, axis=1, keepdims=True)

    moments = [
        inner(zeroth[2], zeroth[2]),
        inner(zeroth[2], first[2]),
        inner(first[2], first[2]),
        inner(first[2], second[2]),
        inner(second[2], second[2]),
        inner(second[2], last),
    ]
    lane = lax.broadcasted_iota(jnp.int32, (8, 128), 1)
    packed = jnp.zeros((8, 128), F32)
    for index, moment in enumerate(moments):
        packed = jnp.where(lane == index, moment, packed)
    values = jnp.concatenate([first[2][:3], second[2][:3], jnp.zeros((2, size), F32)], axis=0)
    for index in range(out_ref.shape[0]):
        out_ref[index, :, :size] = values
        out_ref[index, :, size:] = packed
    for copy in copies:
        copy.wait()


def powers(mine, other, new_low, new_high, new_flow, count):
    chips, _, size = mine.shape
    tiles = 4 * size // 256
    steps = (6 * size // CHUNK + 5) // 6
    return pl.pallas_call(
        functools.partial(powers_kernel, count),
        out_shape=(
            jax.ShapeDtypeStruct((chips, 8, size + 128), F32),
            pltpu.HBM(new_flow.shape, F32),
        ),
        in_specs=[VMEM] * 4 + [HBM],
        out_specs=(VMEM, HBM),
        scratch_shapes=[
            pltpu.VMEM((6 * size + 6 * CHUNK, 48), BF16),
            pltpu.VMEM((48, 6 * size), BF16),
            pltpu.VMEM((16, 6 * size + 6 * CHUNK), BF16),
            pltpu.VMEM((16, 4 * size), F32),
            pltpu.VMEM((tiles, steps, 12 * CHUNK, 256), BF16),
            pltpu.SMEM((tiles,), jnp.int32),
            pltpu.SMEM((tiles,), jnp.int32),
            pltpu.SemaphoreType.DMA((2,)),
        ],
        input_output_aliases={4: 1},
        compiler_params=pltpu.CompilerParams(vmem_limit_bytes=BIG_LIMIT),
        name="powers",
    )(mine, other, new_low, new_high, pltpu.with_memory_space_constraint(new_flow, pltpu.HBM))


def ratio(top, bottom):
    safe = bottom > 0.0
    return jnp.where(safe, top / jnp.where(safe, bottom, 1.0), 0.0)


def weights_of(moments):
    lost = jnp.zeros_like(moments[0])

    def inner(left, right):
        total = size = None
        for i, a in enumerate(left):
            for j, c in enumerate(right):
                term = a * c * moments[i + j]
                total = term if total is None else total + term
                size = jnp.abs(term) if size is None else size + jnp.abs(term)
        return total, jnp.where(total > LOSS * size, 0.0, jnp.where(size > 0.0, 1.0, 0.0))

    one = jnp.ones_like(moments[0])
    residual, search = [one], [one]
    coefficients = [0.0 * one] * ITERS
    energy = moments[0]
    for step in range(ITERS):
        image = [CENTRE_SHIFT * value for value in search] + [0.0 * one]
        for index, value in enumerate(search):
            image[index + 1] = image[index + 1] + value
        along, bad = inner(search, image)
        lost = lost + bad
        length = ratio(energy, along)
        for index, value in enumerate(search):
            coefficients[index] = coefficients[index] + length * value
        if step == ITERS - 1:
            break
        longer = residual + [0.0 * one]
        residual = [value - length * other for value, other in zip(longer, image)]
        fresh, bad = inner(residual, residual)
        lost = lost + bad
        scale = ratio(fresh, energy)
        search = [
            value + scale * (search[index] if index < len(search) else 0.0)
            for index, value in enumerate(residual)
        ]
        energy = fresh
    return coefficients, lost


REACH = 7


def bounds_of(source_z, target_z):
    chunks = source_z.shape[1] // CHUNK
    tiles = target_z.shape[1] // CHUNK

    def edges(values, pieces):
        rows = jnp.concatenate([values[:, i * CHUNK : (i + 1) * CHUNK] for i in range(pieces)], axis=0)
        return jnp.min(rows, axis=1, keepdims=True), jnp.max(rows, axis=1, keepdims=True)

    def across(values):
        return jnp.broadcast_to(values, (tiles, 128)).T[0:1]

    source_low, source_high = edges(source_z, chunks)
    target_low, target_high = edges(target_z, tiles)
    near = jnp.logical_and(
        source_high >= across(target_low) - (1.0 + MARGIN), source_low <= across(target_high) + (1.0 + MARGIN)
    )
    index = lax.broadcasted_iota(jnp.int32, (chunks, tiles), 0).astype(F32)
    low = jnp.min(jnp.where(near, index, float(chunks)), axis=0, keepdims=True)
    high = jnp.max(jnp.where(near, index + 1.0, 0.0), axis=0, keepdims=True)
    return jnp.concatenate([low, high], axis=0)


def first_listed(tile_ref, me):
    return tile_ref[pl.ds(me, 1), :][0, 0]


def points_kernel(tile_ref, mine_ref, other_ref, nodes_ref, source_ref, target_ref, bound_ref):
    size = mine_ref.shape[2]
    core = lax.axis_index("core")
    me = lax.axis_index("chip") * 2 + core
    listed = tile_ref.shape[1]
    start = first_listed(tile_ref, me)
    origin = lax.div((start + 2) * 2, 5).astype(F32)
    third = []
    for index in range(listed):
        data = block_of(mine_ref, other_ref, start + index, core)
        points = local_points(data[3:6], origin)
        third.append(points[2:3])
        source, _ = sides(points)
        source_ref[index * size : (index + 1) * size] = source.T.astype(BF16)
    span = REACH * CHUNK
    far = (lax.broadcasted_iota(jnp.int32, (span, 48), 1) == 3).astype(F32) * 4096.0
    source_ref[listed * size :] = far.astype(BF16)
    points = local_points(nodes_ref[0:3], origin)
    _, target = sides(points)
    target_ref[...] = target.astype(BF16)
    bound_ref[...] = bounds_of(jnp.concatenate(third, axis=1), points[2:3])


def near_points(tile_blocks, mine, other, nodes):
    size = mine.shape[2]
    slots = nodes.shape[1]
    listed = tile_blocks.shape[1]
    return pl.pallas_call(
        points_kernel,
        out_shape=(
            jax.ShapeDtypeStruct((listed * size + REACH * CHUNK, 48), BF16),
            jax.ShapeDtypeStruct((48, slots), BF16),
            jax.ShapeDtypeStruct((2, slots // CHUNK), F32),
        ),
        in_specs=[VMEM] * 4,
        out_specs=(VMEM,) * 3,
        compiler_params=pltpu.CompilerParams(vmem_limit_bytes=SMALL_LIMIT),
        cost_estimate=pl.CostEstimate(flops=1_000_000, bytes_accessed=1_000_000, transcendentals=0),
        name="near_points",
    )(tile_blocks, mine, other, nodes)


def near_kernel(
    tile_ref, count_ref, bound_ref, mine_ref, other_ref, mine_power, other_power, source_side, target_side,
    centre_table, node_table, coef_ref, shift_ref, lost_ref, vector, result, low_ref, step_ref,
):
    size = mine_ref.shape[2]
    slots = target_side.shape[1]
    chips = mine_ref.shape[0]
    core = lax.axis_index("core")
    me = lax.axis_index("chip") * 2 + core
    listed = tile_ref.shape[1]
    start_block = first_listed(tile_ref, me)
    width = CHUNK
    tiles = slots // width
    span = REACH * CHUNK
    total = listed * size

    bounds = bound_ref[...].astype(jnp.int32)
    most = 0
    for tile in range(tiles):
        low = bounds[0, tile]
        steps = lax.div(bounds[1, tile] - low + (REACH - 1), REACH)
        low_ref[tile] = low
        step_ref[tile] = steps
        most = jnp.maximum(most, steps)

    summed = mine_power[0, :, size:] + other_power[0, :, size:]
    for index in range(1, chips):
        summed = summed + (mine_power[index, :, size:] + other_power[index, :, size:])
    weights, lost = weights_of([summed[:, index : index + 1] for index in range(6)])
    lost_ref[...] = jnp.broadcast_to(jnp.max(lost[:3], axis=0, keepdims=True), (1, 128))

    def coefficients_of(block):
        data = block_of(mine_ref, other_ref, block, core)
        power = block_of(mine_power, other_power, block, core)[:, :size]
        values = weights[0] * data + weights[1] * power + weights[2] * pltpu.roll(power, 5, 0)
        keep = lax.broadcasted_iota(jnp.int32, (8, size), 0) < 3
        return jnp.where(keep, values, 0.0)

    for index in range(listed):
        vector[:, index * size : (index + 1) * size] = doubled(coefficients_of(start_block + index))
    vector[:, total:] = jnp.zeros((16, span), BF16)
    coef_ref[...] = moved_back(coefficients_of(me), centre_table[...])

    def lanes_of(tile):
        return pl.ds(pl.multiple_of(tile * width, width), width)

    def one(tile, step):
        start = pl.multiple_of((low_ref[tile] + step * REACH) * CHUNK, CHUNK)
        table = quarter_kernel(source_side[pl.ds(start, span)], target_side[:, lanes_of(tile)])
        window = vector[:, pl.ds(start, span)]
        return jnp.dot(jnp.concatenate([window, window], axis=1), doubled(table), preferred_element_type=F32)

    def two_tiles(step, _):
        for piece in range(2):
            result[:, lanes_of(2 * step + piece)] = one(2 * step + piece, 0)
        return 0

    lax.fori_loop(0, tiles // 2, two_tiles, 0)

    @pl.when(most > 1)
    def _():
        def of_tile(tile, _):
            def add(step, _):
                result[:, lanes_of(tile)] += one(tile, step)
                return 0

            return lax.fori_loop(1, step_ref[tile], add, 0)

        lax.fori_loop(0, tiles, of_tile, 0)

    lane = lax.broadcasted_iota(jnp.int32, count_ref.shape, 1)
    live = jnp.sum(jnp.where(lane == me, count_ref[...], 0).astype(F32), axis=1, keepdims=True)
    slot = lax.broadcasted_iota(jnp.int32, (3, slots), 1).astype(F32)
    both = result[...]
    shift = moved_back(4.0 * (both[:8] + both[8:]), node_table[...])
    shift_ref[...] = jnp.where(slot < live, shift, 0.0)


def near_body(tile_blocks, near_count, bounds, mine, other, mine_power, other_power, sources, targets, centre_table, node_table):
    size = mine.shape[2]
    slots = targets.shape[1]
    total = tile_blocks.shape[1] * size
    return pl.pallas_call(
        near_kernel,
        out_shape=(
            jax.ShapeDtypeStruct((3, size), F32),
            jax.ShapeDtypeStruct((3, slots), F32),
            jax.ShapeDtypeStruct((1, 128), F32),
        ),
        in_specs=[VMEM] * 11,
        out_specs=(VMEM,) * 3,
        scratch_shapes=[
            pltpu.VMEM((16, total + REACH * CHUNK), BF16),
            pltpu.VMEM((16, slots), F32),
            pltpu.SMEM((slots // CHUNK,), jnp.int32),
            pltpu.SMEM((slots // CHUNK,), jnp.int32),
        ],
        compiler_params=pltpu.CompilerParams(vmem_limit_bytes=SMALL_LIMIT),
        name="near_body",
    )(
        tile_blocks, near_count.reshape(1, -1), bounds, mine, other, mine_power, other_power, sources, targets,
        centre_table, node_table,
    )


def gathered(values, partner):
    mine = lax.all_to_all(values, "chip", 0, 0)
    return mine, lax.ppermute(mine, SLAB, partner)


def step_by_step(count, right, centres, tile_blocks, near_count, near_nodes):
    size = centres.shape[1]
    up = [(i, i + 1) for i in range(count - 1)]
    down = [(i + 1, i) for i in range(count - 1)]

    def widened(values):
        return jnp.concatenate([lax.ppermute(values, SLAB, up), values, lax.ppermute(values, SLAB, down)], axis=1)

    def table_of(sources, targets):
        scaled = jnp.sqrt(sum((sources[k][:, None] - targets[k][None, :]) ** 2 for k in range(3))) / SUPPORT
        inside = jnp.maximum(1.0 - scaled, 0.0)
        square_in = inside * inside
        return square_in * square_in * (4.0 * scaled + 1.0)

    def total(left, other):
        return lax.psum(jnp.sum(left * other, axis=1), SLAB)

    def product(values, table):
        return jnp.dot(values, table, precision=lax.Precision.HIGHEST, preferred_element_type=F32)

    around = widened(centres)

    def step(_, held):
        coefficients, residual, search, energy = held
        image = product(widened(search), table_of(around, centres)) + DIAG_SHIFT * search
        length = energy / total(search, image)
        coefficients = coefficients + length[:, None] * search
        residual = residual - length[:, None] * image
        fresh = total(residual, residual)
        return coefficients, residual, residual + (fresh / energy)[:, None] * search, fresh

    coefficients = lax.fori_loop(0, ITERS, step, (jnp.zeros_like(right), right, right, total(right, right)))[0]
    everywhere = lax.all_gather(jnp.concatenate([centres, coefficients], axis=0), SLAB, axis=1, tiled=True)
    me = lax.axis_index(SLAB)
    slots = near_nodes.shape[1]

    def listed(index, sums):
        data = lax.dynamic_slice_in_dim(everywhere, tile_blocks[me, index] * size, size, 1)
        return sums + product(data[3:], table_of(data[:3], near_nodes))

    shift = lax.fori_loop(0, tile_blocks.shape[1], listed, jnp.zeros((3, slots), F32))
    live = lax.iota(jnp.int32, slots) < near_count[me]
    return coefficients, jnp.where(live[None, :], shift, 0.0)


def shards(
    count,
    flow_state,
    flow_speed,
    wall_cell,
    base_shift,
    normals,
    centres,
    tile_blocks,
    near_count,
    near_nodes,
):
    partner = [(i, i ^ 1) for i in range(count)]
    across = [(i, i + 1) for i in range(1, count - 1, 2)]
    across = across + [(j, i) for i, j in across]
    chips, rows = count // 2, flow_state.shape[1]
    send_b = edge_rows(False, flow_state, flow_speed)
    from_b = lax.ppermute(send_b, SLAB, across)
    send_a = edge_rows(True, flow_state, flow_speed)
    from_a = lax.ppermute(send_a, SLAB, partner)
    in_order, centre_table, nodes, node_table = ordered(base_shift, normals, centres, wall_cell, near_nodes)
    new_flow, low, high, base, chosen = inner_flux(flow_state, flow_speed, in_order)
    packed, low, high = right_side(chips, rows, send_a, send_b, from_a, from_b, low, high, base, chosen)
    mine, other = gathered(packed, partner)
    power, new_flow = powers(mine, other, low, high, new_flow, count)
    mine_power, other_power = gathered(power, partner)
    sources, targets, bounds = near_points(tile_blocks, mine, other, nodes)
    coefficients, node_shift, lost = near_body(
        tile_blocks, near_count, bounds, mine, other, mine_power, other_power, sources, targets,
        centre_table, node_table,
    )

    def again(held):
        one = jnp.where(held[0][0, 0] > 0.0, 1.0, 0.0)
        whole = one.astype(jnp.int32)
        own = packed[0] * one
        found, shifted = step_by_step(
            count, own[0:3], own[3:6], tile_blocks * whole, near_count * whole, near_nodes * one
        )
        back = jnp.dot(found, centre_table.astype(F32) * one, precision=lax.Precision.HIGHEST)
        return jnp.zeros_like(held[0]), back, shifted

    _, coefficients, node_shift = lax.while_loop(
        lambda held: held[0][0, 0] > 0.0, again, (lost, coefficients, node_shift)
    )
    return new_flow, coefficients, node_shift


def solution(mesh):
    groups, count = mesh.shape["groups"], mesh.shape["slab"]
    split = Mesh(mesh.devices.reshape(groups, count // 2, 2), ("groups",) + SLAB)
    in_specs = (
        P("groups", SLAB, None),
        P("groups", SLAB, None),
        P(("groups",) + SLAB),
        P("groups", SLAB),
        P("groups", SLAB),
        P("groups", SLAB),
        P("groups", None),
        P("groups"),
        P("groups", SLAB),
    )
    out_specs = (P("groups", SLAB, None), P("groups", SLAB), P("groups", SLAB))
    return jax.shard_map(
        functools.partial(shards, count), mesh=split, in_specs=in_specs, out_specs=out_specs, check_vma=False
    )
```

```python
import functools

import jax
import jax.numpy as jnp
from jax import lax
from jax.experimental import pallas as pl
from jax.experimental.pallas import tpu as pltpu
from jax.sharding import Mesh
from jax.sharding import PartitionSpec as P


FLUX_STEP = 0.2
SUPPORT = 0.15
DIAG_SHIFT = 0.5
CENTRE_SHIFT = DIAG_SHIFT + 1.0
TINY = 1e-12
ITERS = 3
LOSS = 0.01
DEPTH = 0.4
CHUNK = 128
MARGIN = 1e-3
ORDER_FLOPS = 2_000_000_000
BIG_LIMIT = 48 * 1024 * 1024
SMALL_LIMIT = 16 * 1024 * 1024

F32 = jnp.float32
BF16 = jnp.bfloat16
SLAB = ("chip", "core")
VMEM = pl.BlockSpec(memory_space=pltpu.VMEM)
SMEM = pl.BlockSpec(memory_space=pltpu.SMEM)
HBM = pl.BlockSpec(memory_space=pltpu.HBM)


def parts(values):
    first = values.astype(BF16).astype(F32)
    rest = values - first
    second = rest.astype(BF16).astype(F32)
    return first, second, rest - second


def doubled(values):
    high = values.astype(BF16)
    return jnp.concatenate([high, (values - high.astype(F32)).astype(BF16)], axis=0)


def sides(points):
    count = points.shape[1]
    squares = jnp.sum(points * points, axis=0, keepdims=True)
    one = jnp.ones((1, count), F32)
    zero = jnp.zeros((3, count), F32)
    a, b, c = parts(jnp.concatenate([points, squares, one, zero], axis=0))
    d, e, f = parts(jnp.concatenate([-2.0 * points, one, squares, zero], axis=0))
    return jnp.concatenate([a, a, b, a, c, b], axis=0), jnp.concatenate([d, e, d, f, d, e], axis=0)


def quarter_kernel(sources, targets):
    squared = jnp.maximum(jnp.dot(sources, targets, preferred_element_type=F32), TINY)
    inside = jnp.maximum(1.0 - squared * lax.rsqrt(squared), 0.0)
    square_in = inside * inside
    return square_in * square_in * (1.25 - inside)


def local_points(raw, origin):
    x = (raw[0:2] - 0.5) * (1.0 / SUPPORT)
    return jnp.concatenate([x, (raw[2:3] - origin) * (1.0 / SUPPORT)], axis=0)


def rank_of(values):
    count = values.shape[1]
    column = jnp.broadcast_to(values, (8, count)).T[:, 0:1]
    result = []
    for tile in range(count // CHUNK):
        mine = values[:, tile * CHUNK : (tile + 1) * CHUNK]
        total = jnp.zeros((8, CHUNK), F32)
        for chunk in range(count // CHUNK):
            other = column[chunk * CHUNK : (chunk + 1) * CHUNK]
            if chunk < tile:
                before = other <= mine
            elif chunk > tile:
                before = other < mine
            else:
                above = lax.broadcasted_iota(jnp.int32, (CHUNK, CHUNK), 0) < lax.broadcasted_iota(
                    jnp.int32, (CHUNK, CHUNK), 1
                )
                before = jnp.logical_or(other < mine, jnp.logical_and(other == mine, above))
            ones = jnp.where(before, 1.0, 0.0)
            for group in range(CHUNK // 8):
                total = total + ones[group * 8 : group * 8 + 8]
        result.append(jnp.sum(total, axis=0, keepdims=True))
    return jnp.concatenate(result, axis=1)


def moved(values, table):
    rows = values.shape[0]
    stacked = jnp.concatenate(parts(values), axis=0).astype(BF16)
    both = lax.dot_general(
        stacked, table, (((1,), (1,)), ((), ())), preferred_element_type=F32
    )
    return (both[:rows] + both[rows : 2 * rows]) + both[2 * rows :]


def moved_back(values, table):
    both = jnp.dot(doubled(values), table, preferred_element_type=F32)
    return both[:3] + both[8:11]


def chunk_bounds(source_z, target_z, width, low_ref, high_ref):
    chunks = source_z.shape[1] // CHUNK
    tiles = target_z.shape[1] // width

    def edges(values, size, pieces):
        rows = jnp.concatenate([values[:, i * size : (i + 1) * size] for i in range(pieces)], axis=0)
        return jnp.min(rows, axis=1, keepdims=True), jnp.max(rows, axis=1, keepdims=True)

    source_low, source_high = edges(source_z, CHUNK, chunks)
    target_low, target_high = edges(target_z, width, tiles)
    index = lax.broadcasted_iota(jnp.int32, (chunks, 1), 0).astype(F32)
    for tile in range(tiles):
        near = jnp.logical_and(
            source_high >= target_low[tile : tile + 1] - (1.0 + MARGIN),
            source_low <= target_high[tile : tile + 1] + (1.0 + MARGIN),
        )
        low_ref[tile] = jnp.min(jnp.where(near, index, float(chunks))).astype(jnp.int32)
        high_ref[tile] = jnp.max(jnp.where(near, index + 1.0, 0.0)).astype(jnp.int32)


def order_kernel(base_ref, normal_ref, centre_ref, cell_ref, nodes_ref, out_ref, centre_hbm, nodes_out, node_hbm, centre_table, node_table, sems):
    copies = []

    def table_of(ref, target, rank):
        count = rank.shape[1]
        rows = 128
        for start in range(0, count, rows):
            row = lax.broadcasted_iota(jnp.int32, (rows, count), 0).astype(F32) + float(start)
            ref[start : start + rows] = jnp.where(row == rank, 1.0, 0.0).astype(BF16)
            piece = pl.ds(start, rows)
            copies.append(pltpu.make_async_copy(ref.at[piece], target.at[piece], sems.at[len(copies)]))
            copies[-1].start()

    count = centre_ref.shape[1]
    table_of(centre_table, centre_hbm, rank_of(centre_ref[2:3]))
    values = jnp.concatenate(
        [
            base_ref[...],
            normal_ref[...],
            centre_ref[...],
            cell_ref[...].astype(F32),
            jnp.zeros((6, count), F32),
        ],
        axis=0,
    )
    out_ref[...] = moved(values, centre_table[...])
    table_of(node_table, node_hbm, rank_of(nodes_ref[2:3]))
    nodes = jnp.concatenate([nodes_ref[...], jnp.zeros((5, nodes_ref.shape[1]), F32)], axis=0)
    nodes_out[...] = moved(nodes, node_table[...])
    for copy in copies:
        copy.wait()


def ordered(base_shift, normals, centres, wall_cell, near_nodes):
    count, slots = centres.shape[1], near_nodes.shape[1]
    return pl.pallas_call(
        order_kernel,
        out_shape=(
            jax.ShapeDtypeStruct((16, count), F32),
            pltpu.HBM((count, count), BF16),
            jax.ShapeDtypeStruct((8, slots), F32),
            pltpu.HBM((slots, slots), BF16),
        ),
        in_specs=[VMEM] * 5,
        out_specs=(VMEM, HBM, VMEM, HBM),
        scratch_shapes=[
            pltpu.VMEM((count, count), BF16),
            pltpu.VMEM((slots, slots), BF16),
            pltpu.SemaphoreType.DMA(((count + slots) // 128,)),
        ],
        compiler_params=pltpu.CompilerParams(vmem_limit_bytes=SMALL_LIMIT),
        cost_estimate=pl.CostEstimate(flops=ORDER_FLOPS, bytes_accessed=4_000_000, transcendentals=0),
        name="order",
    )(base_shift, normals, centres, wall_cell.reshape(1, -1), near_nodes)


def edge_kernel(even_last, q_ref, w_ref, target, sems):
    count, rows, _ = q_ref.shape

    def move(row):
        copies = []
        for index in range(count + 1):
            source = q_ref.at[index] if index < count else w_ref.at[0]
            copies.append(
                pltpu.make_async_copy(source.at[pl.ds(row, 1)], target.at[pl.ds(index, 1)], sems.at[index])
            )
        for copy in copies:
            copy.start()
        for copy in copies:
            copy.wait()

    core = lax.axis_index("core")

    @pl.when(core == 0)
    def _():
        move(rows - 1 if even_last else 0)

    @pl.when(core != 0)
    def _():
        move(0 if even_last else rows - 1)


def edge_rows(even_last, flow_state, flow_speed):
    count, _, plane = flow_state.shape
    return pl.pallas_call(
        functools.partial(edge_kernel, even_last),
        out_shape=jax.ShapeDtypeStruct((count + 1, plane), F32),
        in_specs=[HBM, HBM],
        out_specs=VMEM,
        scratch_shapes=[pltpu.SemaphoreType.DMA((count + 1,))],
        compiler_params=pltpu.CompilerParams(vmem_limit_bytes=SMALL_LIMIT),
        name="edge_rows",
    )(
        pltpu.with_memory_space_constraint(flow_state, pltpu.HBM),
        pltpu.with_memory_space_constraint(flow_speed, pltpu.HBM),
    )


RATE = 0.5 * FLUX_STEP
PRESSURE = 4


def picked(stacked, chosen, lane):
    high, middle, low = parts(stacked)
    pieces = jnp.concatenate([high, middle, low], axis=1).astype(BF16)
    both = lax.dot_general(pieces, chosen, (((0,), (0,)), ((), ())), preferred_element_type=F32)
    value = (both[:128] + both[128:256]) + both[256:]
    here = lax.broadcasted_iota(jnp.int32, value.shape, 0) == lane
    return jnp.sum(jnp.where(here, value, 0.0), axis=0, keepdims=True)


def stacked_lanes(values):
    return jnp.concatenate([values[:, i : i + 128] for i in range(0, values.shape[1], 128)], axis=0)


def inner_kernel(q_ref, w_ref, sorted_ref, new_hbm, low_ref, high_ref, out_ref, chosen_ref, new_ref, sems):
    count, rows, plane = q_ref.shape
    width = 512
    steps = plane // width
    row = lax.broadcasted_iota(jnp.int32, (rows, width), 0)

    def copy_of(step):
        lanes = pl.ds(pl.multiple_of(step * width, width), width)
        return pltpu.make_async_copy(new_ref.at[:, :, lanes], new_hbm.at[:, :, lanes], sems.at[step])

    def chunk(step, _):
        here = pl.multiple_of(step * width, 128)
        left = pl.multiple_of(lax.rem(here + plane - 128, plane), 128)
        right = pl.multiple_of(lax.rem(here + width, plane), 128)

        def cyclic(ref, index):
            values = ref[index, :, pl.ds(here, width)]
            wide = jnp.concatenate(
                [ref[index, :, pl.ds(left, 128)], values, ref[index, :, pl.ds(right, 128)]], axis=1
            )
            before = pltpu.roll(wide, 1, 1)[:, 128 : 128 + width]
            after = pltpu.roll(wide, width + 255, 1)[:, 128 : 128 + width]
            return values, before, after

        w = w_ref[0, :, pl.ds(here, width)]
        face_low = jnp.where(row == 0, 0.0, RATE * (pltpu.roll(w, 1, 0) + w))
        face_high = jnp.where(row == rows - 1, 0.0, RATE * (w + pltpu.roll(w, rows - 1, 0)))
        speed, speed_before, speed_after = cyclic(w_ref, 1)
        face_left = RATE * (speed_before + speed)
        face_right = RATE * (speed + speed_after)
        low_in = jnp.maximum(face_low, 0.0)
        high_out = jnp.minimum(face_high, 0.0)
        left_in = jnp.maximum(face_left, 0.0)
        right_out = jnp.minimum(face_right, 0.0)
        keep = 1.0 - (
            (jnp.maximum(face_high, 0.0) - jnp.minimum(face_low, 0.0))
            + (jnp.maximum(face_right, 0.0) - jnp.minimum(face_left, 0.0))
        )
        for index in range(count):
            values, before, after = cyclic(q_ref, index)
            new = (
                keep * values
                + low_in * pltpu.roll(values, 1, 0)
                - high_out * pltpu.roll(values, rows - 1, 0)
                + left_in * before
                - right_out * after
            )
            new_ref[index, :, pl.ds(here, width)] = new
            low_ref[index : index + 1, pl.ds(here, width)] = new[0:1]
            high_ref[index : index + 1, pl.ds(here, width)] = new[rows - 1 : rows]
        copy_of(step).start()
        return 0

    lax.fori_loop(0, steps, chunk, 0)

    cells = sorted_ref[9:10].astype(jnp.int32)
    cell_row = cells // plane
    column = cells - cell_row * plane
    group = column // 128
    lane = column - group * 128
    place = group * rows + cell_row
    centres = cells.shape[1]
    lanes = plane // 128
    chosen = (lax.broadcasted_iota(jnp.int32, (rows * lanes, centres), 0) == place).astype(F32).astype(BF16)
    chosen_ref[...] = chosen
    load = picked(stacked_lanes(new_ref[PRESSURE]), chosen, lane)
    out_ref[...] = jnp.concatenate(
        [
            sorted_ref[0:3] + sorted_ref[3:6] * load,
            sorted_ref[3:9],
            lane.astype(F32),
            jnp.zeros((6, centres), F32),
        ],
        axis=0,
    )
    for step in range(steps):
        copy_of(step).wait()


def inner_flux(flow_state, flow_speed, in_order):
    count, rows, plane = flow_state.shape
    centres = in_order.shape[1]
    edge = jax.ShapeDtypeStruct((count, plane), F32)
    return pl.pallas_call(
        inner_kernel,
        out_shape=(
            pltpu.HBM(flow_state.shape, F32),
            edge,
            edge,
            jax.ShapeDtypeStruct((16, centres), F32),
            jax.ShapeDtypeStruct((rows * plane // 128, centres), BF16),
        ),
        in_specs=[VMEM] * 3,
        out_specs=(HBM, VMEM, VMEM, VMEM, VMEM),
        scratch_shapes=[pltpu.VMEM(flow_state.shape, F32), pltpu.SemaphoreType.DMA((plane // 512,))],
        compiler_params=pltpu.CompilerParams(vmem_limit_bytes=SMALL_LIMIT),
        cost_estimate=pl.CostEstimate(flops=20_000_000, bytes_accessed=4_000_000, transcendentals=0),
        name="inner_flux",
    )(flow_state, flow_speed, in_order)


def outer_kernel(
    send_a, send_b, from_a, from_b, low_ref, high_ref, base_ref, chosen_ref, out_ref, new_low, new_high, both_ref
):
    count, plane = low_ref.shape
    rows = both_ref.shape[0]
    even = lax.axis_index("core") == 0
    own_low = jnp.where(even, send_b[...], send_a[...])
    own_high = jnp.where(even, send_a[...], send_b[...])
    below = jnp.where(even, from_b[...], from_a[...])
    above = jnp.where(even, from_a[...], from_b[...])

    def flux(first, second):
        face = RATE * (first[count : count + 1] + second[count : count + 1])
        return jnp.maximum(face, 0.0) * first[:count] + jnp.minimum(face, 0.0) * second[:count]

    low = flux(below, own_low)
    high = flux(own_high, above)
    new_low[...] = low_ref[...] + low
    new_high[...] = high_ref[...] - high
    row = lax.broadcasted_iota(jnp.int32, (rows, plane), 0)
    zero = jnp.zeros((rows, plane), F32)
    added = jnp.where(row == 0, low[PRESSURE : PRESSURE + 1], zero)
    added = added - jnp.where(row == rows - 1, high[PRESSURE : PRESSURE + 1], zero)
    both_ref[...] = added
    base = base_ref[...]
    load = picked(stacked_lanes(both_ref[...]), chosen_ref[...], base[9:10].astype(jnp.int32))
    centres = base.shape[1]
    packed = jnp.concatenate([base[0:3] + base[3:6] * load, base[6:9], jnp.zeros((2, centres), F32)], axis=0)
    for chip in range(out_ref.shape[0]):
        out_ref[chip] = packed


def right_side(chips, rows, send_a, send_b, from_a, from_b, low, high, base, chosen):
    edge = jax.ShapeDtypeStruct(low.shape, F32)
    return pl.pallas_call(
        outer_kernel,
        out_shape=(jax.ShapeDtypeStruct((chips, 8, base.shape[1]), F32), edge, edge),
        in_specs=[VMEM] * 8,
        out_specs=(VMEM,) * 3,
        scratch_shapes=[pltpu.VMEM((rows, low.shape[1]), F32)],
        compiler_params=pltpu.CompilerParams(vmem_limit_bytes=SMALL_LIMIT),
        name="outer_flux",
    )(send_a, send_b, from_a, from_b, low, high, base, chosen)


def block_of(mine_ref, other_ref, block, core):
    chip = lax.div(block, 2)
    own = lax.rem(block, 2) == core
    return jnp.where(own, mine_ref[chip], other_ref[chip])


def powers_kernel(
    count, mine_ref, other_ref, new_low, new_high, new_in, out_ref, new_out,
    source_side, target_side, vector, image, tables, low_ref, high_ref, sems,
):
    del new_in
    rows_per_block = new_out.shape[1]
    copies = [
        pltpu.make_async_copy(new_low, new_out.at[:, 0], sems.at[0]),
        pltpu.make_async_copy(new_high, new_out.at[:, rows_per_block - 1], sems.at[1]),
    ]
    for copy in copies:
        copy.start()
    size = mine_ref.shape[2]
    chip, core = lax.axis_index("chip"), lax.axis_index("core")
    me = chip * 2 + core
    slots, width, reach = 6, 256, 6
    span = reach * CHUNK
    total = slots * size
    origin = lax.div(me * 2, 5).astype(F32)
    value_row = lax.broadcasted_iota(jnp.int32, (8, size), 0) < 3

    live, zeroth, third = [], [], []
    for slot in range(slots):
        block = me + slot - 2
        valid = jnp.logical_and(block >= 0, block < count)
        live.append(valid)
        data = block_of(mine_ref, other_ref, jnp.clip(block, 0, count - 1), core)
        zeroth.append(jnp.where(jnp.logical_and(value_row, valid), data, 0.0))
        middle = (block.astype(F32) + 0.5) * DEPTH
        raw = jnp.concatenate([data[3:5], jnp.where(valid, data[5:6], middle)], axis=0)
        points = local_points(raw, origin)
        third.append(points[2:3])
        source, target = sides(points)
        source_side[slot * size : (slot + 1) * size] = source.T.astype(BF16)
        target_side[:, slot * size : (slot + 1) * size] = target.astype(BF16)
    far = (lax.broadcasted_iota(jnp.int32, (span, 48), 1) == 3).astype(F32) * 4096.0
    source_side[total:] = far.astype(BF16)
    vector[:, total:] = jnp.zeros((16, span), BF16)
    heights = jnp.concatenate(third, axis=1)
    chunk_bounds(heights, heights[:, size : 5 * size], width, low_ref, high_ref)
    tiles = 4 * size // width

    def steps_of(tile):
        return lax.div(high_ref[tile] - low_ref[tile] + (reach - 1), reach)

    most = steps_of(0)
    for tile in range(1, tiles):
        most = jnp.maximum(most, steps_of(tile))
    same = lax.broadcasted_iota(jnp.int32, (CHUNK, CHUNK), 0) == lax.broadcasted_iota(
        jnp.int32, (CHUNK, CHUNK), 1
    )

    def build(tile, step):
        lanes = pl.ds(pl.multiple_of(tile * width + size, width), width)
        chunk = low_ref[tile] + step * reach
        rows = pl.ds(pl.multiple_of(chunk * CHUNK, CHUNK), span)
        table = quarter_kernel(source_side[rows], target_side[:, lanes])
        high = table.astype(BF16)
        tables[tile, step, :span] = high
        tables[tile, step, span:] = (table - high.astype(F32)).astype(BF16)
        for piece in range(width // CHUNK):
            place = (tile * width + size) // CHUNK + piece - chunk
            inside = jnp.logical_and(place >= 0, place < reach)
            place = jnp.clip(place, 0, reach - 1)
            for half in range(2):
                at = pl.ds(pl.multiple_of(place * CHUNK + half * span, CHUNK), CHUNK)
                columns = slice(piece * CHUNK, (piece + 1) * CHUNK)
                old = tables[tile, step, at, columns]
                tables[tile, step, at, columns] = jnp.where(jnp.logical_and(same, inside), 0.0, old.astype(F32)).astype(BF16)

    def one(tile, step):
        lanes = pl.ds(pl.multiple_of((low_ref[tile] + step * reach) * CHUNK, CHUNK), span)
        window = vector[:, lanes]
        return jnp.dot(jnp.concatenate([window, window], axis=1), tables[tile, step], preferred_element_type=F32)

    def lanes_of(tile):
        return pl.ds(pl.multiple_of(tile * width, width), width)

    def further(first, last):
        @pl.when(most > 1)
        def _():
            def of_tile(tile, _):
                def add(step, _):
                    image[:, lanes_of(tile)] += one(tile, step)
                    return 0

                return lax.fori_loop(1, steps_of(tile), add, 0)

            lax.fori_loop(first, last, of_tile, 0)

    def image_of(slot):
        both = image[:, (slot - 1) * size : slot * size]
        return jnp.where(live[slot], 4.0 * (both[:8] + both[8:]), 0.0)

    def power(slots):
        first, last = (slots[0] - 1) * size // width, slots[-1] * size // width
        for tile in range(first, last):
            image[:, tile * width : (tile + 1) * width] = one(tile, 0)
        further(first, last)
        return {slot: image_of(slot) for slot in slots}

    def hold(values, slot):
        vector[:, slot * size : (slot + 1) * size] = doubled(values)

    for slot in range(slots):
        hold(zeroth[slot], slot)

    def tile_step(tile, _):
        before = jnp.maximum(tile - 1, 0)
        image[:, lanes_of(before)] = one(before, 0)
        build(tile, 0)
        return 0

    lax.fori_loop(0, tiles, tile_step, 0)
    image[:, (tiles - 1) * width : tiles * width] = one(tiles - 1, 0)

    @pl.when(most > 1)
    def _():
        def of_tile(tile, _):
            def more(step, _):
                build(tile, step)
                return 0

            return lax.fori_loop(1, steps_of(tile), more, 0)

        lax.fori_loop(0, tiles, of_tile, 0)

    further(0, tiles)
    first = {slot: image_of(slot) for slot in range(1, 5)}
    for slot in range(1, 5):
        hold(first[slot], slot)
    second = power([2, 3])
    hold(jnp.zeros((8, size), F32), 1)
    hold(second[2], 2)
    hold(2.0 * second[3], 3)
    last = power([2])[2]

    def inner(left, right):
        return jnp.sum(left * right, axis=1, keepdims=True)

    moments = [
        inner(zeroth[2], zeroth[2]),
        inner(zeroth[2], first[2]),
        inner(first[2], first[2]),
        inner(first[2], second[2]),
        inner(second[2], second[2]),
        inner(second[2], last),
    ]
    lane = lax.broadcasted_iota(jnp.int32, (8, 128), 1)
    packed = jnp.zeros((8, 128), F32)
    for index, moment in enumerate(moments):
        packed = jnp.where(lane == index, moment, packed)
    values = jnp.concatenate([first[2][:3], second[2][:3], jnp.zeros((2, size), F32)], axis=0)
    for index in range(out_ref.shape[0]):
        out_ref[index, :, :size] = values
        out_ref[index, :, size:] = packed
    for copy in copies:
        copy.wait()


def powers(mine, other, new_low, new_high, new_flow, count):
    chips, _, size = mine.shape
    tiles = 4 * size // 256
    steps = (6 * size // CHUNK + 5) // 6
    return pl.pallas_call(
        functools.partial(powers_kernel, count),
        out_shape=(
            jax.ShapeDtypeStruct((chips, 8, size + 128), F32),
            pltpu.HBM(new_flow.shape, F32),
        ),
        in_specs=[VMEM] * 4 + [HBM],
        out_specs=(VMEM, HBM),
        scratch_shapes=[
            pltpu.VMEM((6 * size + 6 * CHUNK, 48), BF16),
            pltpu.VMEM((48, 6 * size), BF16),
            pltpu.VMEM((16, 6 * size + 6 * CHUNK), BF16),
            pltpu.VMEM((16, 4 * size), F32),
            pltpu.VMEM((tiles, steps, 12 * CHUNK, 256), BF16),
            pltpu.SMEM((tiles,), jnp.int32),
            pltpu.SMEM((tiles,), jnp.int32),
            pltpu.SemaphoreType.DMA((2,)),
        ],
        input_output_aliases={4: 1},
        compiler_params=pltpu.CompilerParams(vmem_limit_bytes=BIG_LIMIT),
        name="powers",
    )(mine, other, new_low, new_high, pltpu.with_memory_space_constraint(new_flow, pltpu.HBM))


def ratio(top, bottom):
    safe = bottom > 0.0
    return jnp.where(safe, top / jnp.where(safe, bottom, 1.0), 0.0)


def weights_of(moments):
    lost = jnp.zeros_like(moments[0])

    def inner(left, right):
        total = size = None
        for i, a in enumerate(left):
            for j, c in enumerate(right):
                term = a * c * moments[i + j]
                total = term if total is None else total + term
                size = jnp.abs(term) if size is None else size + jnp.abs(term)
        return total, jnp.where(total > LOSS * size, 0.0, jnp.where(size > 0.0, 1.0, 0.0))

    one = jnp.ones_like(moments[0])
    residual, search = [one], [one]
    coefficients = [0.0 * one] * ITERS
    energy = moments[0]
    for step in range(ITERS):
        image = [CENTRE_SHIFT * value for value in search] + [0.0 * one]
        for index, value in enumerate(search):
            image[index + 1] = image[index + 1] + value
        along, bad = inner(search, image)
        lost = lost + bad
        length = ratio(energy, along)
        for index, value in enumerate(search):
            coefficients[index] = coefficients[index] + length * value
        if step == ITERS - 1:
            break
        longer = residual + [0.0 * one]
        residual = [value - length * other for value, other in zip(longer, image)]
        fresh, bad = inner(residual, residual)
        lost = lost + bad
        scale = ratio(fresh, energy)
        search = [
            value + scale * (search[index] if index < len(search) else 0.0)
            for index, value in enumerate(residual)
        ]
        energy = fresh
    return coefficients, lost


REACH = 7


def bounds_of(source_z, target_z):
    chunks = source_z.shape[1] // CHUNK
    tiles = target_z.shape[1] // CHUNK

    def edges(values, pieces):
        rows = jnp.concatenate([values[:, i * CHUNK : (i + 1) * CHUNK] for i in range(pieces)], axis=0)
        return jnp.min(rows, axis=1, keepdims=True), jnp.max(rows, axis=1, keepdims=True)

    def across(values):
        return jnp.broadcast_to(values, (tiles, 128)).T[0:1]

    source_low, source_high = edges(source_z, chunks)
    target_low, target_high = edges(target_z, tiles)
    near = jnp.logical_and(
        source_high >= across(target_low) - (1.0 + MARGIN), source_low <= across(target_high) + (1.0 + MARGIN)
    )
    index = lax.broadcasted_iota(jnp.int32, (chunks, tiles), 0).astype(F32)
    low = jnp.min(jnp.where(near, index, float(chunks)), axis=0, keepdims=True)
    high = jnp.max(jnp.where(near, index + 1.0, 0.0), axis=0, keepdims=True)
    return jnp.concatenate([low, high], axis=0)


def first_listed(tile_ref, me):
    return tile_ref[pl.ds(me, 1), :][0, 0]


def scalars_of(bound_ref, low_ref, step_ref):
    bounds = bound_ref[...].astype(jnp.int32)
    most = 0
    for tile in range(bounds.shape[1]):
        low = bounds[0, tile]
        steps = lax.div(bounds[1, tile] - low + (REACH - 1), REACH)
        low_ref[tile] = low
        step_ref[tile] = steps
        most = jnp.maximum(most, steps)
    return most


def near_table(source_ref, target_ref, low_ref, tile, step):
    start = pl.multiple_of((low_ref[tile] + step * REACH) * CHUNK, CHUNK)
    lanes = pl.ds(pl.multiple_of(tile * CHUNK, CHUNK), CHUNK)
    return doubled(quarter_kernel(source_ref[pl.ds(start, REACH * CHUNK)], target_ref[:, lanes]))


def points_kernel(
    tile_ref, mine_ref, other_ref, nodes_ref, source_ref, target_ref, bound_ref, table_ref, low_ref, step_ref
):
    size = mine_ref.shape[2]
    core = lax.axis_index("core")
    me = lax.axis_index("chip") * 2 + core
    listed = tile_ref.shape[1]
    start = first_listed(tile_ref, me)
    origin = lax.div((start + 2) * 2, 5).astype(F32)
    third = []
    for index in range(listed):
        data = block_of(mine_ref, other_ref, start + index, core)
        points = local_points(data[3:6], origin)
        third.append(points[2:3])
        source, _ = sides(points)
        source_ref[index * size : (index + 1) * size] = source.T.astype(BF16)
    span = REACH * CHUNK
    far = (lax.broadcasted_iota(jnp.int32, (span, 48), 1) == 3).astype(F32) * 4096.0
    source_ref[listed * size :] = far.astype(BF16)
    points = local_points(nodes_ref[0:3], origin)
    _, target = sides(points)
    target_ref[...] = target.astype(BF16)
    bound_ref[...] = bounds_of(jnp.concatenate(third, axis=1), points[2:3])
    scalars_of(bound_ref, low_ref, step_ref)

    def two_tiles(step, _):
        for piece in range(2):
            tile = 2 * step + piece
            table_ref[tile] = near_table(source_ref, target_ref, low_ref, tile, 0)
        return 0

    lax.fori_loop(0, table_ref.shape[0] // 2, two_tiles, 0)


def near_points(tile_blocks, mine, other, nodes):
    size = mine.shape[2]
    slots = nodes.shape[1]
    listed = tile_blocks.shape[1]
    return pl.pallas_call(
        points_kernel,
        out_shape=(
            jax.ShapeDtypeStruct((listed * size + REACH * CHUNK, 48), BF16),
            jax.ShapeDtypeStruct((48, slots), BF16),
            jax.ShapeDtypeStruct((2, slots // CHUNK), F32),
            jax.ShapeDtypeStruct((slots // CHUNK // 2, 2 * REACH * CHUNK, CHUNK), BF16),
        ),
        in_specs=[VMEM] * 4,
        out_specs=(VMEM,) * 4,
        scratch_shapes=[
            pltpu.SMEM((slots // CHUNK,), jnp.int32),
            pltpu.SMEM((slots // CHUNK,), jnp.int32),
        ],
        compiler_params=pltpu.CompilerParams(vmem_limit_bytes=SMALL_LIMIT),
        cost_estimate=pl.CostEstimate(flops=1_000_000_000, bytes_accessed=4_000_000, transcendentals=0),
        name="near_points",
    )(tile_blocks, mine, other, nodes)


def near_kernel(
    tile_ref, count_ref, bound_ref, mine_ref, other_ref, mine_power, other_power, source_side, target_side,
    table_ref, centre_hbm, node_hbm, coef_ref, shift_ref, lost_ref,
    centre_table, node_table, vector, result, low_ref, step_ref, sems,
):
    copies = [
        pltpu.make_async_copy(centre_hbm, centre_table, sems.at[0]),
        pltpu.make_async_copy(node_hbm, node_table, sems.at[1]),
    ]
    for copy in copies:
        copy.start()
    size = mine_ref.shape[2]
    slots = target_side.shape[1]
    chips = mine_ref.shape[0]
    core = lax.axis_index("core")
    me = lax.axis_index("chip") * 2 + core
    listed = tile_ref.shape[1]
    start_block = first_listed(tile_ref, me)
    width = CHUNK
    tiles = slots // width
    span = REACH * CHUNK
    total = listed * size

    most = scalars_of(bound_ref, low_ref, step_ref)
    summed = mine_power[0, :, size:] + other_power[0, :, size:]
    for index in range(1, chips):
        summed = summed + (mine_power[index, :, size:] + other_power[index, :, size:])
    weights, lost = weights_of([summed[:, index : index + 1] for index in range(6)])
    lost_ref[...] = jnp.broadcast_to(jnp.max(lost[:3], axis=0, keepdims=True), (1, 128))

    def coefficients_of(block):
        data = block_of(mine_ref, other_ref, block, core)
        power = block_of(mine_power, other_power, block, core)[:, :size]
        values = weights[0] * data + weights[1] * power + weights[2] * pltpu.roll(power, 5, 0)
        keep = lax.broadcasted_iota(jnp.int32, (8, size), 0) < 3
        return jnp.where(keep, values, 0.0)

    for index in range(listed):
        vector[:, index * size : (index + 1) * size] = doubled(coefficients_of(start_block + index))
    vector[:, total:] = jnp.zeros((16, span), BF16)

    def lanes_of(tile):
        return pl.ds(pl.multiple_of(tile * width, width), width)

    def one(tile, step, table):
        start = pl.multiple_of((low_ref[tile] + step * REACH) * CHUNK, CHUNK)
        window = vector[:, pl.ds(start, span)]
        return jnp.dot(jnp.concatenate([window, window], axis=1), table, preferred_element_type=F32)

    early = table_ref.shape[0]
    for tile in range(early):
        result[:, tile * width : (tile + 1) * width] = one(tile, 0, table_ref[tile])

    def two_tiles(step, _):
        for piece in range(2):
            tile = early + 2 * step + piece
            table = near_table(source_side, target_side, low_ref, tile, 0)
            result[:, lanes_of(tile)] = one(tile, 0, table)
        return 0

    lax.fori_loop(0, (tiles - early) // 2, two_tiles, 0)

    @pl.when(most > 1)
    def _():
        def of_tile(tile, _):
            def add(step, _):
                table = near_table(source_side, target_side, low_ref, tile, step)
                result[:, lanes_of(tile)] += one(tile, step, table)
                return 0

            return lax.fori_loop(1, step_ref[tile], add, 0)

        lax.fori_loop(0, tiles, of_tile, 0)

    lane = lax.broadcasted_iota(jnp.int32, count_ref.shape, 1)
    live = jnp.sum(jnp.where(lane == me, count_ref[...], 0).astype(F32), axis=1, keepdims=True)
    slot = lax.broadcasted_iota(jnp.int32, (3, slots), 1).astype(F32)
    both = result[...]
    for copy in copies:
        copy.wait()
    coef_ref[...] = moved_back(coefficients_of(me), centre_table[...])
    shift = moved_back(4.0 * (both[:8] + both[8:]), node_table[...])
    shift_ref[...] = jnp.where(slot < live, shift, 0.0)


def near_body(tile_blocks, near_count, bounds, mine, other, mine_power, other_power, sources, targets, tables, centre_table, node_table):
    size = mine.shape[2]
    slots = targets.shape[1]
    total = tile_blocks.shape[1] * size
    return pl.pallas_call(
        near_kernel,
        out_shape=(
            jax.ShapeDtypeStruct((3, size), F32),
            jax.ShapeDtypeStruct((3, slots), F32),
            jax.ShapeDtypeStruct((1, 128), F32),
        ),
        in_specs=[VMEM] * 10 + [HBM] * 2,
        out_specs=(VMEM,) * 3,
        scratch_shapes=[
            pltpu.VMEM((size, size), BF16),
            pltpu.VMEM((slots, slots), BF16),
            pltpu.VMEM((16, total + REACH * CHUNK), BF16),
            pltpu.VMEM((16, slots), F32),
            pltpu.SMEM((slots // CHUNK,), jnp.int32),
            pltpu.SMEM((slots // CHUNK,), jnp.int32),
            pltpu.SemaphoreType.DMA((2,)),
        ],
        compiler_params=pltpu.CompilerParams(vmem_limit_bytes=SMALL_LIMIT),
        name="near_body",
    )(
        tile_blocks, near_count.reshape(1, -1), bounds, mine, other, mine_power, other_power, sources, targets,
        tables,
        pltpu.with_memory_space_constraint(centre_table, pltpu.HBM),
        pltpu.with_memory_space_constraint(node_table, pltpu.HBM),
    )


def gathered(values, partner):
    mine = lax.all_to_all(values, "chip", 0, 0)
    return mine, lax.ppermute(mine, SLAB, partner)


def step_by_step(count, right, centres, tile_blocks, near_count, near_nodes):
    size = centres.shape[1]
    up = [(i, i + 1) for i in range(count - 1)]
    down = [(i + 1, i) for i in range(count - 1)]

    def widened(values):
        return jnp.concatenate([lax.ppermute(values, SLAB, up), values, lax.ppermute(values, SLAB, down)], axis=1)

    def table_of(sources, targets):
        scaled = jnp.sqrt(sum((sources[k][:, None] - targets[k][None, :]) ** 2 for k in range(3))) / SUPPORT
        inside = jnp.maximum(1.0 - scaled, 0.0)
        square_in = inside * inside
        return square_in * square_in * (4.0 * scaled + 1.0)

    def total(left, other):
        return lax.psum(jnp.sum(left * other, axis=1), SLAB)

    def product(values, table):
        return jnp.dot(values, table, precision=lax.Precision.HIGHEST, preferred_element_type=F32)

    around = widened(centres)

    def step(_, held):
        coefficients, residual, search, energy = held
        image = product(widened(search), table_of(around, centres)) + DIAG_SHIFT * search
        length = energy / total(search, image)
        coefficients = coefficients + length[:, None] * search
        residual = residual - length[:, None] * image
        fresh = total(residual, residual)
        return coefficients, residual, residual + (fresh / energy)[:, None] * search, fresh

    coefficients = lax.fori_loop(0, ITERS, step, (jnp.zeros_like(right), right, right, total(right, right)))[0]
    everywhere = lax.all_gather(jnp.concatenate([centres, coefficients], axis=0), SLAB, axis=1, tiled=True)
    me = lax.axis_index(SLAB)
    slots = near_nodes.shape[1]

    def listed(index, sums):
        data = lax.dynamic_slice_in_dim(everywhere, tile_blocks[me, index] * size, size, 1)
        return sums + product(data[3:], table_of(data[:3], near_nodes))

    shift = lax.fori_loop(0, tile_blocks.shape[1], listed, jnp.zeros((3, slots), F32))
    live = lax.iota(jnp.int32, slots) < near_count[me]
    return coefficients, jnp.where(live[None, :], shift, 0.0)


def shards(
    count,
    flow_state,
    flow_speed,
    wall_cell,
    base_shift,
    normals,
    centres,
    tile_blocks,
    near_count,
    near_nodes,
):
    partner = [(i, i ^ 1) for i in range(count)]
    across = [(i, i + 1) for i in range(1, count - 1, 2)]
    across = across + [(j, i) for i, j in across]
    chips, rows = count // 2, flow_state.shape[1]
    send_b = edge_rows(False, flow_state, flow_speed)
    from_b = lax.ppermute(send_b, SLAB, across)
    send_a = edge_rows(True, flow_state, flow_speed)
    from_a = lax.ppermute(send_a, SLAB, partner)
    in_order, centre_table, nodes, node_table = ordered(base_shift, normals, centres, wall_cell, near_nodes)
    new_flow, low, high, base, chosen = inner_flux(flow_state, flow_speed, in_order)
    packed, low, high = right_side(chips, rows, send_a, send_b, from_a, from_b, low, high, base, chosen)
    mine, other = gathered(packed, partner)
    power, new_flow = powers(mine, other, low, high, new_flow, count)
    mine_power, other_power = gathered(power, partner)
    sources, targets, bounds, tables = near_points(tile_blocks, mine, other, nodes)
    coefficients, node_shift, lost = near_body(
        tile_blocks, near_count, bounds, mine, other, mine_power, other_power, sources, targets,
        tables, centre_table, node_table,
    )

    def again(held):
        one = jnp.where(held[0][0, 0] > 0.0, 1.0, 0.0)
        whole = one.astype(jnp.int32)
        own = packed[0] * one
        found, shifted = step_by_step(
            count, own[0:3], own[3:6], tile_blocks * whole, near_count * whole, near_nodes * one
        )
        back = jnp.dot(found, centre_table.astype(F32) * one, precision=lax.Precision.HIGHEST)
        return jnp.zeros_like(held[0]), back, shifted

    _, coefficients, node_shift = lax.while_loop(
        lambda held: held[0][0, 0] > 0.0, again, (lost, coefficients, node_shift)
    )
    return new_flow, coefficients, node_shift


def solution(mesh):
    groups, count = mesh.shape["groups"], mesh.shape["slab"]
    split = Mesh(mesh.devices.reshape(groups, count // 2, 2), ("groups",) + SLAB)
    in_specs = (
        P("groups", SLAB, None),
        P("groups", SLAB, None),
        P(("groups",) + SLAB),
        P("groups", SLAB),
        P("groups", SLAB),
        P("groups", SLAB),
        P("groups", None),
        P("groups"),
        P("groups", SLAB),
    )
    out_specs = (P("groups", SLAB, None), P("groups", SLAB), P("groups", SLAB))
    return jax.shard_map(
        functools.partial(shards, count), mesh=split, in_specs=in_specs, out_specs=out_specs, check_vma=False
    )
```

```python
import functools

import jax
import jax.numpy as jnp
from jax import lax
from jax.experimental import pallas as pl
from jax.experimental.pallas import tpu as pltpu
from jax.sharding import Mesh
from jax.sharding import PartitionSpec as P


FLUX_STEP = 0.2
SUPPORT = 0.15
DIAG_SHIFT = 0.5
CENTRE_SHIFT = DIAG_SHIFT + 1.0
TINY = 1e-12
ITERS = 3
LOSS = 0.01
DEPTH = 0.4
CHUNK = 128
MARGIN = 1e-3
ORDER_FLOPS = 2_000_000_000
BIG_LIMIT = 48 * 1024 * 1024
SMALL_LIMIT = 16 * 1024 * 1024

F32 = jnp.float32
BF16 = jnp.bfloat16
SLAB = ("chip", "core")
VMEM = pl.BlockSpec(memory_space=pltpu.VMEM)
SMEM = pl.BlockSpec(memory_space=pltpu.SMEM)
HBM = pl.BlockSpec(memory_space=pltpu.HBM)


def parts(values):
    first = values.astype(BF16).astype(F32)
    rest = values - first
    second = rest.astype(BF16).astype(F32)
    return first, second, rest - second


def doubled(values):
    high = values.astype(BF16)
    return jnp.concatenate([high, (values - high.astype(F32)).astype(BF16)], axis=0)


def sides(points):
    count = points.shape[1]
    squares = jnp.sum(points * points, axis=0, keepdims=True)
    one = jnp.ones((1, count), F32)
    zero = jnp.zeros((3, count), F32)
    a, b, c = parts(jnp.concatenate([points, squares, one, zero], axis=0))
    d, e, f = parts(jnp.concatenate([-2.0 * points, one, squares, zero], axis=0))
    return jnp.concatenate([a, a, b, a, c, b], axis=0), jnp.concatenate([d, e, d, f, d, e], axis=0)


def quarter_kernel(sources, targets):
    squared = jnp.maximum(jnp.dot(sources, targets, preferred_element_type=F32), TINY)
    inside = jnp.maximum(1.0 - squared * lax.rsqrt(squared), 0.0)
    square_in = inside * inside
    return square_in * square_in * (1.25 - inside)


def local_points(raw, origin):
    x = (raw[0:2] - 0.5) * (1.0 / SUPPORT)
    return jnp.concatenate([x, (raw[2:3] - origin) * (1.0 / SUPPORT)], axis=0)


def rank_of(values):
    count = values.shape[1]
    column = jnp.broadcast_to(values, (8, count)).T[:, 0:1]
    result = []
    for tile in range(count // CHUNK):
        mine = values[:, tile * CHUNK : (tile + 1) * CHUNK]
        total = jnp.zeros((8, CHUNK), F32)
        for chunk in range(count // CHUNK):
            other = column[chunk * CHUNK : (chunk + 1) * CHUNK]
            if chunk < tile:
                before = other <= mine
            elif chunk > tile:
                before = other < mine
            else:
                above = lax.broadcasted_iota(jnp.int32, (CHUNK, CHUNK), 0) < lax.broadcasted_iota(
                    jnp.int32, (CHUNK, CHUNK), 1
                )
                before = jnp.logical_or(other < mine, jnp.logical_and(other == mine, above))
            ones = jnp.where(before, 1.0, 0.0)
            for group in range(CHUNK // 8):
                total = total + ones[group * 8 : group * 8 + 8]
        result.append(jnp.sum(total, axis=0, keepdims=True))
    return jnp.concatenate(result, axis=1)


def moved(values, table):
    rows = values.shape[0]
    stacked = jnp.concatenate(parts(values), axis=0).astype(BF16)
    both = lax.dot_general(
        stacked, table, (((1,), (1,)), ((), ())), preferred_element_type=F32
    )
    return (both[:rows] + both[rows : 2 * rows]) + both[2 * rows :]


def moved_back(values, table):
    both = jnp.dot(doubled(values), table, preferred_element_type=F32)
    return both[:3] + both[8:11]


def chunk_bounds(source_z, target_z, width, low_ref, high_ref):
    chunks = source_z.shape[1] // CHUNK
    tiles = target_z.shape[1] // width

    def edges(values, size, pieces):
        rows = jnp.concatenate([values[:, i * size : (i + 1) * size] for i in range(pieces)], axis=0)
        return jnp.min(rows, axis=1, keepdims=True), jnp.max(rows, axis=1, keepdims=True)

    source_low, source_high = edges(source_z, CHUNK, chunks)
    target_low, target_high = edges(target_z, width, tiles)
    index = lax.broadcasted_iota(jnp.int32, (chunks, 1), 0).astype(F32)
    for tile in range(tiles):
        near = jnp.logical_and(
            source_high >= target_low[tile : tile + 1] - (1.0 + MARGIN),
            source_low <= target_high[tile : tile + 1] + (1.0 + MARGIN),
        )
        low_ref[tile] = jnp.min(jnp.where(near, index, float(chunks))).astype(jnp.int32)
        high_ref[tile] = jnp.max(jnp.where(near, index + 1.0, 0.0)).astype(jnp.int32)


def order_kernel(base_ref, normal_ref, centre_ref, cell_ref, nodes_ref, out_ref, centre_table, nodes_out, node_table):
    def table_of(ref, rank):
        count = rank.shape[1]
        rows = 128
        for start in range(0, count, rows):
            row = lax.broadcasted_iota(jnp.int32, (rows, count), 0).astype(F32) + float(start)
            ref[start : start + rows] = jnp.where(row == rank, 1.0, 0.0).astype(BF16)

    count = centre_ref.shape[1]
    table_of(centre_table, rank_of(centre_ref[2:3]))
    values = jnp.concatenate(
        [
            base_ref[...],
            normal_ref[...],
            centre_ref[...],
            cell_ref[...].astype(F32),
            jnp.zeros((6, count), F32),
        ],
        axis=0,
    )
    out_ref[...] = moved(values, centre_table[...])
    table_of(node_table, rank_of(nodes_ref[2:3]))
    nodes = jnp.concatenate([nodes_ref[...], jnp.zeros((5, nodes_ref.shape[1]), F32)], axis=0)
    nodes_out[...] = moved(nodes, node_table[...])


def ordered(base_shift, normals, centres, wall_cell, near_nodes):
    count, slots = centres.shape[1], near_nodes.shape[1]
    return pl.pallas_call(
        order_kernel,
        out_shape=(
            jax.ShapeDtypeStruct((16, count), F32),
            jax.ShapeDtypeStruct((count, count), BF16),
            jax.ShapeDtypeStruct((8, slots), F32),
            jax.ShapeDtypeStruct((slots, slots), BF16),
        ),
        in_specs=[VMEM] * 5,
        out_specs=(VMEM,) * 4,
        compiler_params=pltpu.CompilerParams(vmem_limit_bytes=SMALL_LIMIT),
        cost_estimate=pl.CostEstimate(flops=ORDER_FLOPS, bytes_accessed=4_000_000, transcendentals=0),
        name="order",
    )(base_shift, normals, centres, wall_cell.reshape(1, -1), near_nodes)


def edge_kernel(even_last, q_ref, w_ref, target, sems):
    count, rows, _ = q_ref.shape

    def move(row):
        copies = []
        for index in range(count + 1):
            source = q_ref.at[index] if index < count else w_ref.at[0]
            copies.append(
                pltpu.make_async_copy(source.at[pl.ds(row, 1)], target.at[pl.ds(index, 1)], sems.at[index])
            )
        for copy in copies:
            copy.start()
        for copy in copies:
            copy.wait()

    core = lax.axis_index("core")

    @pl.when(core == 0)
    def _():
        move(rows - 1 if even_last else 0)

    @pl.when(core != 0)
    def _():
        move(0 if even_last else rows - 1)


def edge_rows(even_last, flow_state, flow_speed):
    count, _, plane = flow_state.shape
    return pl.pallas_call(
        functools.partial(edge_kernel, even_last),
        out_shape=jax.ShapeDtypeStruct((count + 1, plane), F32),
        in_specs=[HBM, HBM],
        out_specs=VMEM,
        scratch_shapes=[pltpu.SemaphoreType.DMA((count + 1,))],
        compiler_params=pltpu.CompilerParams(vmem_limit_bytes=SMALL_LIMIT),
        name="edge_rows",
    )(
        pltpu.with_memory_space_constraint(flow_state, pltpu.HBM),
        pltpu.with_memory_space_constraint(flow_speed, pltpu.HBM),
    )


RATE = 0.5 * FLUX_STEP
PRESSURE = 4


def picked(stacked, chosen, lane):
    high, middle, low = parts(stacked)
    pieces = jnp.concatenate([high, middle, low], axis=1).astype(BF16)
    both = lax.dot_general(pieces, chosen, (((0,), (0,)), ((), ())), preferred_element_type=F32)
    value = (both[:128] + both[128:256]) + both[256:]
    here = lax.broadcasted_iota(jnp.int32, value.shape, 0) == lane
    return jnp.sum(jnp.where(here, value, 0.0), axis=0, keepdims=True)


def stacked_lanes(values):
    return jnp.concatenate([values[:, i : i + 128] for i in range(0, values.shape[1], 128)], axis=0)


def inner_kernel(q_ref, w_ref, sorted_ref, new_hbm, low_ref, high_ref, out_ref, chosen_ref, new_ref, sems):
    count, rows, plane = q_ref.shape
    width = 512
    steps = plane // width
    row = lax.broadcasted_iota(jnp.int32, (rows, width), 0)

    def copy_of(step):
        lanes = pl.ds(pl.multiple_of(step * width, width), width)
        return pltpu.make_async_copy(new_ref.at[:, :, lanes], new_hbm.at[:, :, lanes], sems.at[step])

    def chunk(step, _):
        here = pl.multiple_of(step * width, 128)
        left = pl.multiple_of(lax.rem(here + plane - 128, plane), 128)
        right = pl.multiple_of(lax.rem(here + width, plane), 128)

        def cyclic(ref, index):
            values = ref[index, :, pl.ds(here, width)]
            wide = jnp.concatenate(
                [ref[index, :, pl.ds(left, 128)], values, ref[index, :, pl.ds(right, 128)]], axis=1
            )
            before = pltpu.roll(wide, 1, 1)[:, 128 : 128 + width]
            after = pltpu.roll(wide, width + 255, 1)[:, 128 : 128 + width]
            return values, before, after

        w = w_ref[0, :, pl.ds(here, width)]
        face_low = jnp.where(row == 0, 0.0, RATE * (pltpu.roll(w, 1, 0) + w))
        face_high = jnp.where(row == rows - 1, 0.0, RATE * (w + pltpu.roll(w, rows - 1, 0)))
        speed, speed_before, speed_after = cyclic(w_ref, 1)
        face_left = RATE * (speed_before + speed)
        face_right = RATE * (speed + speed_after)
        low_in = jnp.maximum(face_low, 0.0)
        high_out = jnp.minimum(face_high, 0.0)
        left_in = jnp.maximum(face_left, 0.0)
        right_out = jnp.minimum(face_right, 0.0)
        keep = 1.0 - (
            (jnp.maximum(face_high, 0.0) - jnp.minimum(face_low, 0.0))
            + (jnp.maximum(face_right, 0.0) - jnp.minimum(face_left, 0.0))
        )
        for index in range(count):
            values, before, after = cyclic(q_ref, index)
            new = (
                keep * values
                + low_in * pltpu.roll(values, 1, 0)
                - high_out * pltpu.roll(values, rows - 1, 0)
                + left_in * before
                - right_out * after
            )
            new_ref[index, :, pl.ds(here, width)] = new
            low_ref[index : index + 1, pl.ds(here, width)] = new[0:1]
            high_ref[index : index + 1, pl.ds(here, width)] = new[rows - 1 : rows]
        copy_of(step).start()
        return 0

    lax.fori_loop(0, steps, chunk, 0)

    cells = sorted_ref[9:10].astype(jnp.int32)
    cell_row = cells // plane
    column = cells - cell_row * plane
    group = column // 128
    lane = column - group * 128
    place = group * rows + cell_row
    centres = cells.shape[1]
    lanes = plane // 128
    chosen = (lax.broadcasted_iota(jnp.int32, (rows * lanes, centres), 0) == place).astype(F32).astype(BF16)
    chosen_ref[...] = chosen
    load = picked(stacked_lanes(new_ref[PRESSURE]), chosen, lane)
    out_ref[...] = jnp.concatenate(
        [
            sorted_ref[0:3] + sorted_ref[3:6] * load,
            sorted_ref[3:9],
            lane.astype(F32),
            jnp.zeros((6, centres), F32),
        ],
        axis=0,
    )
    for step in range(steps):
        copy_of(step).wait()


def inner_flux(flow_state, flow_speed, in_order):
    count, rows, plane = flow_state.shape
    centres = in_order.shape[1]
    edge = jax.ShapeDtypeStruct((count, plane), F32)
    return pl.pallas_call(
        inner_kernel,
        out_shape=(
            pltpu.HBM(flow_state.shape, F32),
            edge,
            edge,
            jax.ShapeDtypeStruct((16, centres), F32),
            jax.ShapeDtypeStruct((rows * plane // 128, centres), BF16),
        ),
        in_specs=[VMEM] * 3,
        out_specs=(HBM, VMEM, VMEM, VMEM, VMEM),
        scratch_shapes=[pltpu.VMEM(flow_state.shape, F32), pltpu.SemaphoreType.DMA((plane // 512,))],
        compiler_params=pltpu.CompilerParams(vmem_limit_bytes=SMALL_LIMIT),
        cost_estimate=pl.CostEstimate(flops=20_000_000, bytes_accessed=4_000_000, transcendentals=0),
        name="inner_flux",
    )(flow_state, flow_speed, in_order)


def outer_kernel(
    send_a, send_b, from_a, from_b, low_ref, high_ref, base_ref, chosen_ref, out_ref, new_low, new_high, both_ref
):
    count, plane = low_ref.shape
    rows = both_ref.shape[0]
    even = lax.axis_index("core") == 0
    own_low = jnp.where(even, send_b[...], send_a[...])
    own_high = jnp.where(even, send_a[...], send_b[...])
    below = jnp.where(even, from_b[...], from_a[...])
    above = jnp.where(even, from_a[...], from_b[...])

    def flux(first, second):
        face = RATE * (first[count : count + 1] + second[count : count + 1])
        return jnp.maximum(face, 0.0) * first[:count] + jnp.minimum(face, 0.0) * second[:count]

    low = flux(below, own_low)
    high = flux(own_high, above)
    new_low[...] = low_ref[...] + low
    new_high[...] = high_ref[...] - high
    row = lax.broadcasted_iota(jnp.int32, (rows, plane), 0)
    zero = jnp.zeros((rows, plane), F32)
    added = jnp.where(row == 0, low[PRESSURE : PRESSURE + 1], zero)
    added = added - jnp.where(row == rows - 1, high[PRESSURE : PRESSURE + 1], zero)
    both_ref[...] = added
    base = base_ref[...]
    load = picked(stacked_lanes(both_ref[...]), chosen_ref[...], base[9:10].astype(jnp.int32))
    centres = base.shape[1]
    packed = jnp.concatenate([base[0:3] + base[3:6] * load, base[6:9], jnp.zeros((2, centres), F32)], axis=0)
    for chip in range(out_ref.shape[0]):
        out_ref[chip] = packed


def right_side(chips, rows, send_a, send_b, from_a, from_b, low, high, base, chosen):
    edge = jax.ShapeDtypeStruct(low.shape, F32)
    return pl.pallas_call(
        outer_kernel,
        out_shape=(jax.ShapeDtypeStruct((chips, 8, base.shape[1]), F32), edge, edge),
        in_specs=[VMEM] * 8,
        out_specs=(VMEM,) * 3,
        scratch_shapes=[pltpu.VMEM((rows, low.shape[1]), F32)],
        compiler_params=pltpu.CompilerParams(vmem_limit_bytes=SMALL_LIMIT),
        name="outer_flux",
    )(send_a, send_b, from_a, from_b, low, high, base, chosen)


def block_of(mine_ref, other_ref, block, core):
    chip = lax.div(block, 2)
    own = lax.rem(block, 2) == core
    return jnp.where(own, mine_ref[chip], other_ref[chip])


def powers_kernel(
    count, mine_ref, other_ref, new_low, new_high, new_in, out_ref, new_out,
    source_side, target_side, vector, image, tables, low_ref, high_ref, sems,
):
    del new_in
    rows_per_block = new_out.shape[1]
    copies = [
        pltpu.make_async_copy(new_low, new_out.at[:, 0], sems.at[0]),
        pltpu.make_async_copy(new_high, new_out.at[:, rows_per_block - 1], sems.at[1]),
    ]
    for copy in copies:
        copy.start()
    size = mine_ref.shape[2]
    chip, core = lax.axis_index("chip"), lax.axis_index("core")
    me = chip * 2 + core
    slots, width, reach = 6, 256, 6
    span = reach * CHUNK
    total = slots * size
    origin = lax.div(me * 2, 5).astype(F32)
    value_row = lax.broadcasted_iota(jnp.int32, (8, size), 0) < 3

    live, zeroth, third = [], [], []
    for slot in range(slots):
        block = me + slot - 2
        valid = jnp.logical_and(block >= 0, block < count)
        live.append(valid)
        data = block_of(mine_ref, other_ref, jnp.clip(block, 0, count - 1), core)
        zeroth.append(jnp.where(jnp.logical_and(value_row, valid), data, 0.0))
        middle = (block.astype(F32) + 0.5) * DEPTH
        raw = jnp.concatenate([data[3:5], jnp.where(valid, data[5:6], middle)], axis=0)
        points = local_points(raw, origin)
        third.append(points[2:3])
        source, target = sides(points)
        source_side[slot * size : (slot + 1) * size] = source.T.astype(BF16)
        target_side[:, slot * size : (slot + 1) * size] = target.astype(BF16)
    far = (lax.broadcasted_iota(jnp.int32, (span, 48), 1) == 3).astype(F32) * 4096.0
    source_side[total:] = far.astype(BF16)
    vector[:, total:] = jnp.zeros((16, span), BF16)
    heights = jnp.concatenate(third, axis=1)
    chunk_bounds(heights, heights[:, size : 5 * size], width, low_ref, high_ref)
    tiles = 4 * size // width

    def steps_of(tile):
        return lax.div(high_ref[tile] - low_ref[tile] + (reach - 1), reach)

    most = steps_of(0)
    for tile in range(1, tiles):
        most = jnp.maximum(most, steps_of(tile))

    skipped, per_tile, mine_first = size // CHUNK, width // CHUNK, size // width
    per_block = size // width

    def tiles_up_to(chunk):
        return lax.div(chunk - skipped + (per_tile - 1), per_tile)

    second_end = high_ref[mine_first]
    for tile in range(mine_first + 1, 2 * mine_first):
        second_end = jnp.maximum(second_end, high_ref[tile])
    second_end = jnp.clip(tiles_up_to(second_end), 2 * per_block, 3 * per_block)
    read_low, read_high = low_ref[mine_first], high_ref[mine_first]
    for tile in range(mine_first + 1, 3 * per_block):
        read = tile < second_end
        read_low = jnp.minimum(read_low, jnp.where(read, low_ref[tile], read_low))
        read_high = jnp.maximum(read_high, jnp.where(read, high_ref[tile], read_high))
    first_start = jnp.clip(lax.div(jnp.maximum(read_low - skipped, 0), per_tile), 0, per_block)
    first_end = jnp.clip(tiles_up_to(read_high), second_end, tiles)
    same = lax.broadcasted_iota(jnp.int32, (CHUNK, CHUNK), 0) == lax.broadcasted_iota(
        jnp.int32, (CHUNK, CHUNK), 1
    )

    def build(tile, step):
        lanes = pl.ds(pl.multiple_of(tile * width + size, width), width)
        chunk = low_ref[tile] + step * reach
        rows = pl.ds(pl.multiple_of(chunk * CHUNK, CHUNK), span)
        table = quarter_kernel(source_side[rows], target_side[:, lanes])
        high = table.astype(BF16)
        tables[tile, step, :span] = high
        tables[tile, step, span:] = (table - high.astype(F32)).astype(BF16)
        for piece in range(width // CHUNK):
            place = (tile * width + size) // CHUNK + piece - chunk
            inside = jnp.logical_and(place >= 0, place < reach)
            place = jnp.clip(place, 0, reach - 1)
            for half in range(2):
                at = pl.ds(pl.multiple_of(place * CHUNK + half * span, CHUNK), CHUNK)
                columns = slice(piece * CHUNK, (piece + 1) * CHUNK)
                old = tables[tile, step, at, columns]
                tables[tile, step, at, columns] = jnp.where(jnp.logical_and(same, inside), 0.0, old.astype(F32)).astype(BF16)

    def one(tile, step):
        lanes = pl.ds(pl.multiple_of((low_ref[tile] + step * reach) * CHUNK, CHUNK), span)
        window = vector[:, lanes]
        return jnp.dot(jnp.concatenate([window, window], axis=1), tables[tile, step], preferred_element_type=F32)

    def lanes_of(tile):
        return pl.ds(pl.multiple_of(tile * width, width), width)

    def further(first, last):
        @pl.when(most > 1)
        def _():
            def of_tile(tile, _):
                def add(step, _):
                    image[:, lanes_of(tile)] += one(tile, step)
                    return 0

                return lax.fori_loop(1, steps_of(tile), add, 0)

            lax.fori_loop(first, last, of_tile, 0)

    def image_of(slot):
        both = image[:, (slot - 1) * size : slot * size]
        return jnp.where(live[slot], 4.0 * (both[:8] + both[8:]), 0.0)

    def power(slots, end):
        first, last = (slots[0] - 1) * per_block, slots[-1] * per_block
        for tile in range(first, last):
            here = slice(tile * width, (tile + 1) * width)
            if tile < 2 * per_block:
                image[:, here] = one(tile, 0)
            else:
                image[:, here] = jnp.zeros((16, width), F32)

                @pl.when(tile < end)
                def _(tile=tile, here=here):
                    image[:, here] = one(tile, 0)

        further(first, end)
        return {slot: image_of(slot) for slot in slots}

    def hold(values, slot):
        vector[:, slot * size : (slot + 1) * size] = doubled(values)

    for slot in range(slots):
        hold(zeroth[slot], slot)

    for tile in (*range(per_block), *range(2 * per_block, tiles)):
        image[:, tile * width : (tile + 1) * width] = jnp.zeros((16, width), F32)

    def tile_step(tile, _):
        before = jnp.maximum(tile - 1, first_start)
        image[:, lanes_of(before)] = one(before, 0)
        build(tile, 0)
        return 0

    lax.fori_loop(first_start, first_end, tile_step, 0)
    image[:, lanes_of(first_end - 1)] = one(first_end - 1, 0)

    @pl.when(most > 1)
    def _():
        def of_tile(tile, _):
            def more(step, _):
                build(tile, step)
                return 0

            return lax.fori_loop(1, steps_of(tile), more, 0)

        lax.fori_loop(first_start, first_end, of_tile, 0)

    further(first_start, first_end)
    first = {slot: image_of(slot) for slot in range(1, 5)}
    for slot in range(1, 5):
        hold(first[slot], slot)
    second = power([2, 3], second_end)
    hold(jnp.zeros((8, size), F32), 1)
    hold(second[2], 2)
    hold(2.0 * second[3], 3)
    last = power([2], 2 * per_block)[2]

    def inner(left, right):
        return jnp.sum(left * right, axis=1, keepdims=True)

    moments = [
        inner(zeroth[2], zeroth[2]),
        inner(zeroth[2], first[2]),
        inner(first[2], first[2]),
        inner(first[2], second[2]),
        inner(second[2], second[2]),
        inner(second[2], last),
    ]
    lane = lax.broadcasted_iota(jnp.int32, (8, 128), 1)
    packed = jnp.zeros((8, 128), F32)
    for index, moment in enumerate(moments):
        packed = jnp.where(lane == index, moment, packed)
    values = jnp.concatenate([first[2][:3], second[2][:3], jnp.zeros((2, size), F32)], axis=0)
    for index in range(out_ref.shape[0]):
        out_ref[index, :, :size] = values
        out_ref[index, :, size:] = packed
    for copy in copies:
        copy.wait()


def powers(mine, other, new_low, new_high, new_flow, count):
    chips, _, size = mine.shape
    tiles = 4 * size // 256
    steps = (6 * size // CHUNK + 5) // 6
    return pl.pallas_call(
        functools.partial(powers_kernel, count),
        out_shape=(
            jax.ShapeDtypeStruct((chips, 8, size + 128), F32),
            pltpu.HBM(new_flow.shape, F32),
        ),
        in_specs=[VMEM] * 4 + [HBM],
        out_specs=(VMEM, HBM),
        scratch_shapes=[
            pltpu.VMEM((6 * size + 6 * CHUNK, 48), BF16),
            pltpu.VMEM((48, 6 * size), BF16),
            pltpu.VMEM((16, 6 * size + 6 * CHUNK), BF16),
            pltpu.VMEM((16, 4 * size), F32),
            pltpu.VMEM((tiles, steps, 12 * CHUNK, 256), BF16),
            pltpu.SMEM((tiles,), jnp.int32),
            pltpu.SMEM((tiles,), jnp.int32),
            pltpu.SemaphoreType.DMA((2,)),
        ],
        input_output_aliases={4: 1},
        compiler_params=pltpu.CompilerParams(vmem_limit_bytes=BIG_LIMIT),
        name="powers",
    )(mine, other, new_low, new_high, pltpu.with_memory_space_constraint(new_flow, pltpu.HBM))


def ratio(top, bottom):
    safe = bottom > 0.0
    return jnp.where(safe, top / jnp.where(safe, bottom, 1.0), 0.0)


def weights_of(moments):
    lost = jnp.zeros_like(moments[0])

    def inner(left, right):
        total = size = None
        for i, a in enumerate(left):
            for j, c in enumerate(right):
                term = a * c * moments[i + j]
                total = term if total is None else total + term
                size = jnp.abs(term) if size is None else size + jnp.abs(term)
        return total, jnp.where(total > LOSS * size, 0.0, jnp.where(size > 0.0, 1.0, 0.0))

    one = jnp.ones_like(moments[0])
    residual, search = [one], [one]
    coefficients = [0.0 * one] * ITERS
    energy = moments[0]
    for step in range(ITERS):
        image = [CENTRE_SHIFT * value for value in search] + [0.0 * one]
        for index, value in enumerate(search):
            image[index + 1] = image[index + 1] + value
        along, bad = inner(search, image)
        lost = lost + bad
        length = ratio(energy, along)
        for index, value in enumerate(search):
            coefficients[index] = coefficients[index] + length * value
        if step == ITERS - 1:
            break
        longer = residual + [0.0 * one]
        residual = [value - length * other for value, other in zip(longer, image)]
        fresh, bad = inner(residual, residual)
        lost = lost + bad
        scale = ratio(fresh, energy)
        search = [
            value + scale * (search[index] if index < len(search) else 0.0)
            for index, value in enumerate(residual)
        ]
        energy = fresh
    return coefficients, lost


REACH = 7


def bounds_of(source_z, target_z):
    chunks = source_z.shape[1] // CHUNK
    tiles = target_z.shape[1] // CHUNK

    def edges(values, pieces):
        rows = jnp.concatenate([values[:, i * CHUNK : (i + 1) * CHUNK] for i in range(pieces)], axis=0)
        return jnp.min(rows, axis=1, keepdims=True), jnp.max(rows, axis=1, keepdims=True)

    def across(values):
        return jnp.broadcast_to(values, (tiles, 128)).T[0:1]

    source_low, source_high = edges(source_z, chunks)
    target_low, target_high = edges(target_z, tiles)
    near = jnp.logical_and(
        source_high >= across(target_low) - (1.0 + MARGIN), source_low <= across(target_high) + (1.0 + MARGIN)
    )
    index = lax.broadcasted_iota(jnp.int32, (chunks, tiles), 0).astype(F32)
    low = jnp.min(jnp.where(near, index, float(chunks)), axis=0, keepdims=True)
    high = jnp.max(jnp.where(near, index + 1.0, 0.0), axis=0, keepdims=True)
    return jnp.concatenate([low, high], axis=0)


def first_listed(tile_ref, me):
    return tile_ref[pl.ds(me, 1), :][0, 0]


def points_kernel(tile_ref, mine_ref, other_ref, nodes_ref, source_ref, target_ref, bound_ref):
    size = mine_ref.shape[2]
    core = lax.axis_index("core")
    me = lax.axis_index("chip") * 2 + core
    listed = tile_ref.shape[1]
    start = first_listed(tile_ref, me)
    origin = lax.div((start + 2) * 2, 5).astype(F32)
    third = []
    for index in range(listed):
        data = block_of(mine_ref, other_ref, start + index, core)
        points = local_points(data[3:6], origin)
        third.append(points[2:3])
        source, _ = sides(points)
        source_ref[index * size : (index + 1) * size] = source.T.astype(BF16)
    span = REACH * CHUNK
    far = (lax.broadcasted_iota(jnp.int32, (span, 48), 1) == 3).astype(F32) * 4096.0
    source_ref[listed * size :] = far.astype(BF16)
    points = local_points(nodes_ref[0:3], origin)
    _, target = sides(points)
    target_ref[...] = target.astype(BF16)
    bound_ref[...] = bounds_of(jnp.concatenate(third, axis=1), points[2:3])


def near_points(tile_blocks, mine, other, nodes):
    size = mine.shape[2]
    slots = nodes.shape[1]
    listed = tile_blocks.shape[1]
    return pl.pallas_call(
        points_kernel,
        out_shape=(
            jax.ShapeDtypeStruct((listed * size + REACH * CHUNK, 48), BF16),
            jax.ShapeDtypeStruct((48, slots), BF16),
            jax.ShapeDtypeStruct((2, slots // CHUNK), F32),
        ),
        in_specs=[VMEM] * 4,
        out_specs=(VMEM,) * 3,
        compiler_params=pltpu.CompilerParams(vmem_limit_bytes=SMALL_LIMIT),
        cost_estimate=pl.CostEstimate(flops=1_000_000, bytes_accessed=1_000_000, transcendentals=0),
        name="near_points",
    )(tile_blocks, mine, other, nodes)


def near_kernel(
    tile_ref, count_ref, bound_ref, mine_ref, other_ref, mine_power, other_power, source_side, target_side,
    centre_table, node_table, coef_ref, shift_ref, lost_ref, vector, result, low_ref, step_ref,
):
    size = mine_ref.shape[2]
    slots = target_side.shape[1]
    chips = mine_ref.shape[0]
    core = lax.axis_index("core")
    me = lax.axis_index("chip") * 2 + core
    listed = tile_ref.shape[1]
    start_block = first_listed(tile_ref, me)
    width = CHUNK
    tiles = slots // width
    span = REACH * CHUNK
    total = listed * size

    bounds = bound_ref[...].astype(jnp.int32)
    most = 0
    for tile in range(tiles):
        low = bounds[0, tile]
        steps = lax.div(bounds[1, tile] - low + (REACH - 1), REACH)
        low_ref[tile] = low
        step_ref[tile] = steps
        most = jnp.maximum(most, steps)

    summed = mine_power[0, :, size:] + other_power[0, :, size:]
    for index in range(1, chips):
        summed = summed + (mine_power[index, :, size:] + other_power[index, :, size:])
    weights, lost = weights_of([summed[:, index : index + 1] for index in range(6)])
    lost_ref[...] = jnp.broadcast_to(jnp.max(lost[:3], axis=0, keepdims=True), (1, 128))

    def coefficients_of(block):
        data = block_of(mine_ref, other_ref, block, core)
        power = block_of(mine_power, other_power, block, core)[:, :size]
        values = weights[0] * data + weights[1] * power + weights[2] * pltpu.roll(power, 5, 0)
        keep = lax.broadcasted_iota(jnp.int32, (8, size), 0) < 3
        return jnp.where(keep, values, 0.0)

    for index in range(listed):
        vector[:, index * size : (index + 1) * size] = doubled(coefficients_of(start_block + index))
    vector[:, total:] = jnp.zeros((16, span), BF16)
    coef_ref[...] = moved_back(coefficients_of(me), centre_table[...])

    def lanes_of(tile):
        return pl.ds(pl.multiple_of(tile * width, width), width)

    def one(tile, step):
        start = pl.multiple_of((low_ref[tile] + step * REACH) * CHUNK, CHUNK)
        table = quarter_kernel(source_side[pl.ds(start, span)], target_side[:, lanes_of(tile)])
        window = vector[:, pl.ds(start, span)]
        return jnp.dot(jnp.concatenate([window, window], axis=1), doubled(table), preferred_element_type=F32)

    def two_tiles(step, _):
        for piece in range(2):
            result[:, lanes_of(2 * step + piece)] = one(2 * step + piece, 0)
        return 0

    lax.fori_loop(0, tiles // 2, two_tiles, 0)

    @pl.when(most > 1)
    def _():
        def of_tile(tile, _):
            def add(step, _):
                result[:, lanes_of(tile)] += one(tile, step)
                return 0

            return lax.fori_loop(1, step_ref[tile], add, 0)

        lax.fori_loop(0, tiles, of_tile, 0)

    lane = lax.broadcasted_iota(jnp.int32, count_ref.shape, 1)
    live = jnp.sum(jnp.where(lane == me, count_ref[...], 0).astype(F32), axis=1, keepdims=True)
    slot = lax.broadcasted_iota(jnp.int32, (3, slots), 1).astype(F32)
    both = result[...]
    shift = moved_back(4.0 * (both[:8] + both[8:]), node_table[...])
    shift_ref[...] = jnp.where(slot < live, shift, 0.0)


def near_body(tile_blocks, near_count, bounds, mine, other, mine_power, other_power, sources, targets, centre_table, node_table):
    size = mine.shape[2]
    slots = targets.shape[1]
    total = tile_blocks.shape[1] * size
    return pl.pallas_call(
        near_kernel,
        out_shape=(
            jax.ShapeDtypeStruct((3, size), F32),
            jax.ShapeDtypeStruct((3, slots), F32),
            jax.ShapeDtypeStruct((1, 128), F32),
        ),
        in_specs=[VMEM] * 11,
        out_specs=(VMEM,) * 3,
        scratch_shapes=[
            pltpu.VMEM((16, total + REACH * CHUNK), BF16),
            pltpu.VMEM((16, slots), F32),
            pltpu.SMEM((slots // CHUNK,), jnp.int32),
            pltpu.SMEM((slots // CHUNK,), jnp.int32),
        ],
        compiler_params=pltpu.CompilerParams(vmem_limit_bytes=SMALL_LIMIT),
        name="near_body",
    )(
        tile_blocks, near_count.reshape(1, -1), bounds, mine, other, mine_power, other_power, sources, targets,
        centre_table, node_table,
    )


def gathered(values, partner):
    mine = lax.all_to_all(values, "chip", 0, 0)
    return mine, lax.ppermute(mine, SLAB, partner)


def step_by_step(count, right, centres, tile_blocks, near_count, near_nodes):
    size = centres.shape[1]
    up = [(i, i + 1) for i in range(count - 1)]
    down = [(i + 1, i) for i in range(count - 1)]

    def widened(values):
        return jnp.concatenate([lax.ppermute(values, SLAB, up), values, lax.ppermute(values, SLAB, down)], axis=1)

    def table_of(sources, targets):
        scaled = jnp.sqrt(sum((sources[k][:, None] - targets[k][None, :]) ** 2 for k in range(3))) / SUPPORT
        inside = jnp.maximum(1.0 - scaled, 0.0)
        square_in = inside * inside
        return square_in * square_in * (4.0 * scaled + 1.0)

    def total(left, other):
        return lax.psum(jnp.sum(left * other, axis=1), SLAB)

    def product(values, table):
        return jnp.dot(values, table, precision=lax.Precision.HIGHEST, preferred_element_type=F32)

    around = widened(centres)

    def step(_, held):
        coefficients, residual, search, energy = held
        image = product(widened(search), table_of(around, centres)) + DIAG_SHIFT * search
        length = energy / total(search, image)
        coefficients = coefficients + length[:, None] * search
        residual = residual - length[:, None] * image
        fresh = total(residual, residual)
        return coefficients, residual, residual + (fresh / energy)[:, None] * search, fresh

    coefficients = lax.fori_loop(0, ITERS, step, (jnp.zeros_like(right), right, right, total(right, right)))[0]
    everywhere = lax.all_gather(jnp.concatenate([centres, coefficients], axis=0), SLAB, axis=1, tiled=True)
    me = lax.axis_index(SLAB)
    slots = near_nodes.shape[1]

    def listed(index, sums):
        data = lax.dynamic_slice_in_dim(everywhere, tile_blocks[me, index] * size, size, 1)
        return sums + product(data[3:], table_of(data[:3], near_nodes))

    shift = lax.fori_loop(0, tile_blocks.shape[1], listed, jnp.zeros((3, slots), F32))
    live = lax.iota(jnp.int32, slots) < near_count[me]
    return coefficients, jnp.where(live[None, :], shift, 0.0)


def shards(
    count,
    flow_state,
    flow_speed,
    wall_cell,
    base_shift,
    normals,
    centres,
    tile_blocks,
    near_count,
    near_nodes,
):
    partner = [(i, i ^ 1) for i in range(count)]
    across = [(i, i + 1) for i in range(1, count - 1, 2)]
    across = across + [(j, i) for i, j in across]
    chips, rows = count // 2, flow_state.shape[1]
    send_b = edge_rows(False, flow_state, flow_speed)
    from_b = lax.ppermute(send_b, SLAB, across)
    send_a = edge_rows(True, flow_state, flow_speed)
    from_a = lax.ppermute(send_a, SLAB, partner)
    in_order, centre_table, nodes, node_table = ordered(base_shift, normals, centres, wall_cell, near_nodes)
    new_flow, low, high, base, chosen = inner_flux(flow_state, flow_speed, in_order)
    packed, low, high = right_side(chips, rows, send_a, send_b, from_a, from_b, low, high, base, chosen)
    mine, other = gathered(packed, partner)
    power, new_flow = powers(mine, other, low, high, new_flow, count)
    mine_power, other_power = gathered(power, partner)
    sources, targets, bounds = near_points(tile_blocks, mine, other, nodes)
    coefficients, node_shift, lost = near_body(
        tile_blocks, near_count, bounds, mine, other, mine_power, other_power, sources, targets,
        centre_table, node_table,
    )

    def again(held):
        one = jnp.where(held[0][0, 0] > 0.0, 1.0, 0.0)
        whole = one.astype(jnp.int32)
        own = packed[0] * one
        found, shifted = step_by_step(
            count, own[0:3], own[3:6], tile_blocks * whole, near_count * whole, near_nodes * one
        )
        back = jnp.dot(found, centre_table.astype(F32) * one, precision=lax.Precision.HIGHEST)
        return jnp.zeros_like(held[0]), back, shifted

    _, coefficients, node_shift = lax.while_loop(
        lambda held: held[0][0, 0] > 0.0, again, (lost, coefficients, node_shift)
    )
    return new_flow, coefficients, node_shift


def solution(mesh):
    groups, count = mesh.shape["groups"], mesh.shape["slab"]
    split = Mesh(mesh.devices.reshape(groups, count // 2, 2), ("groups",) + SLAB)
    in_specs = (
        P("groups", SLAB, None),
        P("groups", SLAB, None),
        P(("groups",) + SLAB),
        P("groups", SLAB),
        P("groups", SLAB),
        P("groups", SLAB),
        P("groups", None),
        P("groups"),
        P("groups", SLAB),
    )
    out_specs = (P("groups", SLAB, None), P("groups", SLAB), P("groups", SLAB))
    return jax.shard_map(
        functools.partial(shards, count), mesh=split, in_specs=in_specs, out_specs=out_specs, check_vma=False
    )
```

```python
import functools

import jax
import jax.numpy as jnp
from jax import lax
from jax.experimental import pallas as pl
from jax.experimental.pallas import tpu as pltpu
from jax.sharding import Mesh
from jax.sharding import PartitionSpec as P


FLUX_STEP = 0.2
SUPPORT = 0.15
DIAG_SHIFT = 0.5
CENTRE_SHIFT = DIAG_SHIFT + 1.0
TINY = 1e-12
ITERS = 3
LOSS = 0.01
DEPTH = 0.4
CHUNK = 128
MARGIN = 1e-3
ORDER_FLOPS = 2_000_000_000
BIG_LIMIT = 48 * 1024 * 1024
SMALL_LIMIT = 16 * 1024 * 1024

F32 = jnp.float32
BF16 = jnp.bfloat16
SLAB = ("chip", "core")
VMEM = pl.BlockSpec(memory_space=pltpu.VMEM)
SMEM = pl.BlockSpec(memory_space=pltpu.SMEM)
HBM = pl.BlockSpec(memory_space=pltpu.HBM)


def parts(values):
    first = values.astype(BF16).astype(F32)
    rest = values - first
    second = rest.astype(BF16).astype(F32)
    return first, second, rest - second


def doubled(values):
    high = values.astype(BF16)
    return jnp.concatenate([high, (values - high.astype(F32)).astype(BF16)], axis=0)


def sides(points):
    count = points.shape[1]
    squares = jnp.sum(points * points, axis=0, keepdims=True)
    one = jnp.ones((1, count), F32)
    zero = jnp.zeros((3, count), F32)
    a, b, c = parts(jnp.concatenate([points, squares, one, zero], axis=0))
    d, e, f = parts(jnp.concatenate([-2.0 * points, one, squares, zero], axis=0))
    return jnp.concatenate([a, a, b, a, c, b], axis=0), jnp.concatenate([d, e, d, f, d, e], axis=0)


def quarter_kernel(sources, targets):
    squared = jnp.maximum(jnp.dot(sources, targets, preferred_element_type=F32), TINY)
    inside = jnp.maximum(1.0 - squared * lax.rsqrt(squared), 0.0)
    square_in = inside * inside
    return square_in * square_in * (1.25 - inside)


def local_points(raw, origin):
    x = (raw[0:2] - 0.5) * (1.0 / SUPPORT)
    return jnp.concatenate([x, (raw[2:3] - origin) * (1.0 / SUPPORT)], axis=0)


def rank_of(values):
    count = values.shape[1]
    column = jnp.broadcast_to(values, (8, count)).T[:, 0:1]
    result = []
    for tile in range(count // CHUNK):
        mine = values[:, tile * CHUNK : (tile + 1) * CHUNK]
        total = jnp.zeros((8, CHUNK), F32)
        for chunk in range(count // CHUNK):
            other = column[chunk * CHUNK : (chunk + 1) * CHUNK]
            if chunk < tile:
                before = other <= mine
            elif chunk > tile:
                before = other < mine
            else:
                above = lax.broadcasted_iota(jnp.int32, (CHUNK, CHUNK), 0) < lax.broadcasted_iota(
                    jnp.int32, (CHUNK, CHUNK), 1
                )
                before = jnp.logical_or(other < mine, jnp.logical_and(other == mine, above))
            ones = jnp.where(before, 1.0, 0.0)
            for group in range(CHUNK // 8):
                total = total + ones[group * 8 : group * 8 + 8]
        result.append(jnp.sum(total, axis=0, keepdims=True))
    return jnp.concatenate(result, axis=1)


def moved(values, table):
    rows = values.shape[0]
    stacked = jnp.concatenate(parts(values), axis=0).astype(BF16)
    both = lax.dot_general(
        stacked, table, (((1,), (1,)), ((), ())), preferred_element_type=F32
    )
    return (both[:rows] + both[rows : 2 * rows]) + both[2 * rows :]


def moved_back(values, table):
    both = jnp.dot(doubled(values), table, preferred_element_type=F32)
    return both[:3] + both[8:11]


def chunk_bounds(source_z, target_z, width, low_ref, high_ref):
    chunks = source_z.shape[1] // CHUNK
    tiles = target_z.shape[1] // width

    def edges(values, size, pieces):
        rows = jnp.concatenate([values[:, i * size : (i + 1) * size] for i in range(pieces)], axis=0)
        return jnp.min(rows, axis=1, keepdims=True), jnp.max(rows, axis=1, keepdims=True)

    source_low, source_high = edges(source_z, CHUNK, chunks)
    target_low, target_high = edges(target_z, width, tiles)
    index = lax.broadcasted_iota(jnp.int32, (chunks, 1), 0).astype(F32)
    for tile in range(tiles):
        near = jnp.logical_and(
            source_high >= target_low[tile : tile + 1] - (1.0 + MARGIN),
            source_low <= target_high[tile : tile + 1] + (1.0 + MARGIN),
        )
        low_ref[tile] = jnp.min(jnp.where(near, index, float(chunks))).astype(jnp.int32)
        high_ref[tile] = jnp.max(jnp.where(near, index + 1.0, 0.0)).astype(jnp.int32)


def order_kernel(base_ref, normal_ref, centre_ref, cell_ref, nodes_ref, out_ref, centre_table, nodes_out, node_table):
    def table_of(ref, rank):
        count = rank.shape[1]
        rows = 128
        for start in range(0, count, rows):
            row = lax.broadcasted_iota(jnp.int32, (rows, count), 0).astype(F32) + float(start)
            ref[start : start + rows] = jnp.where(row == rank, 1.0, 0.0).astype(BF16)

    count = centre_ref.shape[1]
    table_of(centre_table, rank_of(centre_ref[2:3]))
    values = jnp.concatenate(
        [
            base_ref[...],
            normal_ref[...],
            centre_ref[...],
            cell_ref[...].astype(F32),
            jnp.zeros((6, count), F32),
        ],
        axis=0,
    )
    out_ref[...] = moved(values, centre_table[...])
    table_of(node_table, rank_of(nodes_ref[2:3]))
    nodes = jnp.concatenate([nodes_ref[...], jnp.zeros((5, nodes_ref.shape[1]), F32)], axis=0)
    nodes_out[...] = moved(nodes, node_table[...])


def ordered(base_shift, normals, centres, wall_cell, near_nodes):
    count, slots = centres.shape[1], near_nodes.shape[1]
    return pl.pallas_call(
        order_kernel,
        out_shape=(
            jax.ShapeDtypeStruct((16, count), F32),
            jax.ShapeDtypeStruct((count, count), BF16),
            jax.ShapeDtypeStruct((8, slots), F32),
            jax.ShapeDtypeStruct((slots, slots), BF16),
        ),
        in_specs=[VMEM] * 5,
        out_specs=(VMEM,) * 4,
        compiler_params=pltpu.CompilerParams(vmem_limit_bytes=SMALL_LIMIT),
        cost_estimate=pl.CostEstimate(flops=ORDER_FLOPS, bytes_accessed=4_000_000, transcendentals=0),
        name="order",
    )(base_shift, normals, centres, wall_cell.reshape(1, -1), near_nodes)


def edge_kernel(even_last, q_ref, w_ref, target, sems):
    count, rows, _ = q_ref.shape

    def move(row):
        copies = []
        for index in range(count + 1):
            source = q_ref.at[index] if index < count else w_ref.at[0]
            copies.append(
                pltpu.make_async_copy(source.at[pl.ds(row, 1)], target.at[pl.ds(index, 1)], sems.at[index])
            )
        for copy in copies:
            copy.start()
        for copy in copies:
            copy.wait()

    core = lax.axis_index("core")

    @pl.when(core == 0)
    def _():
        move(rows - 1 if even_last else 0)

    @pl.when(core != 0)
    def _():
        move(0 if even_last else rows - 1)


def edge_rows(even_last, flow_state, flow_speed):
    count, _, plane = flow_state.shape
    return pl.pallas_call(
        functools.partial(edge_kernel, even_last),
        out_shape=jax.ShapeDtypeStruct((count + 1, plane), F32),
        in_specs=[HBM, HBM],
        out_specs=VMEM,
        scratch_shapes=[pltpu.SemaphoreType.DMA((count + 1,))],
        compiler_params=pltpu.CompilerParams(vmem_limit_bytes=SMALL_LIMIT),
        name="edge_rows",
    )(
        pltpu.with_memory_space_constraint(flow_state, pltpu.HBM),
        pltpu.with_memory_space_constraint(flow_speed, pltpu.HBM),
    )


RATE = 0.5 * FLUX_STEP
PRESSURE = 4


def picked(stacked, chosen, lane):
    high, middle, low = parts(stacked)
    pieces = jnp.concatenate([high, middle, low], axis=1).astype(BF16)
    both = lax.dot_general(pieces, chosen, (((0,), (0,)), ((), ())), preferred_element_type=F32)
    value = (both[:128] + both[128:256]) + both[256:]
    here = lax.broadcasted_iota(jnp.int32, value.shape, 0) == lane
    return jnp.sum(jnp.where(here, value, 0.0), axis=0, keepdims=True)


def stacked_lanes(values):
    return jnp.concatenate([values[:, i : i + 128] for i in range(0, values.shape[1], 128)], axis=0)


def inner_kernel(q_ref, w_ref, sorted_ref, new_hbm, low_ref, high_ref, out_ref, chosen_ref, new_ref, sems):
    count, rows, plane = q_ref.shape
    width = 512
    steps = plane // width
    row = lax.broadcasted_iota(jnp.int32, (rows, width), 0)

    def copy_of(step):
        lanes = pl.ds(pl.multiple_of(step * width, width), width)
        return pltpu.make_async_copy(new_ref.at[:, :, lanes], new_hbm.at[:, :, lanes], sems.at[step])

    def chunk(step, _):
        here = pl.multiple_of(step * width, 128)
        left = pl.multiple_of(lax.rem(here + plane - 128, plane), 128)
        right = pl.multiple_of(lax.rem(here + width, plane), 128)

        def cyclic(ref, index):
            values = ref[index, :, pl.ds(here, width)]
            wide = jnp.concatenate(
                [ref[index, :, pl.ds(left, 128)], values, ref[index, :, pl.ds(right, 128)]], axis=1
            )
            before = pltpu.roll(wide, 1, 1)[:, 128 : 128 + width]
            after = pltpu.roll(wide, width + 255, 1)[:, 128 : 128 + width]
            return values, before, after

        w = w_ref[0, :, pl.ds(here, width)]
        face_low = jnp.where(row == 0, 0.0, RATE * (pltpu.roll(w, 1, 0) + w))
        face_high = jnp.where(row == rows - 1, 0.0, RATE * (w + pltpu.roll(w, rows - 1, 0)))
        speed, speed_before, speed_after = cyclic(w_ref, 1)
        face_left = RATE * (speed_before + speed)
        face_right = RATE * (speed + speed_after)
        low_in = jnp.maximum(face_low, 0.0)
        high_out = jnp.minimum(face_high, 0.0)
        left_in = jnp.maximum(face_left, 0.0)
        right_out = jnp.minimum(face_right, 0.0)
        keep = 1.0 - (
            (jnp.maximum(face_high, 0.0) - jnp.minimum(face_low, 0.0))
            + (jnp.maximum(face_right, 0.0) - jnp.minimum(face_left, 0.0))
        )
        for index in range(count):
            values, before, after = cyclic(q_ref, index)
            new = (
                keep * values
                + low_in * pltpu.roll(values, 1, 0)
                - high_out * pltpu.roll(values, rows - 1, 0)
                + left_in * before
                - right_out * after
            )
            new_ref[index, :, pl.ds(here, width)] = new
            low_ref[index : index + 1, pl.ds(here, width)] = new[0:1]
            high_ref[index : index + 1, pl.ds(here, width)] = new[rows - 1 : rows]
        copy_of(step).start()
        return 0

    lax.fori_loop(0, steps, chunk, 0)

    cells = sorted_ref[9:10].astype(jnp.int32)
    cell_row = cells // plane
    column = cells - cell_row * plane
    group = column // 128
    lane = column - group * 128
    place = group * rows + cell_row
    centres = cells.shape[1]
    lanes = plane // 128
    chosen = (lax.broadcasted_iota(jnp.int32, (rows * lanes, centres), 0) == place).astype(F32).astype(BF16)
    chosen_ref[...] = chosen
    load = picked(stacked_lanes(new_ref[PRESSURE]), chosen, lane)
    out_ref[...] = jnp.concatenate(
        [
            sorted_ref[0:3] + sorted_ref[3:6] * load,
            sorted_ref[3:9],
            lane.astype(F32),
            jnp.zeros((6, centres), F32),
        ],
        axis=0,
    )
    for step in range(steps):
        copy_of(step).wait()


def inner_flux(flow_state, flow_speed, in_order):
    count, rows, plane = flow_state.shape
    centres = in_order.shape[1]
    edge = jax.ShapeDtypeStruct((count, plane), F32)
    return pl.pallas_call(
        inner_kernel,
        out_shape=(
            pltpu.HBM(flow_state.shape, F32),
            edge,
            edge,
            jax.ShapeDtypeStruct((16, centres), F32),
            jax.ShapeDtypeStruct((rows * plane // 128, centres), BF16),
        ),
        in_specs=[VMEM] * 3,
        out_specs=(HBM, VMEM, VMEM, VMEM, VMEM),
        scratch_shapes=[pltpu.VMEM(flow_state.shape, F32), pltpu.SemaphoreType.DMA((plane // 512,))],
        compiler_params=pltpu.CompilerParams(vmem_limit_bytes=SMALL_LIMIT),
        cost_estimate=pl.CostEstimate(flops=20_000_000, bytes_accessed=4_000_000, transcendentals=0),
        name="inner_flux",
    )(flow_state, flow_speed, in_order)


def outer_kernel(
    send_a, send_b, from_a, from_b, low_ref, high_ref, base_ref, chosen_ref, out_ref, new_low, new_high, both_ref
):
    count, plane = low_ref.shape
    rows = both_ref.shape[0]
    even = lax.axis_index("core") == 0
    own_low = jnp.where(even, send_b[...], send_a[...])
    own_high = jnp.where(even, send_a[...], send_b[...])
    below = jnp.where(even, from_b[...], from_a[...])
    above = jnp.where(even, from_a[...], from_b[...])

    def flux(first, second):
        face = RATE * (first[count : count + 1] + second[count : count + 1])
        return jnp.maximum(face, 0.0) * first[:count] + jnp.minimum(face, 0.0) * second[:count]

    low = flux(below, own_low)
    high = flux(own_high, above)
    new_low[...] = low_ref[...] + low
    new_high[...] = high_ref[...] - high
    row = lax.broadcasted_iota(jnp.int32, (rows, plane), 0)
    zero = jnp.zeros((rows, plane), F32)
    added = jnp.where(row == 0, low[PRESSURE : PRESSURE + 1], zero)
    added = added - jnp.where(row == rows - 1, high[PRESSURE : PRESSURE + 1], zero)
    both_ref[...] = added
    base = base_ref[...]
    load = picked(stacked_lanes(both_ref[...]), chosen_ref[...], base[9:10].astype(jnp.int32))
    centres = base.shape[1]
    packed = jnp.concatenate([base[0:3] + base[3:6] * load, base[6:9], jnp.zeros((2, centres), F32)], axis=0)
    for chip in range(out_ref.shape[0]):
        out_ref[chip] = packed


def right_side(chips, rows, send_a, send_b, from_a, from_b, low, high, base, chosen):
    edge = jax.ShapeDtypeStruct(low.shape, F32)
    return pl.pallas_call(
        outer_kernel,
        out_shape=(jax.ShapeDtypeStruct((chips, 8, base.shape[1]), F32), edge, edge),
        in_specs=[VMEM] * 8,
        out_specs=(VMEM,) * 3,
        scratch_shapes=[pltpu.VMEM((rows, low.shape[1]), F32)],
        compiler_params=pltpu.CompilerParams(vmem_limit_bytes=SMALL_LIMIT),
        name="outer_flux",
    )(send_a, send_b, from_a, from_b, low, high, base, chosen)


def block_of(mine_ref, other_ref, block, core):
    chip = lax.div(block, 2)
    own = lax.rem(block, 2) == core
    return jnp.where(own, mine_ref[chip], other_ref[chip])


def powers_kernel(
    count, mine_ref, other_ref, new_low, new_high, new_in, out_ref, new_out,
    source_side, target_side, vector, image, tables, low_ref, high_ref, sems,
):
    del new_in
    rows_per_block = new_out.shape[1]
    copies = [
        pltpu.make_async_copy(new_low, new_out.at[:, 0], sems.at[0]),
        pltpu.make_async_copy(new_high, new_out.at[:, rows_per_block - 1], sems.at[1]),
    ]
    for copy in copies:
        copy.start()
    size = mine_ref.shape[2]
    chip, core = lax.axis_index("chip"), lax.axis_index("core")
    me = chip * 2 + core
    slots, width, reach = 6, 256, 6
    span = reach * CHUNK
    total = slots * size
    origin = lax.div(me * 2, 5).astype(F32)
    value_row = lax.broadcasted_iota(jnp.int32, (8, size), 0) < 3

    live, zeroth, third = [], [], []
    for slot in range(slots):
        block = me + slot - 2
        valid = jnp.logical_and(block >= 0, block < count)
        live.append(valid)
        data = block_of(mine_ref, other_ref, jnp.clip(block, 0, count - 1), core)
        zeroth.append(jnp.where(jnp.logical_and(value_row, valid), data, 0.0))
        middle = (block.astype(F32) + 0.5) * DEPTH
        raw = jnp.concatenate([data[3:5], jnp.where(valid, data[5:6], middle)], axis=0)
        points = local_points(raw, origin)
        third.append(points[2:3])
        source, target = sides(points)
        source_side[slot * size : (slot + 1) * size] = source.T.astype(BF16)
        target_side[:, slot * size : (slot + 1) * size] = target.astype(BF16)
    far = (lax.broadcasted_iota(jnp.int32, (span, 48), 1) == 3).astype(F32) * 4096.0
    source_side[total:] = far.astype(BF16)
    vector[:, total:] = jnp.zeros((16, span), BF16)
    heights = jnp.concatenate(third, axis=1)
    chunk_bounds(heights, heights[:, size : 5 * size], width, low_ref, high_ref)
    tiles = 4 * size // width

    def steps_of(tile):
        return lax.div(high_ref[tile] - low_ref[tile] + (reach - 1), reach)

    most = steps_of(0)
    for tile in range(1, tiles):
        most = jnp.maximum(most, steps_of(tile))

    skipped, per_tile, mine_first = size // CHUNK, width // CHUNK, size // width
    per_block = size // width

    def tiles_up_to(chunk):
        return lax.div(chunk - skipped + (per_tile - 1), per_tile)

    second_end = high_ref[mine_first]
    for tile in range(mine_first + 1, 2 * mine_first):
        second_end = jnp.maximum(second_end, high_ref[tile])
    second_end = jnp.clip(tiles_up_to(second_end), 2 * per_block, 3 * per_block)
    read_low, read_high = low_ref[mine_first], high_ref[mine_first]
    for tile in range(mine_first + 1, 3 * per_block):
        read = tile < second_end
        read_low = jnp.minimum(read_low, jnp.where(read, low_ref[tile], read_low))
        read_high = jnp.maximum(read_high, jnp.where(read, high_ref[tile], read_high))
    first_start = jnp.clip(lax.div(jnp.maximum(read_low - skipped, 0), per_tile), 0, per_block)
    first_end = jnp.clip(tiles_up_to(read_high), second_end, tiles)
    same = lax.broadcasted_iota(jnp.int32, (CHUNK, CHUNK), 0) == lax.broadcasted_iota(
        jnp.int32, (CHUNK, CHUNK), 1
    )

    def build(tile, step):
        lanes = pl.ds(pl.multiple_of(tile * width + size, width), width)
        chunk = low_ref[tile] + step * reach
        rows = pl.ds(pl.multiple_of(chunk * CHUNK, CHUNK), span)
        table = quarter_kernel(source_side[rows], target_side[:, lanes])
        high = table.astype(BF16)
        tables[tile, step, :span] = high
        tables[tile, step, span:] = (table - high.astype(F32)).astype(BF16)
        for piece in range(width // CHUNK):
            place = (tile * width + size) // CHUNK + piece - chunk
            inside = jnp.logical_and(place >= 0, place < reach)
            place = jnp.clip(place, 0, reach - 1)
            for half in range(2):
                at = pl.ds(pl.multiple_of(place * CHUNK + half * span, CHUNK), CHUNK)
                columns = slice(piece * CHUNK, (piece + 1) * CHUNK)
                old = tables[tile, step, at, columns]
                tables[tile, step, at, columns] = jnp.where(jnp.logical_and(same, inside), 0.0, old.astype(F32)).astype(BF16)

    def one(tile, step):
        lanes = pl.ds(pl.multiple_of((low_ref[tile] + step * reach) * CHUNK, CHUNK), span)
        window = vector[:, lanes]
        return jnp.dot(jnp.concatenate([window, window], axis=1), tables[tile, step], preferred_element_type=F32)

    def lanes_of(tile):
        return pl.ds(pl.multiple_of(tile * width, width), width)

    def further(first, last):
        @pl.when(most > 1)
        def _():
            def of_tile(tile, _):
                def add(step, _):
                    image[:, lanes_of(tile)] += one(tile, step)
                    return 0

                return lax.fori_loop(1, steps_of(tile), add, 0)

            lax.fori_loop(first, last, of_tile, 0)

    def image_of(slot):
        both = image[:, (slot - 1) * size : slot * size]
        return jnp.where(live[slot], 4.0 * (both[:8] + both[8:]), 0.0)

    def power(slots, end):
        first, last = (slots[0] - 1) * per_block, slots[-1] * per_block
        for tile in range(first, last):
            here = slice(tile * width, (tile + 1) * width)
            if tile < 2 * per_block:
                image[:, here] = one(tile, 0)
            else:
                image[:, here] = jnp.zeros((16, width), F32)

                @pl.when(tile < end)
                def _(tile=tile, here=here):
                    image[:, here] = one(tile, 0)

        further(first, end)
        return {slot: image_of(slot) for slot in slots}

    def hold(values, slot):
        vector[:, slot * size : (slot + 1) * size] = doubled(values)

    for slot in range(slots):
        hold(zeroth[slot], slot)

    for tile in (*range(per_block), *range(2 * per_block, tiles)):
        image[:, tile * width : (tile + 1) * width] = jnp.zeros((16, width), F32)

    def tile_step(tile, _):
        before = jnp.maximum(tile - 1, first_start)
        image[:, lanes_of(before)] = one(before, 0)
        build(tile, 0)
        return 0

    lax.fori_loop(first_start, first_end, tile_step, 0)
    image[:, lanes_of(first_end - 1)] = one(first_end - 1, 0)

    @pl.when(most > 1)
    def _():
        def of_tile(tile, _):
            def more(step, _):
                build(tile, step)
                return 0

            return lax.fori_loop(1, steps_of(tile), more, 0)

        lax.fori_loop(first_start, first_end, of_tile, 0)

    further(first_start, first_end)
    first = {slot: image_of(slot) for slot in range(1, 5)}
    for slot in range(1, 5):
        hold(first[slot], slot)
    second = power([2, 3], second_end)
    hold(jnp.zeros((8, size), F32), 1)
    hold(second[2], 2)
    hold(2.0 * second[3], 3)
    last = power([2], 2 * per_block)[2]

    def inner(left, right):
        return jnp.sum(left * right, axis=1, keepdims=True)

    moments = [
        inner(zeroth[2], zeroth[2]),
        inner(zeroth[2], first[2]),
        inner(first[2], first[2]),
        inner(first[2], second[2]),
        inner(second[2], second[2]),
        inner(second[2], last),
    ]
    lane = lax.broadcasted_iota(jnp.int32, (8, 128), 1)
    packed = jnp.zeros((8, 128), F32)
    for index, moment in enumerate(moments):
        packed = jnp.where(lane == index, moment, packed)
    values = jnp.concatenate([first[2][:3], second[2][:3], jnp.zeros((2, size), F32)], axis=0)
    for index in range(out_ref.shape[0]):
        out_ref[index, :, :size] = values
        out_ref[index, :, size:] = packed
    for copy in copies:
        copy.wait()


def powers(mine, other, new_low, new_high, new_flow, count):
    chips, _, size = mine.shape
    tiles = 4 * size // 256
    steps = (6 * size // CHUNK + 5) // 6
    return pl.pallas_call(
        functools.partial(powers_kernel, count),
        out_shape=(
            jax.ShapeDtypeStruct((chips, 8, size + 128), F32),
            pltpu.HBM(new_flow.shape, F32),
        ),
        in_specs=[VMEM] * 4 + [HBM],
        out_specs=(VMEM, HBM),
        scratch_shapes=[
            pltpu.VMEM((6 * size + 6 * CHUNK, 48), BF16),
            pltpu.VMEM((48, 6 * size), BF16),
            pltpu.VMEM((16, 6 * size + 6 * CHUNK), BF16),
            pltpu.VMEM((16, 4 * size), F32),
            pltpu.VMEM((tiles, steps, 12 * CHUNK, 256), BF16),
            pltpu.SMEM((tiles,), jnp.int32),
            pltpu.SMEM((tiles,), jnp.int32),
            pltpu.SemaphoreType.DMA((2,)),
        ],
        input_output_aliases={4: 1},
        compiler_params=pltpu.CompilerParams(vmem_limit_bytes=BIG_LIMIT),
        name="powers",
    )(mine, other, new_low, new_high, pltpu.with_memory_space_constraint(new_flow, pltpu.HBM))


def ratio(top, bottom):
    safe = bottom > 0.0
    return jnp.where(safe, top / jnp.where(safe, bottom, 1.0), 0.0)


def weights_of(moments):
    lost = jnp.zeros_like(moments[0])

    def inner(left, right):
        total = size = None
        for i, a in enumerate(left):
            for j, c in enumerate(right):
                term = a * c * moments[i + j]
                total = term if total is None else total + term
                size = jnp.abs(term) if size is None else size + jnp.abs(term)
        return total, jnp.where(total > LOSS * size, 0.0, jnp.where(size > 0.0, 1.0, 0.0))

    one = jnp.ones_like(moments[0])
    residual, search = [one], [one]
    coefficients = [0.0 * one] * ITERS
    energy = moments[0]
    for step in range(ITERS):
        image = [CENTRE_SHIFT * value for value in search] + [0.0 * one]
        for index, value in enumerate(search):
            image[index + 1] = image[index + 1] + value
        along, bad = inner(search, image)
        lost = lost + bad
        length = ratio(energy, along)
        for index, value in enumerate(search):
            coefficients[index] = coefficients[index] + length * value
        if step == ITERS - 1:
            break
        longer = residual + [0.0 * one]
        residual = [value - length * other for value, other in zip(longer, image)]
        fresh, bad = inner(residual, residual)
        lost = lost + bad
        scale = ratio(fresh, energy)
        search = [
            value + scale * (search[index] if index < len(search) else 0.0)
            for index, value in enumerate(residual)
        ]
        energy = fresh
    return coefficients, lost


REACH = 7


def bounds_of(source_z, target_z):
    chunks = source_z.shape[1] // CHUNK
    tiles = target_z.shape[1] // CHUNK

    def edges(values, pieces):
        rows = jnp.concatenate([values[:, i * CHUNK : (i + 1) * CHUNK] for i in range(pieces)], axis=0)
        return jnp.min(rows, axis=1, keepdims=True), jnp.max(rows, axis=1, keepdims=True)

    def across(values):
        return jnp.broadcast_to(values, (tiles, 128)).T[0:1]

    source_low, source_high = edges(source_z, chunks)
    target_low, target_high = edges(target_z, tiles)
    near = jnp.logical_and(
        source_high >= across(target_low) - (1.0 + MARGIN), source_low <= across(target_high) + (1.0 + MARGIN)
    )
    index = lax.broadcasted_iota(jnp.int32, (chunks, tiles), 0).astype(F32)
    low = jnp.min(jnp.where(near, index, float(chunks)), axis=0, keepdims=True)
    high = jnp.max(jnp.where(near, index + 1.0, 0.0), axis=0, keepdims=True)
    return jnp.concatenate([low, high], axis=0)


def first_listed(tile_ref, me):
    return tile_ref[pl.ds(me, 1), :][0, 0]


def scalars_of(bound_ref, low_ref, step_ref):
    bounds = bound_ref[...].astype(jnp.int32)
    most = 0
    for tile in range(bounds.shape[1]):
        low = bounds[0, tile]
        steps = lax.div(bounds[1, tile] - low + (REACH - 1), REACH)
        low_ref[tile] = low
        step_ref[tile] = steps
        most = jnp.maximum(most, steps)
    return most


def near_table(source_ref, target_ref, low_ref, tile, step):
    start = pl.multiple_of((low_ref[tile] + step * REACH) * CHUNK, CHUNK)
    lanes = pl.ds(pl.multiple_of(tile * CHUNK, CHUNK), CHUNK)
    return doubled(quarter_kernel(source_ref[pl.ds(start, REACH * CHUNK)], target_ref[:, lanes]))


EARLY = 2


def points_kernel(
    tile_ref, mine_ref, other_ref, nodes_ref, source_ref, target_ref, bound_ref, table_ref, low_ref, step_ref
):
    size = mine_ref.shape[2]
    core = lax.axis_index("core")
    me = lax.axis_index("chip") * 2 + core
    listed = tile_ref.shape[1]
    start = first_listed(tile_ref, me)
    origin = lax.div((start + 2) * 2, 5).astype(F32)
    third = []
    for index in range(listed):
        data = block_of(mine_ref, other_ref, start + index, core)
        points = local_points(data[3:6], origin)
        third.append(points[2:3])
        source, _ = sides(points)
        source_ref[index * size : (index + 1) * size] = source.T.astype(BF16)
    span = REACH * CHUNK
    far = (lax.broadcasted_iota(jnp.int32, (span, 48), 1) == 3).astype(F32) * 4096.0
    source_ref[listed * size :] = far.astype(BF16)
    points = local_points(nodes_ref[0:3], origin)
    _, target = sides(points)
    target_ref[...] = target.astype(BF16)
    bound_ref[...] = bounds_of(jnp.concatenate(third, axis=1), points[2:3])
    scalars_of(bound_ref, low_ref, step_ref)
    for tile in range(EARLY):
        table_ref[tile] = near_table(source_ref, target_ref, low_ref, tile, 0)


def near_points(tile_blocks, mine, other, nodes):
    size = mine.shape[2]
    slots = nodes.shape[1]
    listed = tile_blocks.shape[1]
    return pl.pallas_call(
        points_kernel,
        out_shape=(
            jax.ShapeDtypeStruct((listed * size + REACH * CHUNK, 48), BF16),
            jax.ShapeDtypeStruct((48, slots), BF16),
            jax.ShapeDtypeStruct((2, slots // CHUNK), F32),
            jax.ShapeDtypeStruct((EARLY, 2 * REACH * CHUNK, CHUNK), BF16),
        ),
        in_specs=[VMEM] * 4,
        out_specs=(VMEM,) * 4,
        scratch_shapes=[
            pltpu.SMEM((slots // CHUNK,), jnp.int32),
            pltpu.SMEM((slots // CHUNK,), jnp.int32),
        ],
        compiler_params=pltpu.CompilerParams(vmem_limit_bytes=SMALL_LIMIT),
        cost_estimate=pl.CostEstimate(flops=1_000_000, bytes_accessed=1_000_000, transcendentals=0),
        name="near_points",
    )(tile_blocks, mine, other, nodes)


def near_kernel(
    tile_ref, count_ref, bound_ref, mine_ref, other_ref, mine_power, other_power, source_side, target_side,
    table_ref, centre_table, node_table, coef_ref, shift_ref, lost_ref, vector, result, low_ref, step_ref,
):
    size = mine_ref.shape[2]
    slots = target_side.shape[1]
    chips = mine_ref.shape[0]
    core = lax.axis_index("core")
    me = lax.axis_index("chip") * 2 + core
    listed = tile_ref.shape[1]
    start_block = first_listed(tile_ref, me)
    width = CHUNK
    tiles = slots // width
    span = REACH * CHUNK
    total = listed * size

    most = scalars_of(bound_ref, low_ref, step_ref)
    summed = mine_power[0, :, size:] + other_power[0, :, size:]
    for index in range(1, chips):
        summed = summed + (mine_power[index, :, size:] + other_power[index, :, size:])
    weights, lost = weights_of([summed[:, index : index + 1] for index in range(6)])
    lost_ref[...] = jnp.broadcast_to(jnp.max(lost[:3], axis=0, keepdims=True), (1, 128))

    def coefficients_of(block):
        data = block_of(mine_ref, other_ref, block, core)
        power = block_of(mine_power, other_power, block, core)[:, :size]
        values = weights[0] * data + weights[1] * power + weights[2] * pltpu.roll(power, 5, 0)
        keep = lax.broadcasted_iota(jnp.int32, (8, size), 0) < 3
        return jnp.where(keep, values, 0.0)

    for index in range(listed):
        vector[:, index * size : (index + 1) * size] = doubled(coefficients_of(start_block + index))
    vector[:, total:] = jnp.zeros((16, span), BF16)
    coef_ref[...] = moved_back(coefficients_of(me), centre_table[...])

    def lanes_of(tile):
        return pl.ds(pl.multiple_of(tile * width, width), width)

    def one(tile, step, table):
        start = pl.multiple_of((low_ref[tile] + step * REACH) * CHUNK, CHUNK)
        window = vector[:, pl.ds(start, span)]
        return jnp.dot(jnp.concatenate([window, window], axis=1), table, preferred_element_type=F32)

    for tile in range(EARLY):
        result[:, tile * width : (tile + 1) * width] = one(tile, 0, table_ref[tile])

    def two_tiles(step, _):
        for piece in range(2):
            tile = EARLY + 2 * step + piece
            table = near_table(source_side, target_side, low_ref, tile, 0)
            result[:, lanes_of(tile)] = one(tile, 0, table)
        return 0

    lax.fori_loop(0, (tiles - EARLY) // 2, two_tiles, 0)

    @pl.when(most > 1)
    def _():
        def of_tile(tile, _):
            def add(step, _):
                table = near_table(source_side, target_side, low_ref, tile, step)
                result[:, lanes_of(tile)] += one(tile, step, table)
                return 0

            return lax.fori_loop(1, step_ref[tile], add, 0)

        lax.fori_loop(0, tiles, of_tile, 0)

    lane = lax.broadcasted_iota(jnp.int32, count_ref.shape, 1)
    live = jnp.sum(jnp.where(lane == me, count_ref[...], 0).astype(F32), axis=1, keepdims=True)
    slot = lax.broadcasted_iota(jnp.int32, (3, slots), 1).astype(F32)
    both = result[...]
    shift = moved_back(4.0 * (both[:8] + both[8:]), node_table[...])
    shift_ref[...] = jnp.where(slot < live, shift, 0.0)


def near_body(tile_blocks, near_count, bounds, mine, other, mine_power, other_power, sources, targets, tables, centre_table, node_table):
    size = mine.shape[2]
    slots = targets.shape[1]
    total = tile_blocks.shape[1] * size
    return pl.pallas_call(
        near_kernel,
        out_shape=(
            jax.ShapeDtypeStruct((3, size), F32),
            jax.ShapeDtypeStruct((3, slots), F32),
            jax.ShapeDtypeStruct((1, 128), F32),
        ),
        in_specs=[VMEM] * 12,
        out_specs=(VMEM,) * 3,
        scratch_shapes=[
            pltpu.VMEM((16, total + REACH * CHUNK), BF16),
            pltpu.VMEM((16, slots), F32),
            pltpu.SMEM((slots // CHUNK,), jnp.int32),
            pltpu.SMEM((slots // CHUNK,), jnp.int32),
        ],
        compiler_params=pltpu.CompilerParams(vmem_limit_bytes=SMALL_LIMIT),
        name="near_body",
    )(
        tile_blocks, near_count.reshape(1, -1), bounds, mine, other, mine_power, other_power, sources, targets,
        tables, centre_table, node_table,
    )


def gathered(values, partner):
    mine = lax.all_to_all(values, "chip", 0, 0)
    return mine, lax.ppermute(mine, SLAB, partner)


def step_by_step(count, right, centres, tile_blocks, near_count, near_nodes):
    size = centres.shape[1]
    up = [(i, i + 1) for i in range(count - 1)]
    down = [(i + 1, i) for i in range(count - 1)]

    def widened(values):
        return jnp.concatenate([lax.ppermute(values, SLAB, up), values, lax.ppermute(values, SLAB, down)], axis=1)

    def table_of(sources, targets):
        scaled = jnp.sqrt(sum((sources[k][:, None] - targets[k][None, :]) ** 2 for k in range(3))) / SUPPORT
        inside = jnp.maximum(1.0 - scaled, 0.0)
        square_in = inside * inside
        return square_in * square_in * (4.0 * scaled + 1.0)

    def total(left, other):
        return lax.psum(jnp.sum(left * other, axis=1), SLAB)

    def product(values, table):
        return jnp.dot(values, table, precision=lax.Precision.HIGHEST, preferred_element_type=F32)

    around = widened(centres)

    def step(_, held):
        coefficients, residual, search, energy = held
        image = product(widened(search), table_of(around, centres)) + DIAG_SHIFT * search
        length = energy / total(search, image)
        coefficients = coefficients + length[:, None] * search
        residual = residual - length[:, None] * image
        fresh = total(residual, residual)
        return coefficients, residual, residual + (fresh / energy)[:, None] * search, fresh

    coefficients = lax.fori_loop(0, ITERS, step, (jnp.zeros_like(right), right, right, total(right, right)))[0]
    everywhere = lax.all_gather(jnp.concatenate([centres, coefficients], axis=0), SLAB, axis=1, tiled=True)
    me = lax.axis_index(SLAB)
    slots = near_nodes.shape[1]

    def listed(index, sums):
        data = lax.dynamic_slice_in_dim(everywhere, tile_blocks[me, index] * size, size, 1)
        return sums + product(data[3:], table_of(data[:3], near_nodes))

    shift = lax.fori_loop(0, tile_blocks.shape[1], listed, jnp.zeros((3, slots), F32))
    live = lax.iota(jnp.int32, slots) < near_count[me]
    return coefficients, jnp.where(live[None, :], shift, 0.0)


def shards(
    count,
    flow_state,
    flow_speed,
    wall_cell,
    base_shift,
    normals,
    centres,
    tile_blocks,
    near_count,
    near_nodes,
):
    partner = [(i, i ^ 1) for i in range(count)]
    across = [(i, i + 1) for i in range(1, count - 1, 2)]
    across = across + [(j, i) for i, j in across]
    chips, rows = count // 2, flow_state.shape[1]
    send_b = edge_rows(False, flow_state, flow_speed)
    from_b = lax.ppermute(send_b, SLAB, across)
    send_a = edge_rows(True, flow_state, flow_speed)
    from_a = lax.ppermute(send_a, SLAB, partner)
    in_order, centre_table, nodes, node_table = ordered(base_shift, normals, centres, wall_cell, near_nodes)
    new_flow, low, high, base, chosen = inner_flux(flow_state, flow_speed, in_order)
    packed, low, high = right_side(chips, rows, send_a, send_b, from_a, from_b, low, high, base, chosen)
    mine, other = gathered(packed, partner)
    power, new_flow = powers(mine, other, low, high, new_flow, count)
    mine_power, other_power = gathered(power, partner)
    sources, targets, bounds, tables = near_points(tile_blocks, mine, other, nodes)
    coefficients, node_shift, lost = near_body(
        tile_blocks, near_count, bounds, mine, other, mine_power, other_power, sources, targets,
        tables, centre_table, node_table,
    )

    def again(held):
        one = jnp.where(held[0][0, 0] > 0.0, 1.0, 0.0)
        whole = one.astype(jnp.int32)
        own = packed[0] * one
        found, shifted = step_by_step(
            count, own[0:3], own[3:6], tile_blocks * whole, near_count * whole, near_nodes * one
        )
        back = jnp.dot(found, centre_table.astype(F32) * one, precision=lax.Precision.HIGHEST)
        return jnp.zeros_like(held[0]), back, shifted

    _, coefficients, node_shift = lax.while_loop(
        lambda held: held[0][0, 0] > 0.0, again, (lost, coefficients, node_shift)
    )
    return new_flow, coefficients, node_shift


def solution(mesh):
    groups, count = mesh.shape["groups"], mesh.shape["slab"]
    split = Mesh(mesh.devices.reshape(groups, count // 2, 2), ("groups",) + SLAB)
    in_specs = (
        P("groups", SLAB, None),
        P("groups", SLAB, None),
        P(("groups",) + SLAB),
        P("groups", SLAB),
        P("groups", SLAB),
        P("groups", SLAB),
        P("groups", None),
        P("groups"),
        P("groups", SLAB),
    )
    out_specs = (P("groups", SLAB, None), P("groups", SLAB), P("groups", SLAB))
    return jax.shard_map(
        functools.partial(shards, count), mesh=split, in_specs=in_specs, out_specs=out_specs, check_vma=False
    )
```

```python
import functools

import jax
import jax.numpy as jnp
from jax import lax
from jax.experimental import pallas as pl
from jax.experimental.pallas import tpu as pltpu
from jax.sharding import Mesh
from jax.sharding import PartitionSpec as P


FLUX_STEP = 0.2
SUPPORT = 0.15
DIAG_SHIFT = 0.5
CENTRE_SHIFT = DIAG_SHIFT + 1.0
TINY = 1e-12
ITERS = 3
LOSS = 0.01
DEPTH = 0.4
CHUNK = 128
MARGIN = 1e-3
ORDER_FLOPS = 2_000_000_000
BIG_LIMIT = 48 * 1024 * 1024
SMALL_LIMIT = 16 * 1024 * 1024

F32 = jnp.float32
BF16 = jnp.bfloat16
SLAB = ("chip", "core")
VMEM = pl.BlockSpec(memory_space=pltpu.VMEM)
SMEM = pl.BlockSpec(memory_space=pltpu.SMEM)
HBM = pl.BlockSpec(memory_space=pltpu.HBM)


def parts(values):
    first = values.astype(BF16).astype(F32)
    rest = values - first
    second = rest.astype(BF16).astype(F32)
    return first, second, rest - second


def doubled(values):
    high = values.astype(BF16)
    return jnp.concatenate([high, (values - high.astype(F32)).astype(BF16)], axis=0)


def sides(points):
    count = points.shape[1]
    squares = jnp.sum(points * points, axis=0, keepdims=True)
    one = jnp.ones((1, count), F32)
    zero = jnp.zeros((3, count), F32)
    a, b, c = parts(jnp.concatenate([points, squares, one, zero], axis=0))
    d, e, f = parts(jnp.concatenate([-2.0 * points, one, squares, zero], axis=0))
    return jnp.concatenate([a, a, b, a, c, b], axis=0), jnp.concatenate([d, e, d, f, d, e], axis=0)


def quarter_kernel(sources, targets):
    squared = jnp.maximum(jnp.dot(sources, targets, preferred_element_type=F32), TINY)
    inside = jnp.maximum(1.0 - squared * lax.rsqrt(squared), 0.0)
    square_in = inside * inside
    return square_in * square_in * (1.25 - inside)


def local_points(raw, origin):
    x = (raw[0:2] - 0.5) * (1.0 / SUPPORT)
    return jnp.concatenate([x, (raw[2:3] - origin) * (1.0 / SUPPORT)], axis=0)


def rank_of(values):
    count = values.shape[1]
    column = jnp.broadcast_to(values, (8, count)).T[:, 0:1]
    result = []
    for tile in range(count // CHUNK):
        mine = values[:, tile * CHUNK : (tile + 1) * CHUNK]
        total = jnp.zeros((8, CHUNK), F32)
        for chunk in range(count // CHUNK):
            other = column[chunk * CHUNK : (chunk + 1) * CHUNK]
            if chunk < tile:
                before = other <= mine
            elif chunk > tile:
                before = other < mine
            else:
                above = lax.broadcasted_iota(jnp.int32, (CHUNK, CHUNK), 0) < lax.broadcasted_iota(
                    jnp.int32, (CHUNK, CHUNK), 1
                )
                before = jnp.logical_or(other < mine, jnp.logical_and(other == mine, above))
            ones = jnp.where(before, 1.0, 0.0)
            for group in range(CHUNK // 8):
                total = total + ones[group * 8 : group * 8 + 8]
        result.append(jnp.sum(total, axis=0, keepdims=True))
    return jnp.concatenate(result, axis=1)


def moved(values, table):
    rows = values.shape[0]
    stacked = jnp.concatenate(parts(values), axis=0).astype(BF16)
    both = lax.dot_general(
        stacked, table, (((1,), (1,)), ((), ())), preferred_element_type=F32
    )
    return (both[:rows] + both[rows : 2 * rows]) + both[2 * rows :]


def moved_back(values, table):
    both = jnp.dot(doubled(values), table, preferred_element_type=F32)
    return both[:3] + both[8:11]


def chunk_bounds(source_z, target_z, width, low_ref, high_ref):
    chunks = source_z.shape[1] // CHUNK
    tiles = target_z.shape[1] // width

    def edges(values, size, pieces):
        rows = jnp.concatenate([values[:, i * size : (i + 1) * size] for i in range(pieces)], axis=0)
        return jnp.min(rows, axis=1, keepdims=True), jnp.max(rows, axis=1, keepdims=True)

    source_low, source_high = edges(source_z, CHUNK, chunks)
    target_low, target_high = edges(target_z, width, tiles)
    index = lax.broadcasted_iota(jnp.int32, (chunks, 1), 0).astype(F32)
    for tile in range(tiles):
        near = jnp.logical_and(
            source_high >= target_low[tile : tile + 1] - (1.0 + MARGIN),
            source_low <= target_high[tile : tile + 1] + (1.0 + MARGIN),
        )
        low_ref[tile] = jnp.min(jnp.where(near, index, float(chunks))).astype(jnp.int32)
        high_ref[tile] = jnp.max(jnp.where(near, index + 1.0, 0.0)).astype(jnp.int32)


def order_kernel(base_ref, normal_ref, centre_ref, cell_ref, nodes_ref, out_ref, centre_table, nodes_out, node_table):
    def table_of(ref, rank):
        count = rank.shape[1]
        rows = 128
        for start in range(0, count, rows):
            row = lax.broadcasted_iota(jnp.int32, (rows, count), 0).astype(F32) + float(start)
            ref[start : start + rows] = jnp.where(row == rank, 1.0, 0.0).astype(BF16)

    count = centre_ref.shape[1]
    table_of(centre_table, rank_of(centre_ref[2:3]))
    values = jnp.concatenate(
        [
            base_ref[...],
            normal_ref[...],
            centre_ref[...],
            cell_ref[...].astype(F32),
            jnp.zeros((6, count), F32),
        ],
        axis=0,
    )
    out_ref[...] = moved(values, centre_table[...])
    table_of(node_table, rank_of(nodes_ref[2:3]))
    nodes = jnp.concatenate([nodes_ref[...], jnp.zeros((5, nodes_ref.shape[1]), F32)], axis=0)
    nodes_out[...] = moved(nodes, node_table[...])


def ordered(base_shift, normals, centres, wall_cell, near_nodes):
    count, slots = centres.shape[1], near_nodes.shape[1]
    return pl.pallas_call(
        order_kernel,
        out_shape=(
            jax.ShapeDtypeStruct((16, count), F32),
            jax.ShapeDtypeStruct((count, count), BF16),
            jax.ShapeDtypeStruct((8, slots), F32),
            jax.ShapeDtypeStruct((slots, slots), BF16),
        ),
        in_specs=[VMEM] * 5,
        out_specs=(VMEM,) * 4,
        compiler_params=pltpu.CompilerParams(vmem_limit_bytes=SMALL_LIMIT),
        cost_estimate=pl.CostEstimate(flops=ORDER_FLOPS, bytes_accessed=4_000_000, transcendentals=0),
        name="order",
    )(base_shift, normals, centres, wall_cell.reshape(1, -1), near_nodes)


def edge_kernel(even_last, q_ref, w_ref, target, sems):
    count, rows, _ = q_ref.shape

    def move(row):
        copies = []
        for index in range(count + 1):
            source = q_ref.at[index] if index < count else w_ref.at[0]
            copies.append(
                pltpu.make_async_copy(source.at[pl.ds(row, 1)], target.at[pl.ds(index, 1)], sems.at[index])
            )
        for copy in copies:
            copy.start()
        for copy in copies:
            copy.wait()

    core = lax.axis_index("core")

    @pl.when(core == 0)
    def _():
        move(rows - 1 if even_last else 0)

    @pl.when(core != 0)
    def _():
        move(0 if even_last else rows - 1)


def edge_rows(even_last, flow_state, flow_speed):
    count, _, plane = flow_state.shape
    return pl.pallas_call(
        functools.partial(edge_kernel, even_last),
        out_shape=jax.ShapeDtypeStruct((count + 1, plane), F32),
        in_specs=[HBM, HBM],
        out_specs=VMEM,
        scratch_shapes=[pltpu.SemaphoreType.DMA((count + 1,))],
        compiler_params=pltpu.CompilerParams(vmem_limit_bytes=SMALL_LIMIT),
        name="edge_rows",
    )(
        pltpu.with_memory_space_constraint(flow_state, pltpu.HBM),
        pltpu.with_memory_space_constraint(flow_speed, pltpu.HBM),
    )


RATE = 0.5 * FLUX_STEP
PRESSURE = 4


def picked(stacked, chosen, lane):
    high, middle, low = parts(stacked)
    pieces = jnp.concatenate([high, middle, low], axis=1).astype(BF16)
    both = lax.dot_general(pieces, chosen, (((0,), (0,)), ((), ())), preferred_element_type=F32)
    value = (both[:128] + both[128:256]) + both[256:]
    here = lax.broadcasted_iota(jnp.int32, value.shape, 0) == lane
    return jnp.sum(jnp.where(here, value, 0.0), axis=0, keepdims=True)


def stacked_lanes(values):
    return jnp.concatenate([values[:, i : i + 128] for i in range(0, values.shape[1], 128)], axis=0)


def inner_kernel(q_ref, w_ref, sorted_ref, new_hbm, low_ref, high_ref, out_ref, chosen_ref, new_ref, sems):
    count, rows, plane = q_ref.shape
    width = 512
    steps = plane // width
    row = lax.broadcasted_iota(jnp.int32, (rows, width), 0)

    def copy_of(step):
        lanes = pl.ds(pl.multiple_of(step * width, width), width)
        return pltpu.make_async_copy(new_ref.at[:, :, lanes], new_hbm.at[:, :, lanes], sems.at[step])

    def chunk(step, _):
        here = pl.multiple_of(step * width, 128)
        left = pl.multiple_of(lax.rem(here + plane - 128, plane), 128)
        right = pl.multiple_of(lax.rem(here + width, plane), 128)

        def cyclic(ref, index):
            values = ref[index, :, pl.ds(here, width)]
            wide = jnp.concatenate(
                [ref[index, :, pl.ds(left, 128)], values, ref[index, :, pl.ds(right, 128)]], axis=1
            )
            before = pltpu.roll(wide, 1, 1)[:, 128 : 128 + width]
            after = pltpu.roll(wide, width + 255, 1)[:, 128 : 128 + width]
            return values, before, after

        w = w_ref[0, :, pl.ds(here, width)]
        face_low = jnp.where(row == 0, 0.0, RATE * (pltpu.roll(w, 1, 0) + w))
        face_high = jnp.where(row == rows - 1, 0.0, RATE * (w + pltpu.roll(w, rows - 1, 0)))
        speed, speed_before, speed_after = cyclic(w_ref, 1)
        face_left = RATE * (speed_before + speed)
        face_right = RATE * (speed + speed_after)
        low_in = jnp.maximum(face_low, 0.0)
        high_out = jnp.minimum(face_high, 0.0)
        left_in = jnp.maximum(face_left, 0.0)
        right_out = jnp.minimum(face_right, 0.0)
        keep = 1.0 - (
            (jnp.maximum(face_high, 0.0) - jnp.minimum(face_low, 0.0))
            + (jnp.maximum(face_right, 0.0) - jnp.minimum(face_left, 0.0))
        )
        for index in range(count):
            values, before, after = cyclic(q_ref, index)
            new = (
                keep * values
                + low_in * pltpu.roll(values, 1, 0)
                - high_out * pltpu.roll(values, rows - 1, 0)
                + left_in * before
                - right_out * after
            )
            new_ref[index, :, pl.ds(here, width)] = new
            low_ref[index : index + 1, pl.ds(here, width)] = new[0:1]
            high_ref[index : index + 1, pl.ds(here, width)] = new[rows - 1 : rows]
        copy_of(step).start()
        return 0

    lax.fori_loop(0, steps, chunk, 0)

    cells = sorted_ref[9:10].astype(jnp.int32)
    cell_row = cells // plane
    column = cells - cell_row * plane
    group = column // 128
    lane = column - group * 128
    place = group * rows + cell_row
    centres = cells.shape[1]
    lanes = plane // 128
    chosen = (lax.broadcasted_iota(jnp.int32, (rows * lanes, centres), 0) == place).astype(F32).astype(BF16)
    chosen_ref[...] = chosen
    load = picked(stacked_lanes(new_ref[PRESSURE]), chosen, lane)
    out_ref[...] = jnp.concatenate(
        [
            sorted_ref[0:3] + sorted_ref[3:6] * load,
            sorted_ref[3:9],
            lane.astype(F32),
            jnp.zeros((6, centres), F32),
        ],
        axis=0,
    )
    for step in range(steps):
        copy_of(step).wait()


def inner_flux(flow_state, flow_speed, in_order):
    count, rows, plane = flow_state.shape
    centres = in_order.shape[1]
    edge = jax.ShapeDtypeStruct((count, plane), F32)
    return pl.pallas_call(
        inner_kernel,
        out_shape=(
            pltpu.HBM(flow_state.shape, F32),
            edge,
            edge,
            jax.ShapeDtypeStruct((16, centres), F32),
            jax.ShapeDtypeStruct((rows * plane // 128, centres), BF16),
        ),
        in_specs=[VMEM] * 3,
        out_specs=(HBM, VMEM, VMEM, VMEM, VMEM),
        scratch_shapes=[pltpu.VMEM(flow_state.shape, F32), pltpu.SemaphoreType.DMA((plane // 512,))],
        compiler_params=pltpu.CompilerParams(vmem_limit_bytes=SMALL_LIMIT),
        cost_estimate=pl.CostEstimate(flops=20_000_000, bytes_accessed=4_000_000, transcendentals=0),
        name="inner_flux",
    )(flow_state, flow_speed, in_order)


def outer_kernel(
    send_a, send_b, from_a, from_b, low_ref, high_ref, base_ref, chosen_ref, out_ref, new_low, new_high, both_ref
):
    count, plane = low_ref.shape
    rows = both_ref.shape[0]
    even = lax.axis_index("core") == 0
    own_low = jnp.where(even, send_b[...], send_a[...])
    own_high = jnp.where(even, send_a[...], send_b[...])
    below = jnp.where(even, from_b[...], from_a[...])
    above = jnp.where(even, from_a[...], from_b[...])

    def flux(first, second):
        face = RATE * (first[count : count + 1] + second[count : count + 1])
        return jnp.maximum(face, 0.0) * first[:count] + jnp.minimum(face, 0.0) * second[:count]

    low = flux(below, own_low)
    high = flux(own_high, above)
    new_low[...] = low_ref[...] + low
    new_high[...] = high_ref[...] - high
    row = lax.broadcasted_iota(jnp.int32, (rows, plane), 0)
    zero = jnp.zeros((rows, plane), F32)
    added = jnp.where(row == 0, low[PRESSURE : PRESSURE + 1], zero)
    added = added - jnp.where(row == rows - 1, high[PRESSURE : PRESSURE + 1], zero)
    both_ref[...] = added
    base = base_ref[...]
    load = picked(stacked_lanes(both_ref[...]), chosen_ref[...], base[9:10].astype(jnp.int32))
    centres = base.shape[1]
    packed = jnp.concatenate([base[0:3] + base[3:6] * load, base[6:9], jnp.zeros((2, centres), F32)], axis=0)
    for chip in range(out_ref.shape[0]):
        out_ref[chip] = packed


def right_side(chips, rows, send_a, send_b, from_a, from_b, low, high, base, chosen):
    edge = jax.ShapeDtypeStruct(low.shape, F32)
    return pl.pallas_call(
        outer_kernel,
        out_shape=(jax.ShapeDtypeStruct((chips, 8, base.shape[1]), F32), edge, edge),
        in_specs=[VMEM] * 8,
        out_specs=(VMEM,) * 3,
        scratch_shapes=[pltpu.VMEM((rows, low.shape[1]), F32)],
        compiler_params=pltpu.CompilerParams(vmem_limit_bytes=SMALL_LIMIT),
        name="outer_flux",
    )(send_a, send_b, from_a, from_b, low, high, base, chosen)


def block_of(mine_ref, other_ref, block, core):
    chip = lax.div(block, 2)
    own = lax.rem(block, 2) == core
    return jnp.where(own, mine_ref[chip], other_ref[chip])


def moment_place(index):
    row = lax.broadcasted_iota(jnp.int32, (8, 128), 0)
    return lax.broadcasted_iota(jnp.int32, (8, 128), 1) == row * 8 + index


def powers_kernel(
    count, mine_ref, other_ref, new_low, new_high, new_in, out_ref, new_out,
    source_side, target_side, vector, image, tables, low_ref, high_ref, sems,
):
    del new_in
    rows_per_block = new_out.shape[1]
    copies = [
        pltpu.make_async_copy(new_low, new_out.at[:, 0], sems.at[0]),
        pltpu.make_async_copy(new_high, new_out.at[:, rows_per_block - 1], sems.at[1]),
    ]
    for copy in copies:
        copy.start()
    size = mine_ref.shape[2]
    chip, core = lax.axis_index("chip"), lax.axis_index("core")
    me = chip * 2 + core
    slots, width, reach = 6, 256, 6
    span = reach * CHUNK
    total = slots * size
    origin = lax.div(me * 2, 5).astype(F32)
    value_row = lax.broadcasted_iota(jnp.int32, (8, size), 0) < 3

    live, zeroth, third = [], [], []
    for slot in range(slots):
        block = me + slot - 2
        valid = jnp.logical_and(block >= 0, block < count)
        live.append(valid)
        data = block_of(mine_ref, other_ref, jnp.clip(block, 0, count - 1), core)
        zeroth.append(jnp.where(jnp.logical_and(value_row, valid), data, 0.0))
        middle = (block.astype(F32) + 0.5) * DEPTH
        raw = jnp.concatenate([data[3:5], jnp.where(valid, data[5:6], middle)], axis=0)
        points = local_points(raw, origin)
        third.append(points[2:3])
        source, target = sides(points)
        source_side[slot * size : (slot + 1) * size] = source.T.astype(BF16)
        target_side[:, slot * size : (slot + 1) * size] = target.astype(BF16)
    far = (lax.broadcasted_iota(jnp.int32, (span, 48), 1) == 3).astype(F32) * 4096.0
    source_side[total:] = far.astype(BF16)
    vector[:, total:] = jnp.zeros((16, span), BF16)
    heights = jnp.concatenate(third, axis=1)
    chunk_bounds(heights, heights[:, size : 5 * size], width, low_ref, high_ref)
    tiles = 4 * size // width

    def steps_of(tile):
        return lax.div(high_ref[tile] - low_ref[tile] + (reach - 1), reach)

    most = steps_of(0)
    for tile in range(1, tiles):
        most = jnp.maximum(most, steps_of(tile))

    skipped, per_tile, mine_first = size // CHUNK, width // CHUNK, size // width
    per_block = size // width

    def tiles_up_to(chunk):
        return lax.div(chunk - skipped + (per_tile - 1), per_tile)

    second_end = high_ref[mine_first]
    for tile in range(mine_first + 1, 2 * mine_first):
        second_end = jnp.maximum(second_end, high_ref[tile])
    second_end = jnp.clip(tiles_up_to(second_end), 2 * per_block, 3 * per_block)
    read_low, read_high = low_ref[mine_first], high_ref[mine_first]
    for tile in range(mine_first + 1, 3 * per_block):
        read = tile < second_end
        read_low = jnp.minimum(read_low, jnp.where(read, low_ref[tile], read_low))
        read_high = jnp.maximum(read_high, jnp.where(read, high_ref[tile], read_high))
    first_start = jnp.clip(lax.div(jnp.maximum(read_low - skipped, 0), per_tile), 0, per_block)
    first_end = jnp.clip(tiles_up_to(read_high), second_end, tiles)
    same = lax.broadcasted_iota(jnp.int32, (CHUNK, CHUNK), 0) == lax.broadcasted_iota(
        jnp.int32, (CHUNK, CHUNK), 1
    )

    def build(tile, step):
        lanes = pl.ds(pl.multiple_of(tile * width + size, width), width)
        chunk = low_ref[tile] + step * reach
        rows = pl.ds(pl.multiple_of(chunk * CHUNK, CHUNK), span)
        table = quarter_kernel(source_side[rows], target_side[:, lanes])
        high = table.astype(BF16)
        tables[tile, step, :span] = high
        tables[tile, step, span:] = (table - high.astype(F32)).astype(BF16)
        for piece in range(width // CHUNK):
            place = (tile * width + size) // CHUNK + piece - chunk
            inside = jnp.logical_and(place >= 0, place < reach)
            place = jnp.clip(place, 0, reach - 1)
            for half in range(2):
                at = pl.ds(pl.multiple_of(place * CHUNK + half * span, CHUNK), CHUNK)
                columns = slice(piece * CHUNK, (piece + 1) * CHUNK)
                old = tables[tile, step, at, columns]
                tables[tile, step, at, columns] = jnp.where(jnp.logical_and(same, inside), 0.0, old.astype(F32)).astype(BF16)

    def one(tile, step):
        lanes = pl.ds(pl.multiple_of((low_ref[tile] + step * reach) * CHUNK, CHUNK), span)
        window = vector[:, lanes]
        return jnp.dot(jnp.concatenate([window, window], axis=1), tables[tile, step], preferred_element_type=F32)

    def lanes_of(tile):
        return pl.ds(pl.multiple_of(tile * width, width), width)

    def further(first, last):
        @pl.when(most > 1)
        def _():
            def of_tile(tile, _):
                def add(step, _):
                    image[:, lanes_of(tile)] += one(tile, step)
                    return 0

                return lax.fori_loop(1, steps_of(tile), add, 0)

            lax.fori_loop(first, last, of_tile, 0)

    def image_of(slot):
        both = image[:, (slot - 1) * size : slot * size]
        return jnp.where(live[slot], 4.0 * (both[:8] + both[8:]), 0.0)

    def power(slots, end):
        first, last = (slots[0] - 1) * per_block, slots[-1] * per_block
        for tile in range(first, last):
            here = slice(tile * width, (tile + 1) * width)
            if tile < 2 * per_block:
                image[:, here] = one(tile, 0)
            else:
                image[:, here] = jnp.zeros((16, width), F32)

                @pl.when(tile < end)
                def _(tile=tile, here=here):
                    image[:, here] = one(tile, 0)

        further(first, end)
        return {slot: image_of(slot) for slot in slots}

    def hold(values, slot):
        vector[:, slot * size : (slot + 1) * size] = doubled(values)

    for slot in range(slots):
        hold(zeroth[slot], slot)

    for tile in (*range(per_block), *range(2 * per_block, tiles)):
        image[:, tile * width : (tile + 1) * width] = jnp.zeros((16, width), F32)

    def tile_step(tile, _):
        before = jnp.maximum(tile - 1, first_start)
        image[:, lanes_of(before)] = one(before, 0)
        build(tile, 0)
        return 0

    lax.fori_loop(first_start, first_end, tile_step, 0)
    image[:, lanes_of(first_end - 1)] = one(first_end - 1, 0)

    @pl.when(most > 1)
    def _():
        def of_tile(tile, _):
            def more(step, _):
                build(tile, step)
                return 0

            return lax.fori_loop(1, steps_of(tile), more, 0)

        lax.fori_loop(first_start, first_end, of_tile, 0)

    further(first_start, first_end)
    first = {slot: image_of(slot) for slot in range(1, 5)}
    for slot in range(1, 5):
        hold(first[slot], slot)
    second = power([2, 3], second_end)
    hold(jnp.zeros((8, size), F32), 1)
    hold(second[2], 2)
    hold(2.0 * second[3], 3)
    last = power([2], 2 * per_block)[2]

    def inner(left, right):
        return jnp.sum(left * right, axis=1, keepdims=True)

    moments = [
        inner(zeroth[2], zeroth[2]),
        inner(zeroth[2], first[2]),
        inner(first[2], first[2]),
        inner(first[2], second[2]),
        inner(second[2], second[2]),
        inner(second[2], last),
    ]
    packed = jnp.zeros((8, 128), F32)
    for index, moment in enumerate(moments):
        packed = jnp.where(moment_place(index), moment, packed)
    row = jnp.concatenate(
        [jnp.sum(packed, axis=0, keepdims=True), jnp.zeros((1, size - 128), F32)], axis=1
    )
    values = jnp.concatenate([first[2][:3], second[2][:3], row, jnp.zeros((1, size), F32)], axis=0)
    for index in range(out_ref.shape[0]):
        out_ref[index] = values
    for copy in copies:
        copy.wait()


def powers(mine, other, new_low, new_high, new_flow, count):
    chips, _, size = mine.shape
    tiles = 4 * size // 256
    steps = (6 * size // CHUNK + 5) // 6
    return pl.pallas_call(
        functools.partial(powers_kernel, count),
        out_shape=(
            jax.ShapeDtypeStruct((chips, 8, size), F32),
            pltpu.HBM(new_flow.shape, F32),
        ),
        in_specs=[VMEM] * 4 + [HBM],
        out_specs=(VMEM, HBM),
        scratch_shapes=[
            pltpu.VMEM((6 * size + 6 * CHUNK, 48), BF16),
            pltpu.VMEM((48, 6 * size), BF16),
            pltpu.VMEM((16, 6 * size + 6 * CHUNK), BF16),
            pltpu.VMEM((16, 4 * size), F32),
            pltpu.VMEM((tiles, steps, 12 * CHUNK, 256), BF16),
            pltpu.SMEM((tiles,), jnp.int32),
            pltpu.SMEM((tiles,), jnp.int32),
            pltpu.SemaphoreType.DMA((2,)),
        ],
        input_output_aliases={4: 1},
        compiler_params=pltpu.CompilerParams(vmem_limit_bytes=BIG_LIMIT),
        name="powers",
    )(mine, other, new_low, new_high, pltpu.with_memory_space_constraint(new_flow, pltpu.HBM))


def ratio(top, bottom):
    safe = bottom > 0.0
    return jnp.where(safe, top / jnp.where(safe, bottom, 1.0), 0.0)


def weights_of(moments):
    lost = jnp.zeros_like(moments[0])

    def inner(left, right):
        total = size = None
        for i, a in enumerate(left):
            for j, c in enumerate(right):
                term = a * c * moments[i + j]
                total = term if total is None else total + term
                size = jnp.abs(term) if size is None else size + jnp.abs(term)
        return total, jnp.where(total > LOSS * size, 0.0, jnp.where(size > 0.0, 1.0, 0.0))

    one = jnp.ones_like(moments[0])
    residual, search = [one], [one]
    coefficients = [0.0 * one] * ITERS
    energy = moments[0]
    for step in range(ITERS):
        image = [CENTRE_SHIFT * value for value in search] + [0.0 * one]
        for index, value in enumerate(search):
            image[index + 1] = image[index + 1] + value
        along, bad = inner(search, image)
        lost = lost + bad
        length = ratio(energy, along)
        for index, value in enumerate(search):
            coefficients[index] = coefficients[index] + length * value
        if step == ITERS - 1:
            break
        longer = residual + [0.0 * one]
        residual = [value - length * other for value, other in zip(longer, image)]
        fresh, bad = inner(residual, residual)
        lost = lost + bad
        scale = ratio(fresh, energy)
        search = [
            value + scale * (search[index] if index < len(search) else 0.0)
            for index, value in enumerate(residual)
        ]
        energy = fresh
    return coefficients, lost


REACH = 7


def bounds_of(source_z, target_z):
    chunks = source_z.shape[1] // CHUNK
    tiles = target_z.shape[1] // CHUNK

    def edges(values, pieces):
        rows = jnp.concatenate([values[:, i * CHUNK : (i + 1) * CHUNK] for i in range(pieces)], axis=0)
        return jnp.min(rows, axis=1, keepdims=True), jnp.max(rows, axis=1, keepdims=True)

    def across(values):
        return jnp.broadcast_to(values, (tiles, 128)).T[0:1]

    source_low, source_high = edges(source_z, chunks)
    target_low, target_high = edges(target_z, tiles)
    near = jnp.logical_and(
        source_high >= across(target_low) - (1.0 + MARGIN), source_low <= across(target_high) + (1.0 + MARGIN)
    )
    index = lax.broadcasted_iota(jnp.int32, (chunks, tiles), 0).astype(F32)
    low = jnp.min(jnp.where(near, index, float(chunks)), axis=0, keepdims=True)
    high = jnp.max(jnp.where(near, index + 1.0, 0.0), axis=0, keepdims=True)
    return jnp.concatenate([low, high], axis=0)


def first_listed(tile_ref, me):
    return tile_ref[pl.ds(me, 1), :][0, 0]


def scalars_of(bound_ref, low_ref, step_ref):
    bounds = bound_ref[...].astype(jnp.int32)
    most = 0
    for tile in range(bounds.shape[1]):
        low = bounds[0, tile]
        steps = lax.div(bounds[1, tile] - low + (REACH - 1), REACH)
        low_ref[tile] = low
        step_ref[tile] = steps
        most = jnp.maximum(most, steps)
    return most


def near_table(source_ref, target_ref, low_ref, tile, step):
    start = pl.multiple_of((low_ref[tile] + step * REACH) * CHUNK, CHUNK)
    lanes = pl.ds(pl.multiple_of(tile * CHUNK, CHUNK), CHUNK)
    return doubled(quarter_kernel(source_ref[pl.ds(start, REACH * CHUNK)], target_ref[:, lanes]))


EARLY = 2


def points_kernel(
    tile_ref, mine_ref, other_ref, nodes_ref, source_ref, target_ref, bound_ref, table_ref, low_ref, step_ref
):
    size = mine_ref.shape[2]
    core = lax.axis_index("core")
    me = lax.axis_index("chip") * 2 + core
    listed = tile_ref.shape[1]
    start = first_listed(tile_ref, me)
    origin = lax.div((start + 2) * 2, 5).astype(F32)
    third = []
    for index in range(listed):
        data = block_of(mine_ref, other_ref, start + index, core)
        points = local_points(data[3:6], origin)
        third.append(points[2:3])
        source, _ = sides(points)
        source_ref[index * size : (index + 1) * size] = source.T.astype(BF16)
    span = REACH * CHUNK
    far = (lax.broadcasted_iota(jnp.int32, (span, 48), 1) == 3).astype(F32) * 4096.0
    source_ref[listed * size :] = far.astype(BF16)
    points = local_points(nodes_ref[0:3], origin)
    _, target = sides(points)
    target_ref[...] = target.astype(BF16)
    bound_ref[...] = bounds_of(jnp.concatenate(third, axis=1), points[2:3])
    scalars_of(bound_ref, low_ref, step_ref)
    for tile in range(EARLY):
        table_ref[tile] = near_table(source_ref, target_ref, low_ref, tile, 0)


def near_points(tile_blocks, mine, other, nodes):
    size = mine.shape[2]
    slots = nodes.shape[1]
    listed = tile_blocks.shape[1]
    return pl.pallas_call(
        points_kernel,
        out_shape=(
            jax.ShapeDtypeStruct((listed * size + REACH * CHUNK, 48), BF16),
            jax.ShapeDtypeStruct((48, slots), BF16),
            jax.ShapeDtypeStruct((2, slots // CHUNK), F32),
            jax.ShapeDtypeStruct((EARLY, 2 * REACH * CHUNK, CHUNK), BF16),
        ),
        in_specs=[VMEM] * 4,
        out_specs=(VMEM,) * 4,
        scratch_shapes=[
            pltpu.SMEM((slots // CHUNK,), jnp.int32),
            pltpu.SMEM((slots // CHUNK,), jnp.int32),
        ],
        compiler_params=pltpu.CompilerParams(vmem_limit_bytes=SMALL_LIMIT),
        cost_estimate=pl.CostEstimate(flops=1_000_000, bytes_accessed=1_000_000, transcendentals=0),
        name="near_points",
    )(tile_blocks, mine, other, nodes)


def near_kernel(
    tile_ref, count_ref, bound_ref, mine_ref, other_ref, mine_power, other_power, source_side, target_side,
    table_ref, centre_table, node_table, coef_ref, shift_ref, lost_ref, vector, result, low_ref, step_ref,
):
    size = mine_ref.shape[2]
    slots = target_side.shape[1]
    chips = mine_ref.shape[0]
    core = lax.axis_index("core")
    me = lax.axis_index("chip") * 2 + core
    listed = tile_ref.shape[1]
    start_block = first_listed(tile_ref, me)
    width = CHUNK
    tiles = slots // width
    span = REACH * CHUNK
    total = listed * size

    most = scalars_of(bound_ref, low_ref, step_ref)
    summed = mine_power[0, 6:7, :128] + other_power[0, 6:7, :128]
    for index in range(1, chips):
        summed = summed + (mine_power[index, 6:7, :128] + other_power[index, 6:7, :128])
    weights, lost = weights_of(
        [jnp.sum(jnp.where(moment_place(index), summed, 0.0), axis=1, keepdims=True) for index in range(6)]
    )
    lost_ref[...] = jnp.broadcast_to(jnp.max(lost[:3], axis=0, keepdims=True), (1, 128))

    def coefficients_of(block):
        data = block_of(mine_ref, other_ref, block, core)
        power = block_of(mine_power, other_power, block, core)
        values = weights[0] * data + weights[1] * power + weights[2] * pltpu.roll(power, 5, 0)
        keep = lax.broadcasted_iota(jnp.int32, (8, size), 0) < 3
        return jnp.where(keep, values, 0.0)

    for index in range(listed):
        vector[:, index * size : (index + 1) * size] = doubled(coefficients_of(start_block + index))
    vector[:, total:] = jnp.zeros((16, span), BF16)

    def lanes_of(tile):
        return pl.ds(pl.multiple_of(tile * width, width), width)

    def one(tile, step, table):
        start = pl.multiple_of((low_ref[tile] + step * REACH) * CHUNK, CHUNK)
        window = vector[:, pl.ds(start, span)]
        return jnp.dot(jnp.concatenate([window, window], axis=1), table, preferred_element_type=F32)

    for tile in range(EARLY):
        result[:, tile * width : (tile + 1) * width] = one(tile, 0, table_ref[tile])
    coef_ref[...] = moved_back(coefficients_of(me), centre_table[...])

    def two_tiles(step, _):
        for piece in range(2):
            tile = EARLY + 2 * step + piece
            table = near_table(source_side, target_side, low_ref, tile, 0)
            result[:, lanes_of(tile)] = one(tile, 0, table)
        return 0

    lax.fori_loop(0, (tiles - EARLY) // 2, two_tiles, 0, unroll=True)

    @pl.when(most > 1)
    def _():
        def of_tile(tile, _):
            def add(step, _):
                table = near_table(source_side, target_side, low_ref, tile, step)
                result[:, lanes_of(tile)] += one(tile, step, table)
                return 0

            return lax.fori_loop(1, step_ref[tile], add, 0)

        lax.fori_loop(0, tiles, of_tile, 0)

    lane = lax.broadcasted_iota(jnp.int32, count_ref.shape, 1)
    live = jnp.sum(jnp.where(lane == me, count_ref[...], 0).astype(F32), axis=1, keepdims=True)
    slot = lax.broadcasted_iota(jnp.int32, (3, slots), 1).astype(F32)
    both = result[...]
    shift = moved_back(4.0 * (both[:8] + both[8:]), node_table[...])
    shift_ref[...] = jnp.where(slot < live, shift, 0.0)


def near_body(tile_blocks, near_count, bounds, mine, other, mine_power, other_power, sources, targets, tables, centre_table, node_table):
    size = mine.shape[2]
    slots = targets.shape[1]
    total = tile_blocks.shape[1] * size
    return pl.pallas_call(
        near_kernel,
        out_shape=(
            jax.ShapeDtypeStruct((3, size), F32),
            jax.ShapeDtypeStruct((3, slots), F32),
            jax.ShapeDtypeStruct((1, 128), F32),
        ),
        in_specs=[VMEM] * 12,
        out_specs=(VMEM,) * 3,
        scratch_shapes=[
            pltpu.VMEM((16, total + REACH * CHUNK), BF16),
            pltpu.VMEM((16, slots), F32),
            pltpu.SMEM((slots // CHUNK,), jnp.int32),
            pltpu.SMEM((slots // CHUNK,), jnp.int32),
        ],
        compiler_params=pltpu.CompilerParams(vmem_limit_bytes=SMALL_LIMIT),
        name="near_body",
    )(
        tile_blocks, near_count.reshape(1, -1), bounds, mine, other, mine_power, other_power, sources, targets,
        tables, centre_table, node_table,
    )


def gathered(values, partner):
    mine = lax.all_to_all(values, "chip", 0, 0)
    return mine, lax.ppermute(mine, SLAB, partner)


def step_by_step(count, right, centres, tile_blocks, near_count, near_nodes):
    size = centres.shape[1]
    up = [(i, i + 1) for i in range(count - 1)]
    down = [(i + 1, i) for i in range(count - 1)]

    def widened(values):
        return jnp.concatenate([lax.ppermute(values, SLAB, up), values, lax.ppermute(values, SLAB, down)], axis=1)

    def table_of(sources, targets):
        scaled = jnp.sqrt(sum((sources[k][:, None] - targets[k][None, :]) ** 2 for k in range(3))) / SUPPORT
        inside = jnp.maximum(1.0 - scaled, 0.0)
        square_in = inside * inside
        return square_in * square_in * (4.0 * scaled + 1.0)

    def total(left, other):
        return lax.psum(jnp.sum(left * other, axis=1), SLAB)

    def product(values, table):
        return jnp.dot(values, table, precision=lax.Precision.HIGHEST, preferred_element_type=F32)

    around = widened(centres)

    def step(_, held):
        coefficients, residual, search, energy = held
        image = product(widened(search), table_of(around, centres)) + DIAG_SHIFT * search
        length = energy / total(search, image)
        coefficients = coefficients + length[:, None] * search
        residual = residual - length[:, None] * image
        fresh = total(residual, residual)
        return coefficients, residual, residual + (fresh / energy)[:, None] * search, fresh

    coefficients = lax.fori_loop(0, ITERS, step, (jnp.zeros_like(right), right, right, total(right, right)))[0]
    everywhere = lax.all_gather(jnp.concatenate([centres, coefficients], axis=0), SLAB, axis=1, tiled=True)
    me = lax.axis_index(SLAB)
    slots = near_nodes.shape[1]

    def listed(index, sums):
        data = lax.dynamic_slice_in_dim(everywhere, tile_blocks[me, index] * size, size, 1)
        return sums + product(data[3:], table_of(data[:3], near_nodes))

    shift = lax.fori_loop(0, tile_blocks.shape[1], listed, jnp.zeros((3, slots), F32))
    live = lax.iota(jnp.int32, slots) < near_count[me]
    return coefficients, jnp.where(live[None, :], shift, 0.0)


def shards(
    count,
    flow_state,
    flow_speed,
    wall_cell,
    base_shift,
    normals,
    centres,
    tile_blocks,
    near_count,
    near_nodes,
):
    partner = [(i, i ^ 1) for i in range(count)]
    across = [(i, i + 1) for i in range(1, count - 1, 2)]
    across = across + [(j, i) for i, j in across]
    chips, rows = count // 2, flow_state.shape[1]
    send_b = edge_rows(False, flow_state, flow_speed)
    from_b = lax.ppermute(send_b, SLAB, across)
    send_a = edge_rows(True, flow_state, flow_speed)
    from_a = lax.ppermute(send_a, SLAB, partner)
    in_order, centre_table, nodes, node_table = ordered(base_shift, normals, centres, wall_cell, near_nodes)
    new_flow, low, high, base, chosen = inner_flux(flow_state, flow_speed, in_order)
    packed, low, high = right_side(chips, rows, send_a, send_b, from_a, from_b, low, high, base, chosen)
    mine, other = gathered(packed, partner)
    power, new_flow = powers(mine, other, low, high, new_flow, count)
    mine_power, other_power = gathered(power, partner)
    sources, targets, bounds, tables = near_points(tile_blocks, mine, other, nodes)
    coefficients, node_shift, lost = near_body(
        tile_blocks, near_count, bounds, mine, other, mine_power, other_power, sources, targets,
        tables, centre_table, node_table,
    )

    def again(held):
        one = jnp.where(held[0][0, 0] > 0.0, 1.0, 0.0)
        whole = one.astype(jnp.int32)
        own = packed[0] * one
        found, shifted = step_by_step(
            count, own[0:3], own[3:6], tile_blocks * whole, near_count * whole, near_nodes * one
        )
        back = jnp.dot(found, centre_table.astype(F32) * one, precision=lax.Precision.HIGHEST)
        return jnp.zeros_like(held[0]), back, shifted

    _, coefficients, node_shift = lax.while_loop(
        lambda held: held[0][0, 0] > 0.0, again, (lost, coefficients, node_shift)
    )
    return new_flow, coefficients, node_shift


def solution(mesh):
    groups, count = mesh.shape["groups"], mesh.shape["slab"]
    split = Mesh(mesh.devices.reshape(groups, count // 2, 2), ("groups",) + SLAB)
    in_specs = (
        P("groups", SLAB, None),
        P("groups", SLAB, None),
        P(("groups",) + SLAB),
        P("groups", SLAB),
        P("groups", SLAB),
        P("groups", SLAB),
        P("groups", None),
        P("groups"),
        P("groups", SLAB),
    )
    out_specs = (P("groups", SLAB, None), P("groups", SLAB), P("groups", SLAB))
    return jax.shard_map(
        functools.partial(shards, count), mesh=split, in_specs=in_specs, out_specs=out_specs, check_vma=False
    )
```
